32 devices in a mesh: dp: 4 (over y, x), seq: 8 (over z, core).
Axes of the slice: x: 2, y: 2, z: 4, core: 2. Of those that a mesh axis runs over, the one named last changes fastest.
Arguments:
- queries: bfloat16 [4, 2048, 1024], P('dp', 'seq'), may hold values from -8 to 8
- key_rows: bfloat16 [4, 2048, 512], P('dp', 'seq'), may hold values from -4 to 4
- values: bfloat16 [4, 2048, 512], P('dp', 'seq'), may hold values from -6 to 6
- out_weight: bfloat16 [2304, 1024], P(('dp', 'seq')), may hold values from -0.1875 to 0.1875
- out_grad: bfloat16 [4, 2048, 2304], P('dp', 'seq'), may hold values from -6 to 6
Outputs:
- layer_out: bfloat16 [4, 2048, 2304], P('dp', 'seq')
- query_grad: bfloat16 [4, 2048, 1024], P('dp', 'seq')
- key_grad: bfloat16 [4, 2048, 512], P('dp', 'seq')
- value_grad: bfloat16 [4, 2048, 512], P('dp', 'seq')
- weight_grad: float32 [2304, 1024], P(('dp', 'seq'))
The draws below stay inside these ranges and needn't reach their ends.
All inputs are finite; a program needn't handle non-finite values.
Results may differ from the reference program's by a relative error of at most 0.024.
Values may be sent and summed in bfloat16 or wider, within the bound.
No kernel may reach another device: no remote copies, remote signals or barrier semaphores. Data moves between devices by JAX's collectives and lax.ppermute only.
A program may use at most 128 MiB of HBM per device.

```python
import math
import jax
import jax.numpy as jnp
from jax import lax

D = 2304
QH = 4
KH = 2
HD = 256
WINDOW = 2048
SEQS = 4
SEQLEN = 2048


def draw_queries(key, part):
    block_len = WINDOW // 4
    blocks = SEQLEN // block_len
    shape = (SEQS, blocks, block_len, QH, HD)
    bulk = jnp.clip(2.5 * jax.random.normal(jax.random.fold_in(key, 1), shape, jnp.float32), -8.0, 8.0)
    return bulk.reshape(SEQS, SEQLEN, QH * HD).astype(jnp.bfloat16)


def draw_key_rows(key, part):
    block_len = WINDOW // 4
    blocks = SEQLEN // block_len
    shape = (SEQS, blocks, block_len, KH, HD)
    bulk = jnp.clip(jax.random.normal(jax.random.fold_in(key, 2), shape, jnp.float32), -4.0, 4.0)
    return bulk.reshape(SEQS, SEQLEN, KH * HD).astype(jnp.bfloat16)


def raised(values, key, source, target, blocks, factor):
    owner, partner = [(jnp.arange(values.shape[position]) // (values.shape[position] // blocks)).reshape([-1 if axis == position else 1 for axis in range(values.ndim)]) for position in (source, target)]
    chosen = jax.random.permutation(key, blocks)[partner]
    strong = (owner == chosen) | (owner == (partner + blocks // 2) % blocks)
    return jnp.where(strong, factor * values, values)


def steps_of(stream_key, shape, pieces, least, largest):
    def one(axis_at, parts):
        heights = jax.random.uniform(jax.random.fold_in(jax.random.fold_in(stream_key, 6), axis_at), (parts,), jnp.float32, least / len(pieces), largest / len(pieces))
        return jnp.repeat(jnp.exp(heights), shape[axis_at] // parts).reshape((-1,) + (1,) * (len(shape) - axis_at - 1))

    gain = one(*pieces[0])
    for cut in pieces[1:]:
        gain = gain * one(*cut)
    return gain


def scatter_about(stream_key, shape, width, bound, shards=(), kind=jnp.bfloat16):
    values = jax.random.normal(stream_key, shape, jnp.float32) * width
    if len(shards) > 0:
        values = steps_of(stream_key, shape, shards, -0.22, 0.18) * values
    return jnp.clip(values, min=-bound, max=bound).astype(kind)


def gaussian_with(key, extent, deviation, most, pieces, heavy, held_as=jnp.bfloat16):
    result = deviation * jax.random.normal(key, extent, jnp.float32)
    if pieces:
        result = result * steps_of(key, extent, pieces, -0.22, 0.18)
    return jnp.clip(raised(result, jax.random.fold_in(key, 3), *heavy), -most, most).astype(held_as)


def setup_inputs(seed: int = 0) -> dict:
    seeds = jax.random.split(jax.random.key(seed), 6)
    queries = draw_queries(jax.random.fold_in(seeds[5], 71), 0)
    key_rows = draw_key_rows(jax.random.fold_in(seeds[5], 71), 0)
    values = scatter_about(seeds[2], (SEQS, SEQLEN, KH * HD), 1.0, 6.0, ((0, 4), (1, 8)))
    out_weight = scatter_about(seeds[3], (D, QH * HD), (QH * HD) ** -0.5, 0.1875, ((0, 32),))
    out_grad = gaussian_with(seeds[4], (SEQS, SEQLEN, D), 1.0, 6.0, ((0, 4), (1, 8)), (1, 2, 8, 2.0))
    return {"queries": queries, "key_rows": key_rows, "values": values, "out_weight": out_weight, "out_grad": out_grad}


def one_sequence(queries, key_rows, values, out_weight, out_grad):
    groups = QH // KH
    block_rows = min(512, SEQLEN)
    span = WINDOW + block_rows
    score_scale = HD ** (-0.5)
    key_width = KH * HD
    zero_pad = jnp.zeros((WINDOW, key_width), jnp.bfloat16)
    keys_pad = jnp.concatenate([zero_pad, key_rows], axis=0)
    values_pad = jnp.concatenate([zero_pad, values], axis=0)

    def block_step(carried, block_index):
        keys_grad, values_grad, weight_sum = carried
        first_row = (block_index * block_rows).astype(jnp.int32)
        query_pos = first_row + jnp.arange(block_rows, dtype=jnp.int32)
        key_pos = first_row - WINDOW + jnp.arange(span, dtype=jnp.int32)
        allowed = (key_pos[None, :] <= query_pos[:, None]) & (key_pos[None, :] > query_pos[:, None] - WINDOW) & (key_pos[None, :] >= 0)
        query_block = lax.dynamic_slice_in_dim(queries, first_row, block_rows, 0)
        query_heads = query_block.astype(jnp.float32).reshape(block_rows, KH, groups, HD)
        key_heads = lax.dynamic_slice_in_dim(keys_pad, first_row, span, 0).astype(jnp.float32).reshape(span, KH, HD)
        value_heads = lax.dynamic_slice_in_dim(values_pad, first_row, span, 0).astype(jnp.float32).reshape(span, KH, HD)
        scores = jnp.einsum('qkgd,lkd->kgql', query_heads, key_heads) * score_scale
        scores = jnp.where(allowed, scores, -jnp.inf)
        maxima = lax.optimization_barrier(jnp.max(scores, axis=-1, keepdims=True))
        weights = jnp.exp(scores - maxima)
        probs = weights / lax.optimization_barrier(jnp.sum(weights, axis=-1, keepdims=True))
        probs_low = probs.astype(jnp.bfloat16)
        attended = jnp.einsum('kgql,lkd->qkgd', probs_low.astype(jnp.float32), value_heads).astype(jnp.bfloat16)
        attended_flat = attended.reshape(block_rows, QH * HD)
        grad_block = lax.dynamic_slice_in_dim(out_grad, first_row, block_rows, 0)
        out_block = jnp.dot(attended_flat, out_weight.T, preferred_element_type=jnp.float32).astype(jnp.bfloat16)
        attended_grad = jnp.dot(grad_block, out_weight, preferred_element_type=jnp.float32).astype(jnp.bfloat16)
        grad_heads = attended_grad.astype(jnp.float32).reshape(block_rows, KH, groups, HD)
        prob_grad = jnp.einsum('qkgd,lkd->kgql', grad_heads, value_heads)
        delta = jnp.einsum('qkgd,qkgd->kgq', grad_heads, attended.astype(jnp.float32))
        score_grad = (probs * (prob_grad - delta[..., None]) * score_scale).astype(jnp.bfloat16)
        query_grad = jnp.einsum('kgql,lkd->qkgd', score_grad.astype(jnp.float32), key_heads).astype(jnp.bfloat16).reshape(block_rows, QH * HD)
        key_terms = jnp.einsum('kgql,qkgd->lkd', score_grad.astype(jnp.float32), query_heads).reshape(span, key_width)
        value_terms = jnp.einsum('kgql,qkgd->lkd', probs_low.astype(jnp.float32), grad_heads).reshape(span, key_width)
        keys_grad = lax.dynamic_update_slice_in_dim(keys_grad, lax.dynamic_slice_in_dim(keys_grad, first_row, span, 0) + key_terms, first_row, 0)
        values_grad = lax.dynamic_update_slice_in_dim(values_grad, lax.dynamic_slice_in_dim(values_grad, first_row, span, 0) + value_terms, first_row, 0)
        weight_sum = weight_sum + jnp.dot(grad_block.T, attended_flat, preferred_element_type=jnp.float32)
        return ((keys_grad, values_grad, weight_sum), (out_block, query_grad))
    start_carry = (jnp.zeros((WINDOW + SEQLEN, key_width), jnp.float32), jnp.zeros((WINDOW + SEQLEN, key_width), jnp.float32), jnp.zeros((D, QH * HD), jnp.float32))
    finals, stacked = lax.scan(block_step, start_carry, jnp.arange(SEQLEN // block_rows, dtype=jnp.int32))
    keys_grad, values_grad, weight_sum = finals
    out_rows = stacked[0].reshape(SEQLEN, D)
    query_rows = stacked[1].reshape(SEQLEN, QH * HD)
    return (out_rows, query_rows, keys_grad[WINDOW:].astype(jnp.bfloat16), values_grad[WINDOW:].astype(jnp.bfloat16), weight_sum)

def reference(queries, key_rows, values, out_weight, out_grad):
    outs_list = []
    query_list = []
    key_list = []
    value_list = []
    weight_total = jnp.zeros((D, QH * HD), jnp.float32)
    for seq_number in range(SEQS):
        results = one_sequence(queries[seq_number], key_rows[seq_number], values[seq_number], out_weight, out_grad[seq_number])
        outs_list.append(results[0])
        query_list.append(results[1])
        key_list.append(results[2])
        value_list.append(results[3])
        weight_total = weight_total + results[4]
    weight_grad = weight_total / math.sqrt(SEQS * SEQLEN)
    return (jnp.stack(outs_list), jnp.stack(query_list), jnp.stack(key_list), jnp.stack(value_list), weight_grad)
```

```python
import functools
import math

import jax
import jax.numpy as jnp
from jax import lax
from jax.experimental import pallas as pl
from jax.experimental.pallas import tpu as pltpu
from jax.sharding import Mesh
from jax.sharding import PartitionSpec as P

QH = 4
KH = 2
HD = 256
WINDOW = 2048
GROUPS = QH // KH
LANES = 128
NEG = -1e30
F32 = jnp.float32
BF16 = jnp.bfloat16
NT = (((1,), (1,)), ((), ()))
TN = (((0,), (0,)), ((), ()))


def dot(a, b, dims=(((1,), (0,)), ((), ()))):
    return lax.dot_general(a, b, dims, preferred_element_type=F32)


def admitted(step, rows, core, query_axis):
    if step > 0 and (step + 1) * rows <= WINDOW:
        return None
    shape = (rows, rows)
    half = rows // 2
    query = (lax.broadcasted_iota(jnp.int32, shape, query_axis) + core * half) % rows
    key = (lax.broadcasted_iota(jnp.int32, shape, 1 - query_axis) + core * half) % rows
    gap = key - query - step * rows
    return (gap <= 0) & (gap > -WINDOW)


def forward_kernel(steps, rows, first, last, info, q, *refs):
    chunks = refs[: len(steps)]
    refs = refs[len(steps) :]
    if not first:
        m_in, l_in, acc_in = refs[:3]
        refs = refs[3:]
    if last:
        out, lse_t, m_s, l_s, acc_s = refs
    else:
        m_s, l_s, acc_s = refs
    chip, core = info[0], info[1]
    if not first:
        m_s[...] = m_in[...]
        l_s[...] = l_in[...]
        acc_s[...] = acc_in[...]
    for at, step in enumerate(steps):
        mask = admitted(step, rows, core, 0)

        def block(at=at, step=step, mask=mask):
            keys = chunks[at][:, :HD]
            vals = chunks[at][:, HD:]
            for h in range(GROUPS):
                cols = slice(h * HD, (h + 1) * HD)
                stat = slice(h * LANES, (h + 1) * LANES)
                s = dot(q[:, cols], keys, NT)
                if mask is not None:
                    s = jnp.where(mask, s, NEG)
                top = jnp.max(s, axis=1, keepdims=True)
                if step == 0:
                    p = jnp.exp(s - top)
                    total = jnp.sum(p, axis=1, keepdims=True)
                    acc_s[:, cols] = dot(p.astype(BF16), vals)
                else:
                    before = m_s[:, stat][:, :1]
                    top = jnp.maximum(top, before)
                    p = jnp.exp(s - top)
                    keep = jnp.exp(before - top)
                    total = keep * l_s[:, stat][:, :1] + jnp.sum(p, axis=1, keepdims=True)
                    acc_s[:, cols] = keep * acc_s[:, cols] + dot(p.astype(BF16), vals)
                m_s[:, stat] = jnp.broadcast_to(top, (rows, LANES))
                l_s[:, stat] = jnp.broadcast_to(total, (rows, LANES))

        if step == 0:
            block()
        else:
            pl.when(chip >= step)(block)
    if last:
        for h in range(GROUPS):
            cols = slice(h * HD, (h + 1) * HD)
            stat = slice(h * LANES, (h + 1) * LANES)
            total = l_s[:, stat]
            out[:, cols] = (acc_s[:, cols] / total[:, :1]).astype(BF16)
            lse = m_s[:, stat] + jnp.log(total)
            lse_t[h * 8 : (h + 1) * 8, :] = jnp.transpose(lse)[:8, :]


def forward(info, q, chunks, steps, state, last):
    rows = q.shape[0]
    first = state is None
    stat = jax.ShapeDtypeStruct((rows, GROUPS * LANES), F32)
    acc = jax.ShapeDtypeStruct((rows, GROUPS * HD), F32)
    vmem = pl.BlockSpec(memory_space=pltpu.VMEM)
    smem = pl.BlockSpec(memory_space=pltpu.SMEM)
    scratch = []
    if last:
        outs = (
            jax.ShapeDtypeStruct((rows, GROUPS * HD), BF16),
            jax.ShapeDtypeStruct((GROUPS * 8, rows), F32),
        )
        scratch = [pltpu.VMEM(s.shape, F32) for s in (stat, stat, acc)]
    else:
        outs = (stat, stat, acc)
    args = [info, q, *chunks] + ([] if first else list(state))
    return pl.pallas_call(
        functools.partial(forward_kernel, steps, rows, first, last),
        out_shape=outs,
        in_specs=[smem] + [vmem] * (len(args) - 1),
        out_specs=tuple(vmem for _ in outs),
        scratch_shapes=scratch,
        cost_estimate=pl.CostEstimate(
            flops=len(steps) * GROUPS * rows * rows * HD * 4,
            bytes_accessed=4 * rows * rows * len(steps),
            transcendentals=len(steps) * GROUPS * rows * rows,
        ),
        compiler_params=pltpu.CompilerParams(vmem_limit_bytes=32 * 1024 * 1024),
        name="attend_forward",
    )(*args)


def backward_kernel(steps, rows, first, last, info, q, da, lse_t, *refs):
    chunks = refs[: len(steps)]
    refs = refs[len(steps) :]
    if first:
        att = refs[0]
        refs = refs[1:]
    else:
        delta_t, dq_in = refs[:2]
        refs = refs[2:]
    grads = refs[: len(steps)]
    refs = refs[len(steps) :]
    if last:
        dq_out = refs[0]
        refs = refs[1:]
    if first:
        delta_t = refs[0]
        refs = refs[1:]
    dq_s = refs[0]
    chip, core = info[0], info[1]
    if first:
        for h in range(GROUPS):
            cols = slice(h * HD, (h + 1) * HD)
            prod = da[:, cols].astype(F32) * att[:, cols].astype(F32)
            delta = jnp.sum(prod, axis=1, keepdims=True)
            wide = jnp.broadcast_to(delta, (rows, LANES))
            delta_t[h * 8 : (h + 1) * 8, :] = jnp.transpose(wide)[:8, :]
        dq_s[...] = jnp.zeros_like(dq_s)
    else:
        dq_s[...] = dq_in[...]
    for at, step in enumerate(steps):
        mask = admitted(step, rows, core, 1)

        def block(at=at, mask=mask):
            keys = chunks[at][:, :HD]
            vals = chunks[at][:, HD:]
            for h in range(GROUPS):
                cols = slice(h * HD, (h + 1) * HD)
                qh = q[:, cols]
                dah = da[:, cols]
                s = dot(keys, qh, NT)
                p = jnp.exp(s - lse_t[h * 8 : h * 8 + 1, :])
                if mask is not None:
                    p = jnp.where(mask, p, 0.0)
                dp = dot(vals, dah, NT)
                ds = (p * (dp - delta_t[h * 8 : h * 8 + 1, :])).astype(BF16)
                dk = dot(ds, qh)
                dv = dot(p.astype(BF16), dah)
                dq_s[:, cols] += dot(ds, keys, TN)
                if h == 0:
                    dk_sum, dv_sum = dk, dv
                else:
                    dk_sum, dv_sum = dk_sum + dk, dv_sum + dv
            grads[at][:, :HD] = dk_sum.astype(grads[at].dtype)
            grads[at][:, HD:] = dv_sum.astype(grads[at].dtype)

        if step == 0:
            block()
        else:

            def blank(at=at):
                grads[at][...] = jnp.zeros_like(grads[at])

            pl.when(chip >= step)(block)
            pl.when(chip < step)(blank)
    if last:
        dq_out[...] = (dq_s[...] * HD ** (-0.5)).astype(BF16)


def backward(info, q, da, lse_t, chunks, steps, att, carried, last):
    rows = q.shape[0]
    first = carried is None
    vmem = pl.BlockSpec(memory_space=pltpu.VMEM)
    smem = pl.BlockSpec(memory_space=pltpu.SMEM)
    wide = (rows, GROUPS * HD)
    outs = [jax.ShapeDtypeStruct((rows, 2 * HD), F32 if s == 0 else BF16) for s in steps]
    if last:
        outs.append(jax.ShapeDtypeStruct(wide, BF16))
    if first:
        outs.append(jax.ShapeDtypeStruct((GROUPS * 8, rows), F32))
    scratch = []
    if last:
        scratch = [pltpu.VMEM(wide, F32)]
    else:
        outs.append(jax.ShapeDtypeStruct(wide, F32))
    args = [info, q, da, lse_t, *chunks] + ([att] if first else list(carried))
    return pl.pallas_call(
        functools.partial(backward_kernel, steps, rows, first, last),
        out_shape=tuple(outs),
        in_specs=[smem] + [vmem] * (len(args) - 1),
        out_specs=tuple(vmem for _ in outs),
        scratch_shapes=scratch,
        cost_estimate=pl.CostEstimate(
            flops=len(steps) * GROUPS * rows * rows * HD * 10,
            bytes_accessed=6 * rows * rows * len(steps),
            transcendentals=len(steps) * GROUPS * rows * rows,
        ),
        compiler_params=pltpu.CompilerParams(vmem_limit_bytes=32 * 1024 * 1024),
        name="attend_backward",
    )(*args)


def on_device(queries, key_rows, values, out_weight, out_grad):
    chip = lax.axis_index("chip")
    core = lax.axis_index("core")
    row = lax.axis_index("dp")
    chips = lax.axis_size("chip")
    rows_dp = lax.axis_size("dp")
    tok = queries.shape[1]
    rows = 2 * tok
    prior = min(-(-WINDOW // rows), chips - 1)
    steps = tuple(range(prior + 1))
    low = core == 0
    info = jnp.stack([chip, core]).astype(jnp.int32)

    def own(x):
        half = x.shape[1] // 2
        return jnp.where(low, x[:, :half], x[:, half:])

    def other(x):
        half = x.shape[1] // 2
        return jnp.where(low, x[:, half:], x[:, :half])

    def swap(x):
        return lax.ppermute(x, "core", [(0, 1), (1, 0)])

    def in_order(mine, theirs, axis):
        return jnp.where(
            low,
            jnp.concatenate([mine, theirs], axis),
            jnp.concatenate([theirs, mine], axis),
        )

    block = in_order(own(out_weight), swap(other(out_weight)), 0)
    part = block.shape[0]
    if chips <= 4:
        weight_z = jnp.zeros((chips * part, block.shape[1]), BF16)
        weight_z = lax.dynamic_update_slice_in_dim(weight_z, block, chip * part, 0)
        for k in range(1, chips):
            got = lax.ppermute(block, "chip", [(i, (i + k) % chips) for i in range(chips)])
            source = lax.rem(chip - k + chips, chips)
            weight_z = lax.dynamic_update_slice_in_dim(weight_z, got, source * part, 0)
    else:
        weight_z = lax.all_gather(block, "chip", axis=0, tiled=True)
    share = weight_z.shape[0]

    k0, v0 = key_rows[0], values[0]
    kv = jnp.concatenate([own(k0), own(v0)], 1)
    kv = jnp.concatenate([kv, swap(jnp.concatenate([other(k0), other(v0)], 1))], 0)
    chunks = [kv]
    for k in steps[1:]:
        chunks.append(lax.ppermute(kv, "chip", [(i, i + k) for i in range(chips - k)]))

    q0 = queries[0]
    q = jnp.concatenate([own(q0), swap(other(q0))], 0) * jnp.asarray(HD ** (-0.5), BF16)
    grad = jnp.concatenate([out_grad[0], swap(out_grad[0])], 0)

    weight = jnp.zeros((rows_dp * share, block.shape[1]), BF16)
    weight = lax.dynamic_update_slice_in_dim(weight, weight_z, row * share, 0)
    for k in range(1, rows_dp):
        got = lax.ppermute(weight_z, "dp", [(i, i ^ k) for i in range(rows_dp)])
        weight = lax.dynamic_update_slice_in_dim(weight, got, (row ^ k) * share, 0)

    state = forward(info, q, chunks[:-1], steps[:-1], None, False)
    att, lse_t = forward(info, q, chunks[-1:], steps[-1:], state, True)

    dw = dot(grad, att, TN)
    mine = lax.dynamic_slice_in_dim(dw, row * share, share, 0)
    for k in range(1, rows_dp):
        sent = lax.dynamic_slice_in_dim(dw, (row ^ k) * share, share, 0).astype(BF16)
        mine = mine + lax.ppermute(sent, "dp", [(i, i ^ k) for i in range(rows_dp)]).astype(F32)
    if chips <= 4:
        final = lax.dynamic_slice_in_dim(mine, chip * part, part, 0)
        for k in range(1, chips):
            target = lax.rem(chip + k, chips)
            sent = lax.dynamic_slice_in_dim(mine, target * part, part, 0).astype(BF16)
            got = lax.ppermute(sent, "chip", [(i, (i + k) % chips) for i in range(chips)])
            final = final + got.astype(F32)
    else:
        final = lax.psum_scatter(mine, "chip", scatter_dimension=0, tiled=True)
    total_tokens = rows_dp * chips * rows
    final = final * (1.0 / math.sqrt(total_tokens))
    top, bottom = final[: part // 2], final[part // 2 :]
    weight_grad = in_order(jnp.where(low, top, bottom), swap(jnp.where(low, bottom, top)), 1)

    da = dot(grad, weight).astype(BF16)
    carried = None
    sums = {}
    for step in reversed(steps):
        last = step == 0
        res = backward(info, q, da, lse_t, [chunks[step]], (step,), att, carried, last)
        sums[step] = res[0]
        if carried is None:
            delta_t = res[1]
        if last:
            dq = res[1]
        else:
            carried = (delta_t, res[-1])
    kv_grad = sums[0]
    for k in reversed(steps[1:]):
        got = lax.ppermute(sums[k], "chip", [(i + k, i) for i in range(chips - k)])
        kv_grad = kv_grad + got.astype(F32)
    kv_grad = kv_grad.astype(BF16)

    weight_other = swap(weight)
    layer_out = (dot(att[:tok], weight, NT) + dot(swap(att[tok:]), weight_other, NT)).astype(BF16)

    query_grad = in_order(dq[:tok], swap(dq[tok:]), 1)
    theirs = swap(kv_grad[tok:])
    key_grad = in_order(kv_grad[:tok, :HD], theirs[:, :HD], 1)
    value_grad = in_order(kv_grad[:tok, HD:], theirs[:, HD:], 1)
    return (
        layer_out[None],
        query_grad[None],
        key_grad[None],
        value_grad[None],
        weight_grad,
    )


def solution(mesh):
    devices = mesh.devices
    pairs = Mesh(
        devices.reshape(devices.shape[0], devices.shape[1] // 2, 2), ("dp", "chip", "core")
    )
    tokens = P("dp", ("chip", "core"), None)
    features = P(("dp", "chip", "core"), None)
    return jax.shard_map(
        on_device,
        mesh=pairs,
        in_specs=(tokens, tokens, tokens, features, tokens),
        out_specs=(tokens, tokens, tokens, tokens, features),
        check_vma=False,
    )
```

```python
import functools
import math

import jax
import jax.numpy as jnp
from jax import lax
from jax.experimental import pallas as pl
from jax.experimental.pallas import tpu as pltpu
from jax.sharding import Mesh
from jax.sharding import PartitionSpec as P

QH = 4
KH = 2
HD = 256
WINDOW = 2048
GROUPS = QH // KH
LANES = 128
NEG = -1e30
F32 = jnp.float32
BF16 = jnp.bfloat16
NT = (((1,), (1,)), ((), ()))
TN = (((0,), (0,)), ((), ()))


def dot(a, b, dims=(((1,), (0,)), ((), ()))):
    return lax.dot_general(a, b, dims, preferred_element_type=F32)


def admitted(step, rows, core, query_axis):
    if step > 0 and (step + 1) * rows <= WINDOW:
        return None
    shape = (rows, rows)
    half = rows // 2
    query = (lax.broadcasted_iota(jnp.int32, shape, query_axis) + core * half) % rows
    key = (lax.broadcasted_iota(jnp.int32, shape, 1 - query_axis) + core * half) % rows
    gap = key - query - step * rows
    return (gap <= 0) & (gap > -WINDOW)


def forward_kernel(steps, rows, first, last, info, q, *refs):
    chunks = refs[: len(steps)]
    refs = refs[len(steps) :]
    if not first:
        m_in, l_in, acc_in = refs[:3]
        refs = refs[3:]
    if last:
        out, lse_t, m_s, l_s, acc_s = refs
    else:
        m_s, l_s, acc_s = refs
    chip, core = info[0], info[1]
    if not first:
        m_s[...] = m_in[...]
        l_s[...] = l_in[...]
        acc_s[...] = acc_in[...]
    for at, step in enumerate(steps):
        mask = admitted(step, rows, core, 0)

        def block(at=at, step=step, mask=mask):
            keys = chunks[at][:, :HD]
            vals = chunks[at][:, HD:]
            for h in range(GROUPS):
                cols = slice(h * HD, (h + 1) * HD)
                stat = slice(h * LANES, (h + 1) * LANES)
                s = dot(q[:, cols], keys, NT)
                if mask is not None:
                    s = jnp.where(mask, s, NEG)
                top = jnp.max(s, axis=1, keepdims=True)
                if step == 0:
                    p = jnp.exp(s - top)
                    total = jnp.sum(p, axis=1, keepdims=True)
                    acc_s[:, cols] = dot(p.astype(BF16), vals)
                else:
                    before = m_s[:, stat][:, :1]
                    top = jnp.maximum(top, before)
                    p = jnp.exp(s - top)
                    keep = jnp.exp(before - top)
                    total = keep * l_s[:, stat][:, :1] + jnp.sum(p, axis=1, keepdims=True)
                    acc_s[:, cols] = keep * acc_s[:, cols] + dot(p.astype(BF16), vals)
                m_s[:, stat] = jnp.broadcast_to(top, (rows, LANES))
                l_s[:, stat] = jnp.broadcast_to(total, (rows, LANES))

        if step == 0:
            block()
        else:
            pl.when(chip >= step)(block)
    if last:
        for h in range(GROUPS):
            cols = slice(h * HD, (h + 1) * HD)
            stat = slice(h * LANES, (h + 1) * LANES)
            total = l_s[:, stat]
            out[:, cols] = (acc_s[:, cols] / total[:, :1]).astype(BF16)
            lse = m_s[:, stat] + jnp.log(total)
            lse_t[h * 8 : (h + 1) * 8, :] = jnp.transpose(lse)[:8, :]


def forward(info, q, chunks, steps, state, last):
    rows = q.shape[0]
    first = state is None
    stat = jax.ShapeDtypeStruct((rows, GROUPS * LANES), F32)
    acc = jax.ShapeDtypeStruct((rows, GROUPS * HD), F32)
    vmem = pl.BlockSpec(memory_space=pltpu.VMEM)
    smem = pl.BlockSpec(memory_space=pltpu.SMEM)
    scratch = []
    if last:
        outs = (
            jax.ShapeDtypeStruct((rows, GROUPS * HD), BF16),
            jax.ShapeDtypeStruct((GROUPS * 8, rows), F32),
        )
        scratch = [pltpu.VMEM(s.shape, F32) for s in (stat, stat, acc)]
    else:
        outs = (stat, stat, acc)
    args = [info, q, *chunks] + ([] if first else list(state))
    return pl.pallas_call(
        functools.partial(forward_kernel, steps, rows, first, last),
        out_shape=outs,
        in_specs=[smem] + [vmem] * (len(args) - 1),
        out_specs=tuple(vmem for _ in outs),
        scratch_shapes=scratch,
        cost_estimate=pl.CostEstimate(
            flops=len(steps) * GROUPS * rows * rows * HD * 4,
            bytes_accessed=4 * rows * rows * len(steps),
            transcendentals=len(steps) * GROUPS * rows * rows,
        ),
        compiler_params=pltpu.CompilerParams(vmem_limit_bytes=32 * 1024 * 1024),
        name="attend_forward",
    )(*args)


def backward_kernel(steps, rows, first, last, info, q, da, lse_t, *refs):
    chunks = refs[: len(steps)]
    refs = refs[len(steps) :]
    if first:
        att = refs[0]
        refs = refs[1:]
    else:
        delta_t, dq_in = refs[:2]
        refs = refs[2:]
    grads = refs[: len(steps)]
    refs = refs[len(steps) :]
    if last:
        dq_out = refs[0]
        refs = refs[1:]
    if first:
        delta_t = refs[0]
        refs = refs[1:]
    dq_s = refs[0]
    chip, core = info[0], info[1]
    if first:
        for h in range(GROUPS):
            cols = slice(h * HD, (h + 1) * HD)
            prod = da[:, cols].astype(F32) * att[:, cols].astype(F32)
            delta = jnp.sum(prod, axis=1, keepdims=True)
            wide = jnp.broadcast_to(delta, (rows, LANES))
            delta_t[h * 8 : (h + 1) * 8, :] = jnp.transpose(wide)[:8, :]
        dq_s[...] = jnp.zeros_like(dq_s)
    else:
        dq_s[...] = dq_in[...]
    for at, step in enumerate(steps):
        mask = admitted(step, rows, core, 1)

        def block(at=at, mask=mask):
            keys = chunks[at][:, :HD]
            vals = chunks[at][:, HD:]
            for h in range(GROUPS):
                cols = slice(h * HD, (h + 1) * HD)
                qh = q[:, cols]
                dah = da[:, cols]
                s = dot(keys, qh, NT)
                p = jnp.exp(s - lse_t[h * 8 : h * 8 + 1, :])
                if mask is not None:
                    p = jnp.where(mask, p, 0.0)
                dp = dot(vals, dah, NT)
                ds = (p * (dp - delta_t[h * 8 : h * 8 + 1, :])).astype(BF16)
                dk = dot(ds, qh)
                dv = dot(p.astype(BF16), dah)
                dq_s[:, cols] += dot(ds, keys, TN)
                if h == 0:
                    dk_sum, dv_sum = dk, dv
                else:
                    dk_sum, dv_sum = dk_sum + dk, dv_sum + dv
            grads[at][:, :HD] = dk_sum.astype(grads[at].dtype)
            grads[at][:, HD:] = dv_sum.astype(grads[at].dtype)

        if step == 0:
            block()
        else:

            def blank(at=at):
                grads[at][...] = jnp.zeros_like(grads[at])

            pl.when(chip >= step)(block)
            pl.when(chip < step)(blank)
    if last:
        dq_out[...] = (dq_s[...] * HD ** (-0.5)).astype(BF16)


def backward(info, q, da, lse_t, chunks, steps, att, carried, last):
    rows = q.shape[0]
    first = carried is None
    vmem = pl.BlockSpec(memory_space=pltpu.VMEM)
    smem = pl.BlockSpec(memory_space=pltpu.SMEM)
    wide = (rows, GROUPS * HD)
    outs = [jax.ShapeDtypeStruct((rows, 2 * HD), F32 if s == 0 else BF16) for s in steps]
    if last:
        outs.append(jax.ShapeDtypeStruct(wide, BF16))
    if first:
        outs.append(jax.ShapeDtypeStruct((GROUPS * 8, rows), F32))
    scratch = []
    if last:
        scratch = [pltpu.VMEM(wide, F32)]
    else:
        outs.append(jax.ShapeDtypeStruct(wide, F32))
    args = [info, q, da, lse_t, *chunks] + ([att] if first else list(carried))
    return pl.pallas_call(
        functools.partial(backward_kernel, steps, rows, first, last),
        out_shape=tuple(outs),
        in_specs=[smem] + [vmem] * (len(args) - 1),
        out_specs=tuple(vmem for _ in outs),
        scratch_shapes=scratch,
        cost_estimate=pl.CostEstimate(
            flops=len(steps) * GROUPS * rows * rows * HD * 10,
            bytes_accessed=6 * rows * rows * len(steps),
            transcendentals=len(steps) * GROUPS * rows * rows,
        ),
        compiler_params=pltpu.CompilerParams(vmem_limit_bytes=32 * 1024 * 1024),
        name="attend_backward",
    )(*args)


def on_device(queries, key_rows, values, out_weight, out_grad):
    chip = lax.axis_index("chip")
    core = lax.axis_index("core")
    row = lax.axis_index("dp")
    chips = lax.axis_size("chip")
    rows_dp = lax.axis_size("dp")
    tok = queries.shape[1]
    rows = 2 * tok
    prior = min(-(-WINDOW // rows), chips - 1)
    steps = tuple(range(prior + 1))
    low = core == 0
    info = jnp.stack([chip, core]).astype(jnp.int32)
    together = lax.optimization_barrier

    def own(x):
        half = x.shape[-1] // 2
        return jnp.where(low, x[..., :half], x[..., half:])

    def other(x):
        half = x.shape[-1] // 2
        return jnp.where(low, x[..., half:], x[..., :half])

    def swap(x):
        return lax.ppermute(x, "core", [(0, 1), (1, 0)])

    def up(x, k):
        return lax.ppermute(x, "chip", [(i, i + k) for i in range(chips - k)])

    def down(x, k):
        return lax.ppermute(x, "chip", [(i + k, i) for i in range(chips - k)])

    def round_chips(x, k):
        return lax.ppermute(x, "chip", [(i, (i + k) % chips) for i in range(chips)])

    def across(x, k):
        return lax.ppermute(x, "dp", [(i, i ^ k) for i in range(rows_dp)])

    def in_order(mine, theirs, axis):
        return jnp.where(
            low,
            jnp.concatenate([mine, theirs], axis),
            jnp.concatenate([theirs, mine], axis),
        )

    k0, v0, q0, g0 = key_rows[0], values[0], queries[0], out_grad[0]
    near = chips <= 4
    moved = [round_chips(out_weight, k) for k in range(1, chips)] if near else []
    kv_theirs = swap(jnp.concatenate([other(k0), other(v0)], 1))
    grad_theirs = swap(g0)
    kv_theirs, grad_theirs, *moved = together((kv_theirs, grad_theirs, *moved))

    kv = jnp.concatenate([own(k0), own(v0)], 1)
    kv = jnp.concatenate([kv, kv_theirs], 0)
    chunks = [kv] + [up(kv, k) for k in steps[1:3]]
    piece = out_weight.shape[0]
    part = 2 * piece
    if near:
        column = jnp.zeros((chips, *out_weight.shape), BF16)
        column = lax.dynamic_update_index_in_dim(column, out_weight, chip, 0)
        for k, got in enumerate(moved, 1):
            source = lax.rem(chip - k + chips, chips)
            column = lax.dynamic_update_index_in_dim(column, got, source, 0)
    else:
        column = lax.all_gather(out_weight, "chip", axis=0)
    column_theirs, q_theirs = together((swap(other(column)), swap(other(q0))))
    ours = in_order(own(column)[:, None], column_theirs[:, None], 1)
    ours = ours.reshape(chips * part, ours.shape[-1])
    share = ours.shape[0]
    half = share // 2

    by_x, by_y, *chunks = together((across(ours, 1), across(ours, 2), *chunks))
    for k in steps[3:]:
        chunks.append(up(chunks[-1], 1))
    diagonal = [across(by_y[:half], 1), across(by_x[half:], 2)]
    weight = jnp.zeros((rows_dp * share, ours.shape[1]), BF16)
    for got, at in (
        (ours, row * share),
        (by_x, (row ^ 1) * share),
        (by_y, (row ^ 2) * share),
        (diagonal[0], (row ^ 3) * share),
        (diagonal[1], (row ^ 3) * share + half),
    ):
        weight = lax.dynamic_update_slice_in_dim(weight, got, at, 0)

    q = jnp.concatenate([own(q0), q_theirs], 0) * jnp.asarray(HD ** (-0.5), BF16)
    grad = jnp.concatenate([g0, grad_theirs], 0)
    turned = grad.T
    blocks = [
        lax.dynamic_slice_in_dim(turned, (row ^ k) * share, share, 0) for k in range(rows_dp)
    ]
    state = forward(info, q, chunks[:-1], steps[:-1], None, False)
    da = dot(grad, weight).astype(BF16)
    da, chunks[-1], *blocks = together((da, chunks[-1], *blocks))
    att, lse_t = forward(info, q, chunks[-1:], steps[-1:], state, True)

    dw = [dot(b, att) for b in blocks]
    far = dw[3].astype(BF16)
    far, da = together((far, da))
    from_x, from_y = across(far[:half], 1), across(far[half:], 2)
    carried = None
    terms = {}
    order = [*range(prior, 2, -1), *([1, 2] if prior >= 2 else [1][:prior]), 0]
    for step in order:
        last = step == 0
        res = backward(info, q, da, lse_t, [chunks[step]], (step,), att, carried, last)
        terms[step] = res[0]
        if carried is None:
            delta_t = res[1]
        if last:
            dq = res[1]
        else:
            carried = (delta_t, res[-1])
    to_x = jnp.concatenate([dw[1][:half], dw[1][half:] + from_y.astype(F32)], 0).astype(BF16)
    to_y = jnp.concatenate([dw[2][:half] + from_x.astype(F32), dw[2][half:]], 0).astype(BF16)
    coming = [down(terms[1], 1), down(terms[prior], 1)] if prior >= 2 else []
    by_x, by_y, dq_theirs, *coming = together(
        (across(to_x, 1), across(to_y, 2), swap(dq[tok:]), *coming)
    )
    mine = dw[0] + by_x.astype(F32) + by_y.astype(F32)

    kv_grad = terms[0]
    if prior >= 2:
        far_term = coming[1]
        for k in range(prior - 1, 2, -1):
            far_term = down((terms[k].astype(F32) + far_term.astype(F32)).astype(BF16), 1)
        passing = terms[2]
        if prior >= 3:
            passing = (passing.astype(F32) + far_term.astype(F32)).astype(BF16)
        kv_grad = kv_grad + coming[0].astype(F32)
        coming = down(passing, 2)
    else:
        coming = down(terms[1], 1)
    att, mine = together((att, mine))
    partial = dot(att, weight, NT)
    layer_theirs = swap(partial[tok:].astype(BF16))
    if near:
        final = lax.dynamic_slice_in_dim(mine, chip * part, part, 0)
        got = []
        for k in range(1, chips):
            target = lax.rem(chip + k, chips)
            sent = lax.dynamic_slice_in_dim(mine, target * part, part, 0).astype(BF16)
            got.append(round_chips(sent, k))
        coming, layer_theirs, *got = together((coming, layer_theirs, *got))
        for x in got:
            final = final + x.astype(F32)
    else:
        final = lax.psum_scatter(mine, "chip", scatter_dimension=0, tiled=True)
    layer_out = (partial[:tok] + layer_theirs.astype(F32)).astype(BF16)
    total_tokens = rows_dp * chips * rows
    final = final * (1.0 / math.sqrt(total_tokens))
    first_rows, last_rows = final[:piece], final[piece:]
    weight_grad = in_order(
        jnp.where(low, first_rows, last_rows), swap(jnp.where(low, last_rows, first_rows)), 1
    )
    kv_grad = (kv_grad + coming.astype(F32)).astype(BF16)
    query_grad = in_order(dq[:tok], dq_theirs, 1)
    theirs = swap(kv_grad[tok:])
    key_grad = in_order(kv_grad[:tok, :HD], theirs[:, :HD], 1)
    value_grad = in_order(kv_grad[:tok, HD:], theirs[:, HD:], 1)
    return (
        layer_out[None],
        query_grad[None],
        key_grad[None],
        value_grad[None],
        weight_grad,
    )


def solution(mesh):
    devices = mesh.devices
    pairs = Mesh(
        devices.reshape(devices.shape[0], devices.shape[1] // 2, 2), ("dp", "chip", "core")
    )
    tokens = P("dp", ("chip", "core"), None)
    features = P(("dp", "chip", "core"), None)
    return jax.shard_map(
        on_device,
        mesh=pairs,
        in_specs=(tokens, tokens, tokens, features, tokens),
        out_specs=(tokens, tokens, tokens, tokens, features),
        check_vma=False,
    )
```

```python
import functools
import math

import jax
import jax.numpy as jnp
from jax import lax
from jax.experimental import pallas as pl
from jax.experimental.pallas import tpu as pltpu
from jax.sharding import Mesh
from jax.sharding import PartitionSpec as P

QH = 4
KH = 2
HD = 256
WINDOW = 2048
GROUPS = QH // KH
LANES = 128
NEG = -1e30
F32 = jnp.float32
BF16 = jnp.bfloat16
NT = (((1,), (1,)), ((), ()))
TN = (((0,), (0,)), ((), ()))


def dot(a, b, dims=(((1,), (0,)), ((), ()))):
    return lax.dot_general(a, b, dims, preferred_element_type=F32)


def admitted(step, rows, core, query_axis):
    if step > 0 and (step + 1) * rows <= WINDOW:
        return None
    shape = (rows, rows)
    half = rows // 2
    query = (lax.broadcasted_iota(jnp.int32, shape, query_axis) + core * half) % rows
    key = (lax.broadcasted_iota(jnp.int32, shape, 1 - query_axis) + core * half) % rows
    gap = key - query - step * rows
    return (gap <= 0) & (gap > -WINDOW)


def forward_kernel(steps, rows, first, last, info, q, *refs):
    chunks = refs[: len(steps)]
    refs = refs[len(steps) :]
    if not first:
        m_in, l_in, acc_in = refs[:3]
        refs = refs[3:]
    if last:
        out, lse_t, m_s, l_s, acc_s = refs
    else:
        m_s, l_s, acc_s = refs
    chip, core = info[0], info[1]
    if not first:
        m_s[...] = m_in[...]
        l_s[...] = l_in[...]
        acc_s[...] = acc_in[...]
    for at, step in enumerate(steps):
        mask = admitted(step, rows, core, 0)

        def block(at=at, step=step, mask=mask):
            keys = chunks[at][:, :HD]
            vals = chunks[at][:, HD:]
            for h in range(GROUPS):
                cols = slice(h * HD, (h + 1) * HD)
                stat = slice(h * LANES, (h + 1) * LANES)
                s = dot(q[:, cols], keys, NT)
                if mask is not None:
                    s = jnp.where(mask, s, NEG)
                top = jnp.max(s, axis=1, keepdims=True)
                if step == 0:
                    p = jnp.exp(s - top)
                    total = jnp.sum(p, axis=1, keepdims=True)
                    acc_s[:, cols] = dot(p.astype(BF16), vals)
                else:
                    before = m_s[:, stat][:, :1]
                    top = jnp.maximum(top, before)
                    p = jnp.exp(s - top)
                    keep = jnp.exp(before - top)
                    total = keep * l_s[:, stat][:, :1] + jnp.sum(p, axis=1, keepdims=True)
                    acc_s[:, cols] = keep * acc_s[:, cols] + dot(p.astype(BF16), vals)
                m_s[:, stat] = jnp.broadcast_to(top, (rows, LANES))
                l_s[:, stat] = jnp.broadcast_to(total, (rows, LANES))

        if step == 0:
            block()
        else:
            pl.when(chip >= step)(block)
    if last:
        for h in range(GROUPS):
            cols = slice(h * HD, (h + 1) * HD)
            stat = slice(h * LANES, (h + 1) * LANES)
            total = l_s[:, stat]
            out[:, cols] = (acc_s[:, cols] / total[:, :1]).astype(BF16)
            lse = m_s[:, stat] + jnp.log(total)
            lse_t[h * 8 : (h + 1) * 8, :] = jnp.transpose(lse)[:8, :]


def forward(info, q, chunks, steps, state, last):
    rows = q.shape[0]
    first = state is None
    stat = jax.ShapeDtypeStruct((rows, GROUPS * LANES), F32)
    acc = jax.ShapeDtypeStruct((rows, GROUPS * HD), F32)
    vmem = pl.BlockSpec(memory_space=pltpu.VMEM)
    smem = pl.BlockSpec(memory_space=pltpu.SMEM)
    scratch = []
    if last:
        outs = (
            jax.ShapeDtypeStruct((rows, GROUPS * HD), BF16),
            jax.ShapeDtypeStruct((GROUPS * 8, rows), F32),
        )
        scratch = [pltpu.VMEM(s.shape, F32) for s in (stat, stat, acc)]
    else:
        outs = (stat, stat, acc)
    args = [info, q, *chunks] + ([] if first else list(state))
    return pl.pallas_call(
        functools.partial(forward_kernel, steps, rows, first, last),
        out_shape=outs,
        in_specs=[smem] + [vmem] * (len(args) - 1),
        out_specs=tuple(vmem for _ in outs),
        scratch_shapes=scratch,
        cost_estimate=pl.CostEstimate(
            flops=len(steps) * GROUPS * rows * rows * HD * 4,
            bytes_accessed=4 * rows * rows * len(steps),
            transcendentals=len(steps) * GROUPS * rows * rows,
        ),
        compiler_params=pltpu.CompilerParams(vmem_limit_bytes=32 * 1024 * 1024),
        name="attend_forward",
    )(*args)


def backward_kernel(steps, rows, first, last, info, q, da, lse_t, *refs):
    chunks = refs[: len(steps)]
    refs = refs[len(steps) :]
    if first:
        att = refs[0]
        refs = refs[1:]
    else:
        delta_t, dq_in = refs[:2]
        refs = refs[2:]
    grads = refs[: len(steps)]
    refs = refs[len(steps) :]
    if last:
        dq_out = refs[0]
        refs = refs[1:]
    if first:
        delta_t = refs[0]
        refs = refs[1:]
    dq_s = refs[0]
    chip, core = info[0], info[1]
    if first:
        for h in range(GROUPS):
            cols = slice(h * HD, (h + 1) * HD)
            prod = da[:, cols].astype(F32) * att[:, cols].astype(F32)
            delta = jnp.sum(prod, axis=1, keepdims=True)
            wide = jnp.broadcast_to(delta, (rows, LANES))
            delta_t[h * 8 : (h + 1) * 8, :] = jnp.transpose(wide)[:8, :]
        dq_s[...] = jnp.zeros_like(dq_s)
    else:
        dq_s[...] = dq_in[...]
    for at, step in enumerate(steps):
        mask = admitted(step, rows, core, 1)

        def block(at=at, mask=mask):
            keys = chunks[at][:, :HD]
            vals = chunks[at][:, HD:]
            for h in range(GROUPS):
                cols = slice(h * HD, (h + 1) * HD)
                qh = q[:, cols]
                dah = da[:, cols]
                s = dot(keys, qh, NT)
                p = jnp.exp(s - lse_t[h * 8 : h * 8 + 1, :])
                if mask is not None:
                    p = jnp.where(mask, p, 0.0)
                dp = dot(vals, dah, NT)
                ds = (p * (dp - delta_t[h * 8 : h * 8 + 1, :])).astype(BF16)
                dk = dot(ds, qh)
                dv = dot(p.astype(BF16), dah)
                dq_s[:, cols] += dot(ds, keys, TN)
                if h == 0:
                    dk_sum, dv_sum = dk, dv
                else:
                    dk_sum, dv_sum = dk_sum + dk, dv_sum + dv
            grads[at][:, :HD] = dk_sum.astype(grads[at].dtype)
            grads[at][:, HD:] = dv_sum.astype(grads[at].dtype)

        if step == 0:
            block()
        else:

            def blank(at=at):
                grads[at][...] = jnp.zeros_like(grads[at])

            pl.when(chip >= step)(block)
            pl.when(chip < step)(blank)
    if last:
        dq_out[...] = (dq_s[...] * HD ** (-0.5)).astype(BF16)


def backward(info, q, da, lse_t, chunks, steps, att, carried, last):
    rows = q.shape[0]
    first = carried is None
    vmem = pl.BlockSpec(memory_space=pltpu.VMEM)
    smem = pl.BlockSpec(memory_space=pltpu.SMEM)
    wide = (rows, GROUPS * HD)
    outs = [jax.ShapeDtypeStruct((rows, 2 * HD), F32 if s == 0 else BF16) for s in steps]
    if last:
        outs.append(jax.ShapeDtypeStruct(wide, BF16))
    if first:
        outs.append(jax.ShapeDtypeStruct((GROUPS * 8, rows), F32))
    scratch = []
    if last:
        scratch = [pltpu.VMEM(wide, F32)]
    else:
        outs.append(jax.ShapeDtypeStruct(wide, F32))
    args = [info, q, da, lse_t, *chunks] + ([att] if first else list(carried))
    return pl.pallas_call(
        functools.partial(backward_kernel, steps, rows, first, last),
        out_shape=tuple(outs),
        in_specs=[smem] + [vmem] * (len(args) - 1),
        out_specs=tuple(vmem for _ in outs),
        scratch_shapes=scratch,
        cost_estimate=pl.CostEstimate(
            flops=len(steps) * GROUPS * rows * rows * HD * 10,
            bytes_accessed=6 * rows * rows * len(steps),
            transcendentals=len(steps) * GROUPS * rows * rows,
        ),
        compiler_params=pltpu.CompilerParams(vmem_limit_bytes=32 * 1024 * 1024),
        name="attend_backward",
    )(*args)


def on_device(queries, key_rows, values, out_weight, out_grad):
    chip = lax.axis_index("chip")
    core = lax.axis_index("core")
    row = lax.axis_index("dp")
    chips = lax.axis_size("chip")
    rows_dp = lax.axis_size("dp")
    tok = queries.shape[1]
    rows = 2 * tok
    prior = min(-(-WINDOW // rows), chips - 1)
    steps = tuple(range(prior + 1))
    low = core == 0
    info = jnp.stack([chip, core]).astype(jnp.int32)
    together = lax.optimization_barrier

    def own(x):
        half = x.shape[-1] // 2
        return jnp.where(low, x[..., :half], x[..., half:])

    def other(x):
        half = x.shape[-1] // 2
        return jnp.where(low, x[..., half:], x[..., :half])

    def swap(x):
        return lax.ppermute(x, "core", [(0, 1), (1, 0)])

    def up(x, k):
        return lax.ppermute(x, "chip", [(i, i + k) for i in range(chips - k)])

    def down(x, k):
        return lax.ppermute(x, "chip", [(i + k, i) for i in range(chips - k)])

    def round_chips(x, k):
        return lax.ppermute(x, "chip", [(i, (i + k) % chips) for i in range(chips)])

    def across(x, k):
        return lax.ppermute(x, "dp", [(i, i ^ k) for i in range(rows_dp)])

    def in_order(mine, theirs, axis):
        return jnp.where(
            low,
            jnp.concatenate([mine, theirs], axis),
            jnp.concatenate([theirs, mine], axis),
        )

    k0, v0, q0, g0 = key_rows[0], values[0], queries[0], out_grad[0]
    near = chips <= 4
    moved = [round_chips(out_weight, k) for k in range(1, chips)] if near else []
    kv_theirs = swap(jnp.concatenate([other(k0), other(v0)], 1))
    kv = jnp.concatenate([own(k0), own(v0)], 1)
    kv = jnp.concatenate([kv, kv_theirs], 0)
    hop = up(kv, 1)
    hop, grad_theirs, *moved = together((hop, swap(g0), *moved))
    chunks = [kv, hop]

    piece = out_weight.shape[0]
    part = 2 * piece
    if near:
        column = jnp.zeros((chips, *out_weight.shape), BF16)
        column = lax.dynamic_update_index_in_dim(column, out_weight, chip, 0)
        for k, got in enumerate(moved, 1):
            source = lax.rem(chip - k + chips, chips)
            column = lax.dynamic_update_index_in_dim(column, got, source, 0)
    else:
        column = lax.all_gather(out_weight, "chip", axis=0)
    column_theirs, q_theirs = together((swap(other(column)), swap(other(q0))))
    ours = in_order(own(column)[:, None], column_theirs[:, None], 1)
    ours = ours.reshape(chips * part, ours.shape[-1])
    share = ours.shape[0]
    half = share // 2

    by_x, by_y, hop = together((across(ours, 1), across(ours, 2), up(hop, 1)))
    chunks.append(hop)
    diagonal = [across(by_y[:half], 1), across(by_x[half:], 2)]
    diagonal[0], diagonal[1], hop = together((*diagonal, up(hop, 1)))
    chunks.append(hop)
    for _ in steps[4:]:
        chunks.append(up(chunks[-1], 1))
    weight = jnp.zeros((rows_dp * share, ours.shape[1]), BF16)
    for got, at in (
        (ours, row * share),
        (by_x, (row ^ 1) * share),
        (by_y, (row ^ 2) * share),
        (diagonal[0], (row ^ 3) * share),
        (diagonal[1], (row ^ 3) * share + half),
    ):
        weight = lax.dynamic_update_slice_in_dim(weight, got, at, 0)

    q = jnp.concatenate([own(q0), q_theirs], 0) * jnp.asarray(HD ** (-0.5), BF16)
    grad = jnp.concatenate([g0, grad_theirs], 0)
    turned = grad.T
    blocks = [
        lax.dynamic_slice_in_dim(turned, (row ^ k) * share, share, 0) for k in range(rows_dp)
    ]
    state = None
    for step in steps:
        state = forward(info, q, chunks[step : step + 1], (step,), state, step == prior)
    att, lse_t = state
    da = dot(grad, weight).astype(BF16)

    dw = [dot(b, att) for b in blocks]
    far = dw[3].astype(BF16)
    far, da = together((far, da))
    from_x, from_y = across(far[:half], 1), across(far[half:], 2)
    carried = None
    terms = {}
    for step in reversed(steps):
        last = step == 0
        res = backward(info, q, da, lse_t, [chunks[step]], (step,), att, carried, last)
        terms[step] = res[0]
        if carried is None:
            delta_t = res[1]
        if last:
            dq = res[1]
        else:
            carried = (delta_t, res[-1])

    passing = terms[prior]
    for step in range(prior - 1, 2, -1):
        passing = (terms[step].astype(F32) + down(passing, 1).astype(F32)).astype(BF16)
    from_x, from_y, got = together((from_x, from_y, down(passing, 1)))
    passing = (terms[2].astype(F32) + got.astype(F32)).astype(BF16)
    to_x = jnp.concatenate([dw[1][:half], dw[1][half:] + from_y.astype(F32)], 0).astype(BF16)
    to_y = jnp.concatenate([dw[2][:half] + from_x.astype(F32), dw[2][half:]], 0).astype(BF16)
    by_x, by_y, dq_theirs, got = together(
        (across(to_x, 1), across(to_y, 2), swap(dq[tok:]), down(passing, 1))
    )
    mine = dw[0] + by_x.astype(F32) + by_y.astype(F32)

    passing = (terms[1].astype(F32) + got.astype(F32)).astype(BF16)
    coming = down(passing, 1)
    att, mine = together((att, mine))
    partial = dot(att, weight, NT)
    layer_theirs = swap(partial[tok:].astype(BF16))
    if near:
        final = lax.dynamic_slice_in_dim(mine, chip * part, part, 0)
        got = []
        for k in range(1, chips):
            target = lax.rem(chip + k, chips)
            sent = lax.dynamic_slice_in_dim(mine, target * part, part, 0).astype(BF16)
            got.append(round_chips(sent, k))
        coming, layer_theirs, *got = together((coming, layer_theirs, *got))
        for x in got:
            final = final + x.astype(F32)
    else:
        final = lax.psum_scatter(mine, "chip", scatter_dimension=0, tiled=True)
    layer_out = (partial[:tok] + layer_theirs.astype(F32)).astype(BF16)
    total_tokens = rows_dp * chips * rows
    final = final * (1.0 / math.sqrt(total_tokens))
    first_rows, last_rows = final[:piece], final[piece:]
    weight_grad = in_order(
        jnp.where(low, first_rows, last_rows), swap(jnp.where(low, last_rows, first_rows)), 1
    )
    kv_grad = (terms[0] + coming.astype(F32)).astype(BF16)
    query_grad = in_order(dq[:tok], dq_theirs, 1)
    theirs = swap(kv_grad[tok:])
    key_grad = in_order(kv_grad[:tok, :HD], theirs[:, :HD], 1)
    value_grad = in_order(kv_grad[:tok, HD:], theirs[:, HD:], 1)
    return (
        layer_out[None],
        query_grad[None],
        key_grad[None],
        value_grad[None],
        weight_grad,
    )


def solution(mesh):
    devices = mesh.devices
    pairs = Mesh(
        devices.reshape(devices.shape[0], devices.shape[1] // 2, 2), ("dp", "chip", "core")
    )
    tokens = P("dp", ("chip", "core"), None)
    features = P(("dp", "chip", "core"), None)
    return jax.shard_map(
        on_device,
        mesh=pairs,
        in_specs=(tokens, tokens, tokens, features, tokens),
        out_specs=(tokens, tokens, tokens, tokens, features),
        check_vma=False,
    )
```

```python
import functools
import math

import jax
import jax.numpy as jnp
from jax import lax
from jax.experimental import pallas as pl
from jax.experimental.pallas import tpu as pltpu
from jax.sharding import Mesh
from jax.sharding import PartitionSpec as P

QH = 4
KH = 2
HD = 256
WINDOW = 2048
GROUPS = QH // KH
LANES = 128
NEG = -1e30
F32 = jnp.float32
BF16 = jnp.bfloat16
NT = (((1,), (1,)), ((), ()))
TN = (((0,), (0,)), ((), ()))


def dot(a, b, dims=(((1,), (0,)), ((), ()))):
    return lax.dot_general(a, b, dims, preferred_element_type=F32)


def admitted(step, rows, core, query_axis):
    if step > 0 and (step + 1) * rows <= WINDOW:
        return None
    shape = (rows, rows)
    half = rows // 2
    query = (lax.broadcasted_iota(jnp.int32, shape, query_axis) + core * half) % rows
    key = (lax.broadcasted_iota(jnp.int32, shape, 1 - query_axis) + core * half) % rows
    gap = key - query - step * rows
    return (gap <= 0) & (gap > -WINDOW)


def forward_kernel(steps, rows, first, last, info, q, *refs):
    chunks = refs[: len(steps)]
    refs = refs[len(steps) :]
    if not first:
        m_in, l_in, acc_in = refs[:3]
        refs = refs[3:]
    if last:
        out, lse_t, m_s, l_s, acc_s = refs
    else:
        m_s, l_s, acc_s = refs
    chip, core = info[0], info[1]
    if not first:
        m_s[...] = m_in[...]
        l_s[...] = l_in[...]
        acc_s[...] = acc_in[...]
    for at, step in enumerate(steps):
        mask = admitted(step, rows, core, 0)

        def block(at=at, step=step, mask=mask):
            keys = chunks[at][:, :HD]
            vals = chunks[at][:, HD:]
            for h in range(GROUPS):
                cols = slice(h * HD, (h + 1) * HD)
                stat = slice(h * LANES, (h + 1) * LANES)
                s = dot(q[:, cols], keys, NT)
                if mask is not None:
                    s = jnp.where(mask, s, NEG)
                top = jnp.max(s, axis=1, keepdims=True)
                if step == 0:
                    p = jnp.exp(s - top)
                    total = jnp.sum(p, axis=1, keepdims=True)
                    acc_s[:, cols] = dot(p.astype(BF16), vals)
                else:
                    before = m_s[:, stat][:, :1]
                    top = jnp.maximum(top, before)
                    p = jnp.exp(s - top)
                    keep = jnp.exp(before - top)
                    total = keep * l_s[:, stat][:, :1] + jnp.sum(p, axis=1, keepdims=True)
                    acc_s[:, cols] = keep * acc_s[:, cols] + dot(p.astype(BF16), vals)
                m_s[:, stat] = jnp.broadcast_to(top, (rows, LANES))
                l_s[:, stat] = jnp.broadcast_to(total, (rows, LANES))

        if step == 0:
            block()
        else:
            pl.when(chip >= step)(block)
    if last:
        for h in range(GROUPS):
            cols = slice(h * HD, (h + 1) * HD)
            stat = slice(h * LANES, (h + 1) * LANES)
            total = l_s[:, stat]
            out[:, cols] = (acc_s[:, cols] / total[:, :1]).astype(BF16)
            lse = m_s[:, stat] + jnp.log(total)
            lse_t[h * 8 : (h + 1) * 8, :] = jnp.transpose(lse)[:8, :]


def forward(info, q, chunks, steps, state, last):
    rows = q.shape[0]
    first = state is None
    stat = jax.ShapeDtypeStruct((rows, GROUPS * LANES), F32)
    acc = jax.ShapeDtypeStruct((rows, GROUPS * HD), F32)
    vmem = pl.BlockSpec(memory_space=pltpu.VMEM)
    smem = pl.BlockSpec(memory_space=pltpu.SMEM)
    scratch = []
    if last:
        outs = (
            jax.ShapeDtypeStruct((rows, GROUPS * HD), BF16),
            jax.ShapeDtypeStruct((GROUPS * 8, rows), F32),
        )
        scratch = [pltpu.VMEM(s.shape, F32) for s in (stat, stat, acc)]
    else:
        outs = (stat, stat, acc)
    args = [info, q, *chunks] + ([] if first else list(state))
    return pl.pallas_call(
        functools.partial(forward_kernel, steps, rows, first, last),
        out_shape=outs,
        in_specs=[smem] + [vmem] * (len(args) - 1),
        out_specs=tuple(vmem for _ in outs),
        scratch_shapes=scratch,
        cost_estimate=pl.CostEstimate(
            flops=len(steps) * GROUPS * rows * rows * HD * 4,
            bytes_accessed=4 * rows * rows * len(steps),
            transcendentals=len(steps) * GROUPS * rows * rows,
        ),
        compiler_params=pltpu.CompilerParams(vmem_limit_bytes=32 * 1024 * 1024),
        name="attend_forward",
    )(*args)


def backward_kernel(steps, rows, first, last, info, q, da, lse_t, *refs):
    chunks = refs[: len(steps)]
    refs = refs[len(steps) :]
    if first:
        att = refs[0]
        refs = refs[1:]
    else:
        delta_t, dq_in = refs[:2]
        refs = refs[2:]
    grads = refs[: len(steps)]
    refs = refs[len(steps) :]
    if last:
        dq_out = refs[0]
        refs = refs[1:]
    if first:
        delta_t = refs[0]
        refs = refs[1:]
    dq_s = refs[0]
    chip, core = info[0], info[1]
    if first:
        for h in range(GROUPS):
            cols = slice(h * HD, (h + 1) * HD)
            prod = da[:, cols].astype(F32) * att[:, cols].astype(F32)
            delta = jnp.sum(prod, axis=1, keepdims=True)
            wide = jnp.broadcast_to(delta, (rows, LANES))
            delta_t[h * 8 : (h + 1) * 8, :] = jnp.transpose(wide)[:8, :]
        dq_s[...] = jnp.zeros_like(dq_s)
    else:
        dq_s[...] = dq_in[...]
    for at, step in enumerate(steps):
        mask = admitted(step, rows, core, 1)

        def block(at=at, mask=mask):
            keys = chunks[at][:, :HD]
            vals = chunks[at][:, HD:]
            for h in range(GROUPS):
                cols = slice(h * HD, (h + 1) * HD)
                qh = q[:, cols]
                dah = da[:, cols]
                s = dot(keys, qh, NT)
                p = jnp.exp(s - lse_t[h * 8 : h * 8 + 1, :])
                if mask is not None:
                    p = jnp.where(mask, p, 0.0)
                dp = dot(vals, dah, NT)
                ds = (p * (dp - delta_t[h * 8 : h * 8 + 1, :])).astype(BF16)
                dk = dot(ds, qh)
                dv = dot(p.astype(BF16), dah)
                dq_s[:, cols] += dot(ds, keys, TN)
                if h == 0:
                    dk_sum, dv_sum = dk, dv
                else:
                    dk_sum, dv_sum = dk_sum + dk, dv_sum + dv
            grads[at][:, :HD] = dk_sum.astype(grads[at].dtype)
            grads[at][:, HD:] = dv_sum.astype(grads[at].dtype)

        if step == 0:
            block()
        else:

            def blank(at=at):
                grads[at][...] = jnp.zeros_like(grads[at])

            pl.when(chip >= step)(block)
            pl.when(chip < step)(blank)
    if last:
        dq_out[...] = (dq_s[...] * HD ** (-0.5)).astype(BF16)


def backward(info, q, da, lse_t, chunks, steps, att, carried, last):
    rows = q.shape[0]
    first = carried is None
    vmem = pl.BlockSpec(memory_space=pltpu.VMEM)
    smem = pl.BlockSpec(memory_space=pltpu.SMEM)
    wide = (rows, GROUPS * HD)
    outs = [jax.ShapeDtypeStruct((rows, 2 * HD), F32 if s == 0 else BF16) for s in steps]
    if last:
        outs.append(jax.ShapeDtypeStruct(wide, BF16))
    if first:
        outs.append(jax.ShapeDtypeStruct((GROUPS * 8, rows), F32))
    scratch = []
    if last:
        scratch = [pltpu.VMEM(wide, F32)]
    else:
        outs.append(jax.ShapeDtypeStruct(wide, F32))
    args = [info, q, da, lse_t, *chunks] + ([att] if first else list(carried))
    return pl.pallas_call(
        functools.partial(backward_kernel, steps, rows, first, last),
        out_shape=tuple(outs),
        in_specs=[smem] + [vmem] * (len(args) - 1),
        out_specs=tuple(vmem for _ in outs),
        scratch_shapes=scratch,
        cost_estimate=pl.CostEstimate(
            flops=len(steps) * GROUPS * rows * rows * HD * 10,
            bytes_accessed=6 * rows * rows * len(steps),
            transcendentals=len(steps) * GROUPS * rows * rows,
        ),
        compiler_params=pltpu.CompilerParams(vmem_limit_bytes=32 * 1024 * 1024),
        name="attend_backward",
    )(*args)


def on_device(queries, key_rows, values, out_weight, out_grad):
    chip = lax.axis_index("chip")
    core = lax.axis_index("core")
    row = lax.axis_index("dp")
    chips = lax.axis_size("chip")
    rows_dp = lax.axis_size("dp")
    tok = queries.shape[1]
    rows = 2 * tok
    prior = min(-(-WINDOW // rows), chips - 1)
    steps = tuple(range(prior + 1))
    low = core == 0
    info = jnp.stack([chip, core]).astype(jnp.int32)
    together = lax.optimization_barrier

    def own(x):
        half = x.shape[-1] // 2
        return jnp.where(low, x[..., :half], x[..., half:])

    def other(x):
        half = x.shape[-1] // 2
        return jnp.where(low, x[..., half:], x[..., :half])

    def swap(x):
        return lax.ppermute(x, "core", [(0, 1), (1, 0)])

    def up(x, k):
        return lax.ppermute(x, "chip", [(i, i + k) for i in range(chips - k)])

    def down(x, k):
        return lax.ppermute(x, "chip", [(i + k, i) for i in range(chips - k)])

    def round_chips(x, k):
        return lax.ppermute(x, "chip", [(i, (i + k) % chips) for i in range(chips)])

    def across(x, k):
        return lax.ppermute(x, "dp", [(i, i ^ k) for i in range(rows_dp)])

    def in_order(mine, theirs, axis):
        return jnp.where(
            low,
            jnp.concatenate([mine, theirs], axis),
            jnp.concatenate([theirs, mine], axis),
        )

    k0, v0, q0, g0 = key_rows[0], values[0], queries[0], out_grad[0]
    near = chips <= 4
    moved = [round_chips(out_weight, k) for k in range(1, chips)] if near else []
    kv_theirs = swap(jnp.concatenate([other(k0), other(v0)], 1))
    kv = jnp.concatenate([own(k0), own(v0)], 1)
    kv = jnp.concatenate([kv, kv_theirs], 0)
    hop = up(kv, 1)
    q = jnp.concatenate([own(q0), swap(other(q0))], 0) * jnp.asarray(HD ** (-0.5), BF16)
    state = forward(info, q, [kv], (0,), None, False)
    hop, q, state, *moved = together((hop, q, state, *moved))
    chunks = [kv, hop]

    piece = out_weight.shape[0]
    part = 2 * piece
    if near:
        column = jnp.zeros((chips, *out_weight.shape), BF16)
        column = lax.dynamic_update_index_in_dim(column, out_weight, chip, 0)
        for k, got in enumerate(moved, 1):
            source = lax.rem(chip - k + chips, chips)
            column = lax.dynamic_update_index_in_dim(column, got, source, 0)
    else:
        column = lax.all_gather(out_weight, "chip", axis=0)
    ours = in_order(own(column)[:, None], swap(other(column))[:, None], 1)
    ours = ours.reshape(chips * part, ours.shape[-1])
    share = ours.shape[0]
    half = share // 2

    lower, upper = ours[:half], ours[half:]
    hop = up(hop, 1)
    state = forward(info, q, chunks[1:2], (1,), state, False)
    *by_plane, hop, state = together(
        (across(lower, 1), across(upper, 1), across(lower, 2), across(upper, 2), hop, state)
    )
    chunks.append(hop)
    diagonal = [across(by_plane[2], 1), across(by_plane[1], 2)]
    grad = jnp.concatenate([g0, swap(g0)], 0)
    turned = grad.T
    blocks = [
        lax.dynamic_slice_in_dim(turned, (row ^ k) * share + at, half, 0)
        for k in range(rows_dp)
        for at in (0, half)
    ]
    last_hop = up(hop, 1)
    for step in steps[2:prior]:
        state = forward(info, q, [hop], (step,), state, False)
        hop = last_hop
        if step + 1 < prior:
            chunks.append(hop)
            last_hop = up(hop, 1)
    weight = jnp.zeros((rows_dp * share, ours.shape[1]), BF16)
    for got, k, at in (
        (ours, 0, 0),
        (by_plane[0], 1, 0),
        (by_plane[1], 1, half),
        (by_plane[2], 2, 0),
        (by_plane[3], 2, half),
        (diagonal[0], 3, 0),
        (diagonal[1], 3, half),
    ):
        weight = lax.dynamic_update_slice_in_dim(weight, got, (row ^ k) * share + at, 0)
    da = dot(grad, weight).astype(BF16)
    da, last_hop, state, *blocks = together((da, last_hop, state, *blocks))
    chunks.append(last_hop)
    att, lse_t = forward(info, q, [last_hop], (prior,), state, True)

    to_x, to_y, far_x, far_y = [dot(blocks[i], att).astype(BF16) for i in (2, 5, 6, 7)]
    to_x, to_y, far_x, far_y, da, att = together((to_x, to_y, far_x, far_y, da, att))
    partial = dot(att, weight, NT)
    part_mine, part_sent = partial[:tok], partial[tok:].astype(BF16)
    carried = None
    terms = {}
    for step in reversed(steps):
        last = step == 0
        res = backward(info, q, da, lse_t, [chunks[step]], (step,), att, carried, last)
        terms[step] = res[0]
        if carried is None:
            delta_t = res[1]
        if last:
            dq = res[1]
        else:
            carried = (delta_t, res[-1])

    passing = terms[prior]
    for step in range(prior - 1, 2, -1):
        passing = (terms[step].astype(F32) + down(passing, 1).astype(F32)).astype(BF16)
    from_x, from_y, by_x0, by_y1, got, part_sent = together(
        (
            across(far_x, 1),
            across(far_y, 2),
            across(to_x, 1),
            across(to_y, 2),
            down(passing, 1),
            part_sent,
        )
    )
    passing = (terms[2].astype(F32) + got.astype(F32)).astype(BF16)
    to_x = (dot(blocks[3], att) + from_y.astype(F32)).astype(BF16)
    to_y = (dot(blocks[4], att) + from_x.astype(F32)).astype(BF16)
    by_x1, by_y0, dq_theirs, layer_theirs, got = together(
        (across(to_x, 1), across(to_y, 2), swap(dq[tok:]), swap(part_sent), down(passing, 1))
    )
    passing = (terms[1].astype(F32) + got.astype(F32)).astype(BF16)
    coming = down(passing, 1)
    mine = jnp.concatenate(
        [
            dot(blocks[0], att) + by_x0.astype(F32) + by_y0.astype(F32),
            dot(blocks[1], att) + by_x1.astype(F32) + by_y1.astype(F32),
        ],
        0,
    )

    layer_out = (part_mine + layer_theirs.astype(F32)).astype(BF16)
    query_grad = in_order(dq[:tok], dq_theirs, 1)
    if near:
        final = lax.dynamic_slice_in_dim(mine, chip * part, part, 0)
        got = []
        for k in range(1, chips):
            target = lax.rem(chip + k, chips)
            sent = lax.dynamic_slice_in_dim(mine, target * part, part, 0).astype(BF16)
            got.append(round_chips(sent, k))
        coming, layer_out, query_grad, *got = together((coming, layer_out, query_grad, *got))
        for x in got:
            final = final + x.astype(F32)
    else:
        final = lax.psum_scatter(mine, "chip", scatter_dimension=0, tiled=True)
    total_tokens = rows_dp * chips * rows
    final = final * (1.0 / math.sqrt(total_tokens))
    first_rows, last_rows = final[:piece], final[piece:]
    weight_grad = in_order(
        jnp.where(low, first_rows, last_rows), swap(jnp.where(low, last_rows, first_rows)), 1
    )
    kv_grad = (terms[0] + coming.astype(F32)).astype(BF16)
    theirs = swap(kv_grad[tok:])
    key_grad = in_order(kv_grad[:tok, :HD], theirs[:, :HD], 1)
    value_grad = in_order(kv_grad[:tok, HD:], theirs[:, HD:], 1)
    return (
        layer_out[None],
        query_grad[None],
        key_grad[None],
        value_grad[None],
        weight_grad,
    )


def solution(mesh):
    devices = mesh.devices
    pairs = Mesh(
        devices.reshape(devices.shape[0], devices.shape[1] // 2, 2), ("dp", "chip", "core")
    )
    tokens = P("dp", ("chip", "core"), None)
    features = P(("dp", "chip", "core"), None)
    return jax.shard_map(
        on_device,
        mesh=pairs,
        in_specs=(tokens, tokens, tokens, features, tokens),
        out_specs=(tokens, tokens, tokens, tokens, features),
        check_vma=False,
    )
```

```python
import functools
import math

import jax
import jax.numpy as jnp
from jax import lax
from jax.experimental import pallas as pl
from jax.experimental.pallas import tpu as pltpu
from jax.sharding import Mesh
from jax.sharding import PartitionSpec as P

QH = 4
KH = 2
HD = 256
WINDOW = 2048
GROUPS = QH // KH
LANES = 128
NEG = -1e30
F32 = jnp.float32
BF16 = jnp.bfloat16
NT = (((1,), (1,)), ((), ()))
TN = (((0,), (0,)), ((), ()))
FILLER = pl.CostEstimate(flops=1, bytes_accessed=1, transcendentals=0)


def dot(a, b, dims=(((1,), (0,)), ((), ()))):
    return lax.dot_general(a, b, dims, preferred_element_type=F32)


def admitted(step, rows, core, query_axis):
    if step > 0 and (step + 1) * rows <= WINDOW:
        return None
    shape = (rows, rows)
    half = rows // 2
    query = (lax.broadcasted_iota(jnp.int32, shape, query_axis) + core * half) % rows
    key = (lax.broadcasted_iota(jnp.int32, shape, 1 - query_axis) + core * half) % rows
    gap = key - query - step * rows
    return (gap <= 0) & (gap > -WINDOW)


def forward_kernel(step, rows, first, last, info, q, kv, *refs):
    if not first:
        m_in, l_in, acc_in = refs[:3]
        refs = refs[3:]
    if last:
        out, lse_t, m_s, l_s, acc_s = refs
    else:
        m_s, l_s, acc_s = refs
    chip, core = info[0], info[1]
    mask = admitted(step, rows, core, 1)

    def block():
        keys = kv[:, :HD]
        vals_t = jnp.transpose(kv[:, HD:])
        for h in range(GROUPS):
            cols = slice(h * HD, (h + 1) * HD)
            stat = slice(h * 8, h * 8 + 1)
            whole = slice(h * 8, (h + 1) * 8)
            s = dot(keys, q[:, cols], NT)
            if mask is not None:
                s = jnp.where(mask, s, NEG)
            top = jnp.max(s, axis=0, keepdims=True)
            if first:
                p = jnp.exp(s - top)
                total = jnp.sum(p, axis=0, keepdims=True)
                acc_s[cols, :] = dot(vals_t, p.astype(BF16))
            else:
                before = m_in[stat, :]
                top = jnp.maximum(top, before)
                p = jnp.exp(s - top)
                keep = jnp.exp(before - top)
                total = keep * l_in[stat, :] + jnp.sum(p, axis=0, keepdims=True)
                acc_s[cols, :] = keep * acc_in[cols, :] + dot(vals_t, p.astype(BF16))
            m_s[whole, :] = jnp.broadcast_to(top, (8, rows))
            l_s[whole, :] = jnp.broadcast_to(total, (8, rows))

    if first:
        block()
    else:

        def keep_all():
            m_s[...] = m_in[...]
            l_s[...] = l_in[...]
            acc_s[...] = acc_in[...]

        pl.when(chip >= step)(block)
        pl.when(chip < step)(keep_all)
    if last:
        for h in range(GROUPS):
            cols = slice(h * HD, (h + 1) * HD)
            total = l_s[h * 8 : h * 8 + 1, :]
            out[:, cols] = jnp.transpose(acc_s[cols, :] / total).astype(BF16)
        lse_t[...] = m_s[...] + jnp.log(l_s[...])


def forward(info, q, kv, step, state, last):
    rows = q.shape[0]
    first = state is None
    stat = jax.ShapeDtypeStruct((GROUPS * 8, rows), F32)
    acc = jax.ShapeDtypeStruct((GROUPS * HD, rows), F32)
    vmem = pl.BlockSpec(memory_space=pltpu.VMEM)
    smem = pl.BlockSpec(memory_space=pltpu.SMEM)
    scratch = []
    if last:
        outs = (jax.ShapeDtypeStruct((rows, GROUPS * HD), BF16), stat)
        scratch = [pltpu.VMEM(s.shape, F32) for s in (stat, stat, acc)]
    else:
        outs = (stat, stat, acc)
    args = [info, q, kv] + ([] if first else list(state))
    return pl.pallas_call(
        functools.partial(forward_kernel, step, rows, first, last),
        out_shape=outs,
        in_specs=[smem] + [vmem] * (len(args) - 1),
        out_specs=tuple(vmem for _ in outs),
        scratch_shapes=scratch,
        cost_estimate=FILLER,
        compiler_params=pltpu.CompilerParams(vmem_limit_bytes=16 * 1024 * 1024),
        name="attend_forward",
    )(*args)


def backward_kernel(steps, rows, first, last, info, q, da, lse_t, *refs):
    chunks = refs[: len(steps)]
    refs = refs[len(steps) :]
    if first:
        att = refs[0]
        refs = refs[1:]
    else:
        delta_t, dq_in = refs[:2]
        refs = refs[2:]
    grads = refs[: len(steps)]
    refs = refs[len(steps) :]
    if last:
        dq_out = refs[0]
        refs = refs[1:]
    if first:
        delta_t = refs[0]
        refs = refs[1:]
    dq_s = refs[0]
    chip, core = info[0], info[1]
    if first:
        for h in range(GROUPS):
            cols = slice(h * HD, (h + 1) * HD)
            prod = da[:, cols].astype(F32) * att[:, cols].astype(F32)
            delta = jnp.sum(prod, axis=1, keepdims=True)
            wide = jnp.broadcast_to(delta, (rows, LANES))
            delta_t[h * 8 : (h + 1) * 8, :] = jnp.transpose(wide)[:8, :]
        dq_s[...] = jnp.zeros_like(dq_s)
    else:
        dq_s[...] = dq_in[...]
    for at, step in enumerate(steps):
        mask = admitted(step, rows, core, 1)

        def block(at=at, mask=mask):
            keys = chunks[at][:, :HD]
            keys_t = jnp.transpose(keys)
            vals = chunks[at][:, HD:]
            for h in range(GROUPS):
                cols = slice(h * HD, (h + 1) * HD)
                qh = q[:, cols]
                dah = da[:, cols]
                s = dot(keys, qh, NT)
                p = jnp.exp(s - lse_t[h * 8 : h * 8 + 1, :])
                if mask is not None:
                    p = jnp.where(mask, p, 0.0)
                dp = dot(vals, dah, NT)
                ds = (p * (dp - delta_t[h * 8 : h * 8 + 1, :])).astype(BF16)
                dk = dot(ds, qh)
                dv = dot(p.astype(BF16), dah)
                dq_s[cols, :] += dot(keys_t, ds)
                if h == 0:
                    dk_sum, dv_sum = dk, dv
                else:
                    dk_sum, dv_sum = dk_sum + dk, dv_sum + dv
            grads[at][:, :HD] = dk_sum.astype(grads[at].dtype)
            grads[at][:, HD:] = dv_sum.astype(grads[at].dtype)

        if step == 0:
            block()
        else:

            def blank(at=at):
                grads[at][...] = jnp.zeros_like(grads[at])

            pl.when(chip >= step)(block)
            pl.when(chip < step)(blank)
    if last:
        for h in range(GROUPS):
            cols = slice(h * HD, (h + 1) * HD)
            dq_out[:, cols] = jnp.transpose(dq_s[cols, :] * HD ** (-0.5)).astype(BF16)


def backward(info, q, da, lse_t, chunks, steps, att, carried, last):
    rows = q.shape[0]
    first = carried is None
    vmem = pl.BlockSpec(memory_space=pltpu.VMEM)
    smem = pl.BlockSpec(memory_space=pltpu.SMEM)
    wide = (rows, GROUPS * HD)
    tall = (GROUPS * HD, rows)
    outs = [jax.ShapeDtypeStruct((rows, 2 * HD), F32 if s == 0 else BF16) for s in steps]
    if last:
        outs.append(jax.ShapeDtypeStruct(wide, BF16))
    if first:
        outs.append(jax.ShapeDtypeStruct((GROUPS * 8, rows), F32))
    scratch = []
    if last:
        scratch = [pltpu.VMEM(tall, F32)]
    else:
        outs.append(jax.ShapeDtypeStruct(tall, F32))
    args = [info, q, da, lse_t, *chunks] + ([att] if first else list(carried))
    return pl.pallas_call(
        functools.partial(backward_kernel, steps, rows, first, last),
        out_shape=tuple(outs),
        in_specs=[smem] + [vmem] * (len(args) - 1),
        out_specs=tuple(vmem for _ in outs),
        scratch_shapes=scratch,
        cost_estimate=FILLER,
        compiler_params=pltpu.CompilerParams(vmem_limit_bytes=16 * 1024 * 1024),
        name="attend_backward",
    )(*args)


def product_kernel(x, w, *outs):
    result = dot(x[...], w[...], NT if len(outs) == 2 else (((1,), (0,)), ((), ())))
    if len(outs) == 2:
        half = result.shape[0] // 2
        outs[0][...] = result[:half]
        outs[1][...] = result[half:].astype(BF16)
    else:
        outs[0][...] = result


def layer_product(att, weight):
    rows, depth = att.shape
    features = weight.shape[0]
    wide = 256
    block = pl.BlockSpec((rows // 2, wide), lambda i: (0, i))
    return pl.pallas_call(
        product_kernel,
        grid=(features // wide,),
        out_shape=(
            jax.ShapeDtypeStruct((rows // 2, features), F32),
            jax.ShapeDtypeStruct((rows // 2, features), BF16),
        ),
        in_specs=[
            pl.BlockSpec((rows, depth), lambda i: (0, 0)),
            pl.BlockSpec((wide, depth), lambda i: (i, 0)),
        ],
        out_specs=(block, block),
        cost_estimate=FILLER,
        compiler_params=pltpu.CompilerParams(vmem_limit_bytes=16 * 1024 * 1024),
        name="layer_product",
    )(att, weight)


def strip_product(strips, att):
    rows, depth = strips.shape
    tall = rows // 4
    return pl.pallas_call(
        product_kernel,
        grid=(4,),
        out_shape=jax.ShapeDtypeStruct((rows, att.shape[1]), F32),
        in_specs=[
            pl.BlockSpec((tall, depth), lambda i: (i, 0)),
            pl.BlockSpec(att.shape, lambda i: (0, 0)),
        ],
        out_specs=pl.BlockSpec((tall, att.shape[1]), lambda i: (i, 0)),
        cost_estimate=FILLER,
        compiler_params=pltpu.CompilerParams(vmem_limit_bytes=16 * 1024 * 1024),
        name="strip_product",
    )(strips, att)


def on_device(queries, key_rows, values, out_weight, out_grad):
    chip = lax.axis_index("chip")
    core = lax.axis_index("core")
    row = lax.axis_index("dp")
    chips = lax.axis_size("chip")
    rows_dp = lax.axis_size("dp")
    tok = queries.shape[1]
    rows = 2 * tok
    prior = min(-(-WINDOW // rows), chips - 1)
    steps = tuple(range(prior + 1))
    low = core == 0
    info = jnp.stack([chip, core]).astype(jnp.int32)
    together = lax.optimization_barrier

    def own(x):
        half = x.shape[-1] // 2
        return jnp.where(low, x[..., :half], x[..., half:])

    def other(x):
        half = x.shape[-1] // 2
        return jnp.where(low, x[..., half:], x[..., :half])

    def swap(x):
        return lax.ppermute(x, "core", [(0, 1), (1, 0)])

    def up(x, k):
        return lax.ppermute(x, "chip", [(i, i + k) for i in range(chips - k)])

    def down(x, k):
        return lax.ppermute(x, "chip", [(i + k, i) for i in range(chips - k)])

    def round_chips(x, k):
        return lax.ppermute(x, "chip", [(i, (i + k) % chips) for i in range(chips)])

    def across(x, k):
        return lax.ppermute(x, "dp", [(i, i ^ k) for i in range(rows_dp)])

    def in_order(mine, theirs, axis):
        return jnp.where(
            low,
            jnp.concatenate([mine, theirs], axis),
            jnp.concatenate([theirs, mine], axis),
        )

    k0, v0, q0, g0 = key_rows[0], values[0], queries[0], out_grad[0]
    near = chips <= 4
    moved = [round_chips(out_weight, k) for k in range(1, chips)] if near else []
    kv_theirs = swap(jnp.concatenate([other(k0), other(v0)], 1))
    kv = jnp.concatenate([own(k0), own(v0)], 1)
    kv = jnp.concatenate([kv, kv_theirs], 0)
    hop = up(kv, 1)
    q = jnp.concatenate([own(q0), swap(other(q0))], 0) * jnp.asarray(HD ** (-0.5), BF16)
    state = forward(info, q, kv, 0, None, False)
    hop, q, state, grad_theirs, *moved = together((hop, q, state, swap(g0), *moved))
    chunks = [kv, hop]

    piece = out_weight.shape[0]
    part = 2 * piece
    if near:
        column = jnp.zeros((chips, *out_weight.shape), BF16)
        column = lax.dynamic_update_index_in_dim(column, out_weight, chip, 0)
        for k, got in enumerate(moved, 1):
            source = lax.rem(chip - k + chips, chips)
            column = lax.dynamic_update_index_in_dim(column, got, source, 0)
    else:
        column = lax.all_gather(out_weight, "chip", axis=0)
    ours = in_order(own(column)[:, None], swap(other(column))[:, None], 1)
    ours = ours.reshape(chips * part, ours.shape[-1])
    share = ours.shape[0]
    half = share // 2
    ours, *state = together((ours, *state))

    lower, upper = ours[:half], ours[half:]
    hop = up(hop, 1)
    state = forward(info, q, chunks[1], 1, state, False)
    *by_plane, hop, state = together(
        (across(lower, 1), across(upper, 1), across(lower, 2), across(upper, 2), hop, state)
    )
    chunks.append(hop)
    diagonal = [across(by_plane[2], 1), across(by_plane[1], 2)]
    grad = jnp.concatenate([g0, grad_theirs], 0)
    turned = grad.T

    def strip(k, at, size):
        return lax.dynamic_slice_in_dim(turned, (row ^ k) * share + at, size, 0)

    strips = [
        jnp.concatenate([strip(3, 0, half), strip(1, 0, half)], 0),
        jnp.concatenate([strip(3, half, half), strip(2, half, half)], 0),
        jnp.concatenate([strip(1, half, half), strip(2, 0, half), strip(0, 0, share)], 0),
    ]
    last_hop = up(hop, 1)
    for step in steps[2:prior]:
        state = forward(info, q, hop, step, state, False)
        hop = last_hop
        if step + 1 < prior:
            chunks.append(hop)
            last_hop = up(hop, 1)
    weight = jnp.zeros((rows_dp * share, ours.shape[1]), BF16)
    for got, k, at in (
        (ours, 0, 0),
        (by_plane[0], 1, 0),
        (by_plane[1], 1, half),
        (by_plane[2], 2, 0),
        (by_plane[3], 2, half),
        (diagonal[0], 3, 0),
        (diagonal[1], 3, half),
    ):
        weight = lax.dynamic_update_slice_in_dim(weight, got, (row ^ k) * share + at, 0)
    da = dot(grad, weight).astype(BF16)
    da, last_hop, state, *strips = together((da, last_hop, state, *strips))
    chunks.append(last_hop)
    att, lse_t = forward(info, q, last_hop, prior, state, True)

    to_x, to_y = [dot(x, att).astype(BF16) for x in strips[:2]]
    to_x, to_y, da, att = together((to_x, to_y, da, att))
    part_mine, part_sent = layer_product(att, weight)
    carried = None
    terms = {}
    for step in reversed(steps):
        last = step == 0
        res = backward(info, q, da, lse_t, [chunks[step]], (step,), att, carried, last)
        terms[step] = res[0]
        if carried is None:
            delta_t = res[1]
        if last:
            dq = res[1]
        else:
            carried = (delta_t, res[-1])

    passing = terms[prior]
    for step in range(prior - 1, 2, -1):
        passing = (terms[step].astype(F32) + down(passing, 1).astype(F32)).astype(BF16)
    rest = strip_product(strips[2], att)
    from_x, from_y, got, part_sent, rest, terms, dq = together(
        (across(to_x, 1), across(to_y, 2), down(passing, 1), part_sent, rest, terms, dq)
    )
    later_x, later_y, here = rest[:half], rest[half:share], rest[share:]
    passing = (terms[2].astype(F32) + got.astype(F32)).astype(BF16)
    to_x = (later_x + from_y[:half].astype(F32)).astype(BF16)
    to_y = (later_y + from_x[:half].astype(F32)).astype(BF16)
    by_x1, by_y0, dq_theirs, layer_theirs, got = together(
        (across(to_x, 1), across(to_y, 2), swap(dq[tok:]), swap(part_sent), down(passing, 1))
    )
    passing = (terms[1].astype(F32) + got.astype(F32)).astype(BF16)
    coming = down(passing, 1)
    mine = here + jnp.concatenate(
        [
            from_x[half:].astype(F32) + by_y0.astype(F32),
            by_x1.astype(F32) + from_y[half:].astype(F32),
        ],
        0,
    )

    layer_out = (part_mine + layer_theirs.astype(F32)).astype(BF16)
    query_grad = in_order(dq[:tok], dq_theirs, 1)
    if near:
        final = lax.dynamic_slice_in_dim(mine, chip * part, part, 0)
        got = []
        for k in range(1, chips):
            target = lax.rem(chip + k, chips)
            sent = lax.dynamic_slice_in_dim(mine, target * part, part, 0).astype(BF16)
            got.append(round_chips(sent, k))
        coming, layer_out, query_grad, *got = together((coming, layer_out, query_grad, *got))
        for x in got:
            final = final + x.astype(F32)
    else:
        final = lax.psum_scatter(mine, "chip", scatter_dimension=0, tiled=True)
    total_tokens = rows_dp * chips * rows
    final = final * (1.0 / math.sqrt(total_tokens))
    first_rows, last_rows = final[:piece], final[piece:]
    weight_grad = in_order(
        jnp.where(low, first_rows, last_rows), swap(jnp.where(low, last_rows, first_rows)), 1
    )
    kv_grad = (terms[0] + coming.astype(F32)).astype(BF16)
    theirs = swap(kv_grad[tok:])
    key_grad = in_order(kv_grad[:tok, :HD], theirs[:, :HD], 1)
    value_grad = in_order(kv_grad[:tok, HD:], theirs[:, HD:], 1)
    return (
        layer_out[None],
        query_grad[None],
        key_grad[None],
        value_grad[None],
        weight_grad,
    )


def solution(mesh):
    devices = mesh.devices
    pairs = Mesh(
        devices.reshape(devices.shape[0], devices.shape[1] // 2, 2), ("dp", "chip", "core")
    )
    tokens = P("dp", ("chip", "core"), None)
    features = P(("dp", "chip", "core"), None)
    return jax.shard_map(
        on_device,
        mesh=pairs,
        in_specs=(tokens, tokens, tokens, features, tokens),
        out_specs=(tokens, tokens, tokens, tokens, features),
        check_vma=False,
    )
```

```python
import functools
import math

import jax
import jax.numpy as jnp
from jax import lax
from jax.experimental import pallas as pl
from jax.experimental.pallas import tpu as pltpu
from jax.sharding import Mesh
from jax.sharding import PartitionSpec as P

QH = 4
KH = 2
HD = 256
WINDOW = 2048
GROUPS = QH // KH
LANES = 128
NEG = -1e30
F32 = jnp.float32
BF16 = jnp.bfloat16
NT = (((1,), (1,)), ((), ()))
TN = (((0,), (0,)), ((), ()))
FILLER = pl.CostEstimate(flops=1, bytes_accessed=1, transcendentals=0)


def dot(a, b, dims=(((1,), (0,)), ((), ()))):
    return lax.dot_general(a, b, dims, preferred_element_type=F32)


def admitted(step, rows, core, query_axis):
    if step > 0 and (step + 1) * rows <= WINDOW:
        return None
    shape = (rows, rows)
    half = rows // 2
    query = (lax.broadcasted_iota(jnp.int32, shape, query_axis) + core * half) % rows
    key = (lax.broadcasted_iota(jnp.int32, shape, 1 - query_axis) + core * half) % rows
    gap = key - query - step * rows
    return (gap <= 0) & (gap > -WINDOW)


def forward_kernel(step, rows, first, last, info, q, kv, *refs):
    if not first:
        m_in, l_in, acc_in = refs[:3]
        refs = refs[3:]
    if last:
        out, lse_t, m_s, l_s, acc_s = refs
    else:
        m_s, l_s, acc_s = refs
    chip, core = info[0], info[1]
    mask = admitted(step, rows, core, 1)

    def block():
        keys = kv[:, :HD]
        vals_t = jnp.transpose(kv[:, HD:])
        for h in range(GROUPS):
            cols = slice(h * HD, (h + 1) * HD)
            stat = slice(h * 8, h * 8 + 1)
            whole = slice(h * 8, (h + 1) * 8)
            s = dot(keys, q[:, cols], NT)
            if mask is not None:
                s = jnp.where(mask, s, NEG)
            top = jnp.max(s, axis=0, keepdims=True)
            if first:
                p = jnp.exp(s - top)
                total = jnp.sum(p, axis=0, keepdims=True)
                acc_s[cols, :] = dot(vals_t, p.astype(BF16))
            else:
                before = m_in[stat, :]
                top = jnp.maximum(top, before)
                p = jnp.exp(s - top)
                keep = jnp.exp(before - top)
                total = keep * l_in[stat, :] + jnp.sum(p, axis=0, keepdims=True)
                acc_s[cols, :] = keep * acc_in[cols, :] + dot(vals_t, p.astype(BF16))
            m_s[whole, :] = jnp.broadcast_to(top, (8, rows))
            l_s[whole, :] = jnp.broadcast_to(total, (8, rows))

    if first:
        block()
    else:

        def keep_all():
            m_s[...] = m_in[...]
            l_s[...] = l_in[...]
            acc_s[...] = acc_in[...]

        pl.when(chip >= step)(block)
        pl.when(chip < step)(keep_all)
    if last:
        for h in range(GROUPS):
            cols = slice(h * HD, (h + 1) * HD)
            total = l_s[h * 8 : h * 8 + 1, :]
            out[:, cols] = jnp.transpose(acc_s[cols, :] / total).astype(BF16)
        lse_t[...] = m_s[...] + jnp.log(l_s[...])


def forward(info, q, kv, step, state, last):
    rows = q.shape[0]
    first = state is None
    stat = jax.ShapeDtypeStruct((GROUPS * 8, rows), F32)
    acc = jax.ShapeDtypeStruct((GROUPS * HD, rows), F32)
    vmem = pl.BlockSpec(memory_space=pltpu.VMEM)
    smem = pl.BlockSpec(memory_space=pltpu.SMEM)
    scratch = []
    if last:
        outs = (jax.ShapeDtypeStruct((rows, GROUPS * HD), BF16), stat)
        scratch = [pltpu.VMEM(s.shape, F32) for s in (stat, stat, acc)]
    else:
        outs = (stat, stat, acc)
    args = [info, q, kv] + ([] if first else list(state))
    return pl.pallas_call(
        functools.partial(forward_kernel, step, rows, first, last),
        out_shape=outs,
        in_specs=[smem] + [vmem] * (len(args) - 1),
        out_specs=tuple(vmem for _ in outs),
        scratch_shapes=scratch,
        cost_estimate=FILLER,
        compiler_params=pltpu.CompilerParams(vmem_limit_bytes=16 * 1024 * 1024),
        name="attend_forward",
    )(*args)


def backward_kernel(steps, rows, first, last, info, q, da, lse_t, *refs):
    chunks = refs[: len(steps)]
    refs = refs[len(steps) :]
    if first:
        att = refs[0]
        refs = refs[1:]
    else:
        delta_t, dq_in = refs[:2]
        refs = refs[2:]
    grads = refs[: len(steps)]
    refs = refs[len(steps) :]
    if last:
        dq_out = refs[0]
        refs = refs[1:]
    if first:
        delta_t = refs[0]
        refs = refs[1:]
    dq_s = refs[0]
    chip, core = info[0], info[1]
    if first:
        for h in range(GROUPS):
            cols = slice(h * HD, (h + 1) * HD)
            prod = da[:, cols].astype(F32) * att[:, cols].astype(F32)
            delta = jnp.sum(prod, axis=1, keepdims=True)
            wide = jnp.broadcast_to(delta, (rows, LANES))
            delta_t[h * 8 : (h + 1) * 8, :] = jnp.transpose(wide)[:8, :]
        dq_s[...] = jnp.zeros_like(dq_s)
    else:
        dq_s[...] = dq_in[...]
    for at, step in enumerate(steps):
        mask = admitted(step, rows, core, 1)

        def block(at=at, mask=mask):
            keys = chunks[at][:, :HD]
            keys_t = jnp.transpose(keys)
            vals = chunks[at][:, HD:]
            for h in range(GROUPS):
                cols = slice(h * HD, (h + 1) * HD)
                qh = q[:, cols]
                dah = da[:, cols]
                s = dot(keys, qh, NT)
                p = jnp.exp(s - lse_t[h * 8 : h * 8 + 1, :])
                if mask is not None:
                    p = jnp.where(mask, p, 0.0)
                dp = dot(vals, dah, NT)
                ds = (p * (dp - delta_t[h * 8 : h * 8 + 1, :])).astype(BF16)
                dk = dot(ds, qh)
                dv = dot(p.astype(BF16), dah)
                dq_s[cols, :] += dot(keys_t, ds)
                if h == 0:
                    dk_sum, dv_sum = dk, dv
                else:
                    dk_sum, dv_sum = dk_sum + dk, dv_sum + dv
            grads[at][:, :HD] = dk_sum.astype(grads[at].dtype)
            grads[at][:, HD:] = dv_sum.astype(grads[at].dtype)

        if step == 0:
            block()
        else:

            def blank(at=at):
                grads[at][...] = jnp.zeros_like(grads[at])

            pl.when(chip >= step)(block)
            pl.when(chip < step)(blank)
    if last:
        for h in range(GROUPS):
            cols = slice(h * HD, (h + 1) * HD)
            dq_out[:, cols] = jnp.transpose(dq_s[cols, :] * HD ** (-0.5)).astype(BF16)


def backward(info, q, da, lse_t, chunks, steps, att, carried, last):
    rows = q.shape[0]
    first = carried is None
    vmem = pl.BlockSpec(memory_space=pltpu.VMEM)
    smem = pl.BlockSpec(memory_space=pltpu.SMEM)
    wide = (rows, GROUPS * HD)
    tall = (GROUPS * HD, rows)
    outs = [jax.ShapeDtypeStruct((rows, 2 * HD), F32 if s == 0 else BF16) for s in steps]
    if last:
        outs.append(jax.ShapeDtypeStruct(wide, BF16))
    if first:
        outs.append(jax.ShapeDtypeStruct((GROUPS * 8, rows), F32))
    scratch = []
    if last:
        scratch = [pltpu.VMEM(tall, F32)]
    else:
        outs.append(jax.ShapeDtypeStruct(tall, F32))
    args = [info, q, da, lse_t, *chunks] + ([att] if first else list(carried))
    return pl.pallas_call(
        functools.partial(backward_kernel, steps, rows, first, last),
        out_shape=tuple(outs),
        in_specs=[smem] + [vmem] * (len(args) - 1),
        out_specs=tuple(vmem for _ in outs),
        scratch_shapes=scratch,
        cost_estimate=FILLER,
        compiler_params=pltpu.CompilerParams(vmem_limit_bytes=16 * 1024 * 1024),
        name="attend_backward",
    )(*args)


def column_kernel(info, *refs):
    *pieces, own, other = refs
    chip, core = info[0], info[1]
    chips = len(pieces)
    half = own.shape[2]
    for k, ref in enumerate(pieces):
        at = lax.rem(chip - k + chips, chips)
        left, right = ref[:, :half], ref[:, half:]
        own[at] = jnp.where(core == 0, left, right)
        other[at] = jnp.where(core == 0, right, left)


def column_halves(info, pieces):
    rows, width = pieces[0].shape
    shape = jax.ShapeDtypeStruct((len(pieces), rows, width // 2), BF16)
    vmem = pl.BlockSpec(memory_space=pltpu.VMEM)
    return pl.pallas_call(
        column_kernel,
        out_shape=(shape, shape),
        in_specs=[pl.BlockSpec(memory_space=pltpu.SMEM)] + [vmem] * len(pieces),
        out_specs=(vmem, vmem),
        cost_estimate=pl.CostEstimate(flops=4 * 10**9, bytes_accessed=1, transcendentals=0),
        compiler_params=pltpu.CompilerParams(vmem_limit_bytes=8 * 1024 * 1024),
        name="column_halves",
    )(info, *pieces)


def into_heads_kernel(places, info, grad, *refs):
    *pieces, weight, out = refs
    half = pieces[0].shape[0]
    for (k, at), ref in zip(places, pieces):
        start = ((info[2] ^ k) * 2 + at) * half
        weight[pl.ds(pl.multiple_of(start, half), half), :] = ref[...]
    depth = weight.shape[0]
    wide = 256
    total = dot(grad[:, :wide], weight[:wide, :])
    for i in range(wide, depth, wide):
        total = total + dot(grad[:, i : i + wide], weight[i : i + wide, :])
    out[...] = total.astype(BF16)


def gradient_into_heads(info, grad, pieces):
    arrays = [x for x, _, _ in pieces]
    half, width = arrays[0].shape
    vmem = pl.BlockSpec(memory_space=pltpu.VMEM)
    return pl.pallas_call(
        functools.partial(into_heads_kernel, [(k, at) for _, k, at in pieces]),
        out_shape=(
            jax.ShapeDtypeStruct((half * len(pieces), width), BF16),
            jax.ShapeDtypeStruct((grad.shape[0], width), BF16),
        ),
        in_specs=[pl.BlockSpec(memory_space=pltpu.SMEM)] + [vmem] * (1 + len(pieces)),
        out_specs=(vmem, vmem),
        cost_estimate=FILLER,
        compiler_params=pltpu.CompilerParams(vmem_limit_bytes=20 * 1024 * 1024),
        name="gradient_into_heads",
    )(info, grad, *arrays)


def product_kernel(x, w, *outs):
    result = dot(x[...], w[...], NT if len(outs) == 2 else (((1,), (0,)), ((), ())))
    if len(outs) == 2:
        half = result.shape[0] // 2
        outs[0][...] = result[:half]
        outs[1][...] = result[half:].astype(BF16)
    else:
        outs[0][...] = result


def layer_product(att, weight):
    rows, depth = att.shape
    features = weight.shape[0]
    wide = 256
    block = pl.BlockSpec((rows // 2, wide), lambda i: (0, i))
    return pl.pallas_call(
        product_kernel,
        grid=(features // wide,),
        out_shape=(
            jax.ShapeDtypeStruct((rows // 2, features), F32),
            jax.ShapeDtypeStruct((rows // 2, features), BF16),
        ),
        in_specs=[
            pl.BlockSpec((rows, depth), lambda i: (0, 0)),
            pl.BlockSpec((wide, depth), lambda i: (i, 0)),
        ],
        out_specs=(block, block),
        cost_estimate=FILLER,
        compiler_params=pltpu.CompilerParams(vmem_limit_bytes=16 * 1024 * 1024),
        name="layer_product",
    )(att, weight)


def strip_product(strips, att):
    rows, depth = strips.shape
    tall = rows // 4
    return pl.pallas_call(
        product_kernel,
        grid=(4,),
        out_shape=jax.ShapeDtypeStruct((rows, att.shape[1]), F32),
        in_specs=[
            pl.BlockSpec((tall, depth), lambda i: (i, 0)),
            pl.BlockSpec(att.shape, lambda i: (0, 0)),
        ],
        out_specs=pl.BlockSpec((tall, att.shape[1]), lambda i: (i, 0)),
        cost_estimate=FILLER,
        compiler_params=pltpu.CompilerParams(vmem_limit_bytes=16 * 1024 * 1024),
        name="strip_product",
    )(strips, att)


def on_device(queries, key_rows, values, out_weight, out_grad):
    chip = lax.axis_index("chip")
    core = lax.axis_index("core")
    row = lax.axis_index("dp")
    chips = lax.axis_size("chip")
    rows_dp = lax.axis_size("dp")
    tok = queries.shape[1]
    rows = 2 * tok
    prior = min(-(-WINDOW // rows), chips - 1)
    steps = tuple(range(prior + 1))
    low = core == 0
    info = jnp.stack([chip, core, row]).astype(jnp.int32)
    together = lax.optimization_barrier

    def own(x):
        half = x.shape[-1] // 2
        return jnp.where(low, x[..., :half], x[..., half:])

    def other(x):
        half = x.shape[-1] // 2
        return jnp.where(low, x[..., half:], x[..., :half])

    def swap(x):
        return lax.ppermute(x, "core", [(0, 1), (1, 0)])

    def up(x, k):
        return lax.ppermute(x, "chip", [(i, i + k) for i in range(chips - k)])

    def down(x, k):
        return lax.ppermute(x, "chip", [(i + k, i) for i in range(chips - k)])

    def round_chips(x, k):
        return lax.ppermute(x, "chip", [(i, (i + k) % chips) for i in range(chips)])

    def across(x, k):
        return lax.ppermute(x, "dp", [(i, i ^ k) for i in range(rows_dp)])

    def in_order(mine, theirs, axis):
        return jnp.where(
            low,
            jnp.concatenate([mine, theirs], axis),
            jnp.concatenate([theirs, mine], axis),
        )

    k0, v0, q0, g0 = key_rows[0], values[0], queries[0], out_grad[0]
    near = chips <= 4
    moved = [round_chips(out_weight, k) for k in range(1, chips)] if near else []
    kv_theirs = swap(jnp.concatenate([other(k0), other(v0)], 1))
    kv = jnp.concatenate([own(k0), own(v0)], 1)
    kv = jnp.concatenate([kv, kv_theirs], 0)
    hop = up(kv, 1)
    q = jnp.concatenate([own(q0), swap(other(q0))], 0) * jnp.asarray(HD ** (-0.5), BF16)
    state = forward(info, q, kv, 0, None, False)
    piece = out_weight.shape[0]
    part = 2 * piece
    if near:
        column, column_theirs = column_halves(info, [out_weight, *moved])
    else:
        column = lax.all_gather(out_weight, "chip", axis=0)
        column, column_theirs = own(column), other(column)
    ours = in_order(column[:, None], swap(column_theirs)[:, None], 1)
    ours = ours.reshape(chips * part, ours.shape[-1])
    share = ours.shape[0]
    half = share // 2
    lower, upper = ours[:half], ours[half:]
    hop, q, state, lower, upper = together((hop, q, state, lower, upper))
    chunks = [kv, hop]

    hop = up(hop, 1)
    state = forward(info, q, chunks[1], 1, state, False)
    upper_x, lower_y, grad_theirs, hop, state, lower, upper = together(
        (across(upper, 1), across(lower, 2), swap(g0), hop, state, lower, upper)
    )
    chunks.append(hop)
    last_hop = up(hop, 1)
    lower_x, upper_y = across(lower, 1), across(upper, 2)
    diagonal = [across(lower_y, 1), across(upper_x, 2)]
    grad = jnp.concatenate([g0, grad_theirs], 0)
    turned = grad.T

    def strip(k, at, size):
        return lax.dynamic_slice_in_dim(turned, (row ^ k) * share + at, size, 0)

    strips = [
        jnp.concatenate([strip(3, 0, half), strip(1, 0, half)], 0),
        jnp.concatenate([strip(3, half, half), strip(2, half, half)], 0),
        jnp.concatenate([strip(1, half, half), strip(2, 0, half), strip(0, 0, share)], 0),
    ]
    for step in steps[2:prior]:
        state = forward(info, q, hop, step, state, False)
        hop = last_hop
        if step + 1 < prior:
            chunks.append(hop)
            last_hop = up(hop, 1)
    last_hop, state, *strips = together((last_hop, state, *strips))
    chunks.append(last_hop)
    att, lse_t = forward(info, q, last_hop, prior, state, True)

    to_x, to_y = [dot(x, att).astype(BF16) for x in strips[:2]]
    to_x, to_y, att, grad = together((to_x, to_y, att, grad))
    weight, da = gradient_into_heads(
        info,
        grad,
        [(lower, 0, 0), (upper, 0, 1), (lower_x, 1, 0), (upper_x, 1, 1), (lower_y, 2, 0)]
        + [(upper_y, 2, 1), (diagonal[0], 3, 0), (diagonal[1], 3, 1)],
    )
    carried = None
    terms = {}
    for step in reversed(steps):
        last = step == 0
        res = backward(info, q, da, lse_t, [chunks[step]], (step,), att, carried, last)
        terms[step] = res[0]
        if carried is None:
            delta_t = res[1]
        if last:
            dq = res[1]
        else:
            carried = (delta_t, res[-1])

    passing = terms[prior]
    for step in range(prior - 1, 2, -1):
        passing = (terms[step].astype(F32) + down(passing, 1).astype(F32)).astype(BF16)
    rest = strip_product(strips[2], att)
    from_x, from_y, got, rest, terms, dq, att = together(
        (across(to_x, 1), across(to_y, 2), down(passing, 1), rest, terms, dq, att)
    )
    part_mine, part_sent = layer_product(att, weight)
    later_x, later_y, here = rest[:half], rest[half:share], rest[share:]
    passing = (terms[2].astype(F32) + got.astype(F32)).astype(BF16)
    to_x = (later_x + from_y[:half].astype(F32)).astype(BF16)
    to_y = (later_y + from_x[:half].astype(F32)).astype(BF16)
    by_x1, by_y0, dq_theirs, part_sent, got = together(
        (across(to_x, 1), across(to_y, 2), swap(dq[tok:]), part_sent, down(passing, 1))
    )
    passing = (terms[1].astype(F32) + got.astype(F32)).astype(BF16)
    coming = down(passing, 1)
    mine = here + jnp.concatenate(
        [
            from_x[half:].astype(F32) + by_y0.astype(F32),
            by_x1.astype(F32) + from_y[half:].astype(F32),
        ],
        0,
    )

    layer_out = (part_mine + swap(part_sent).astype(F32)).astype(BF16)
    query_grad = in_order(dq[:tok], dq_theirs, 1)
    if near:
        final = lax.dynamic_slice_in_dim(mine, chip * part, part, 0)
        got = []
        for k in range(1, chips):
            target = lax.rem(chip + k, chips)
            sent = lax.dynamic_slice_in_dim(mine, target * part, part, 0).astype(BF16)
            got.append(round_chips(sent, k))
        coming, layer_out, query_grad, *got = together((coming, layer_out, query_grad, *got))
        for x in got:
            final = final + x.astype(F32)
    else:
        final = lax.psum_scatter(mine, "chip", scatter_dimension=0, tiled=True)
    total_tokens = rows_dp * chips * rows
    final = final * (1.0 / math.sqrt(total_tokens))
    first_rows, last_rows = final[:piece], final[piece:]
    weight_grad = in_order(
        jnp.where(low, first_rows, last_rows), swap(jnp.where(low, last_rows, first_rows)), 1
    )
    kv_grad = (terms[0] + coming.astype(F32)).astype(BF16)
    theirs = swap(kv_grad[tok:])
    key_grad = in_order(kv_grad[:tok, :HD], theirs[:, :HD], 1)
    value_grad = in_order(kv_grad[:tok, HD:], theirs[:, HD:], 1)
    return (
        layer_out[None],
        query_grad[None],
        key_grad[None],
        value_grad[None],
        weight_grad,
    )


def solution(mesh):
    devices = mesh.devices
    pairs = Mesh(
        devices.reshape(devices.shape[0], devices.shape[1] // 2, 2), ("dp", "chip", "core")
    )
    tokens = P("dp", ("chip", "core"), None)
    features = P(("dp", "chip", "core"), None)
    return jax.shard_map(
        on_device,
        mesh=pairs,
        in_specs=(tokens, tokens, tokens, features, tokens),
        out_specs=(tokens, tokens, tokens, tokens, features),
        check_vma=False,
    )
```

```python
import functools
import math

import jax
import jax.numpy as jnp
from jax import lax
from jax.experimental import pallas as pl
from jax.experimental.pallas import tpu as pltpu
from jax.sharding import Mesh
from jax.sharding import PartitionSpec as P

QH = 4
KH = 2
HD = 256
WINDOW = 2048
GROUPS = QH // KH
LANES = 128
NEG = -1e30
F32 = jnp.float32
BF16 = jnp.bfloat16
NT = (((1,), (1,)), ((), ()))
TN = (((0,), (0,)), ((), ()))
FILLER = pl.CostEstimate(flops=1, bytes_accessed=1, transcendentals=0)


def dot(a, b, dims=(((1,), (0,)), ((), ()))):
    return lax.dot_general(a, b, dims, preferred_element_type=F32)


def admitted(step, rows, core, query_axis):
    if step > 0 and (step + 1) * rows <= WINDOW:
        return None
    shape = (rows, rows)
    half = rows // 2
    query = (lax.broadcasted_iota(jnp.int32, shape, query_axis) + core * half) % rows
    key = (lax.broadcasted_iota(jnp.int32, shape, 1 - query_axis) + core * half) % rows
    gap = key - query - step * rows
    return (gap <= 0) & (gap > -WINDOW)


def forward_kernel(step, rows, first, last, info, q, kv, *refs):
    if not first:
        m_in, l_in, acc_in = refs[:3]
        refs = refs[3:]
    if last:
        strip_x, strip_y, out, lse_t, to_x, to_y, m_s, l_s, acc_s = refs
    else:
        m_s, l_s, acc_s = refs
    chip, core = info[0], info[1]
    mask = admitted(step, rows, core, 1)

    def block():
        keys = kv[:, :HD]
        vals_t = jnp.transpose(kv[:, HD:])
        for h in range(GROUPS):
            cols = slice(h * HD, (h + 1) * HD)
            stat = slice(h * 8, h * 8 + 1)
            whole = slice(h * 8, (h + 1) * 8)
            s = dot(keys, q[:, cols], NT)
            if mask is not None:
                s = jnp.where(mask, s, NEG)
            top = jnp.max(s, axis=0, keepdims=True)
            if first:
                p = jnp.exp(s - top)
                total = jnp.sum(p, axis=0, keepdims=True)
                acc_s[cols, :] = dot(vals_t, p.astype(BF16))
            else:
                before = m_in[stat, :]
                top = jnp.maximum(top, before)
                p = jnp.exp(s - top)
                keep = jnp.exp(before - top)
                total = keep * l_in[stat, :] + jnp.sum(p, axis=0, keepdims=True)
                acc_s[cols, :] = keep * acc_in[cols, :] + dot(vals_t, p.astype(BF16))
            m_s[whole, :] = jnp.broadcast_to(top, (8, rows))
            l_s[whole, :] = jnp.broadcast_to(total, (8, rows))

    if first:
        block()
    else:

        def keep_all():
            m_s[...] = m_in[...]
            l_s[...] = l_in[...]
            acc_s[...] = acc_in[...]

        pl.when(chip >= step)(block)
        pl.when(chip < step)(keep_all)
    if last:
        for h in range(GROUPS):
            cols = slice(h * HD, (h + 1) * HD)
            total = l_s[h * 8 : h * 8 + 1, :]
            out[:, cols] = jnp.transpose(acc_s[cols, :] / total).astype(BF16)
        lse_t[...] = m_s[...] + jnp.log(l_s[...])
        to_x[...] = dot(strip_x[...], out[...]).astype(BF16)
        to_y[...] = dot(strip_y[...], out[...]).astype(BF16)


def forward(info, q, kv, step, state, strips=()):
    rows = q.shape[0]
    first = state is None
    last = len(strips) > 0
    stat = jax.ShapeDtypeStruct((GROUPS * 8, rows), F32)
    acc = jax.ShapeDtypeStruct((GROUPS * HD, rows), F32)
    vmem = pl.BlockSpec(memory_space=pltpu.VMEM)
    smem = pl.BlockSpec(memory_space=pltpu.SMEM)
    scratch = []
    if last:
        outs = (jax.ShapeDtypeStruct((rows, GROUPS * HD), BF16), stat)
        outs += tuple(jax.ShapeDtypeStruct((x.shape[0], GROUPS * HD), BF16) for x in strips)
        scratch = [pltpu.VMEM(s.shape, F32) for s in (stat, stat, acc)]
    else:
        outs = (stat, stat, acc)
    args = [info, q, kv] + ([] if first else list(state)) + list(strips)
    return pl.pallas_call(
        functools.partial(forward_kernel, step, rows, first, last),
        out_shape=outs,
        in_specs=[smem] + [vmem] * (len(args) - 1),
        out_specs=tuple(vmem for _ in outs),
        scratch_shapes=scratch,
        cost_estimate=FILLER,
        compiler_params=pltpu.CompilerParams(vmem_limit_bytes=16 * 1024 * 1024),
        name="attend_forward",
    )(*args)


def backward_kernel(steps, rows, first, last, info, q, da, lse_t, *refs):
    chunks = refs[: len(steps)]
    refs = refs[len(steps) :]
    if first:
        att = refs[0]
        refs = refs[1:]
    else:
        delta_t, dq_in = refs[:2]
        refs = refs[2:]
    grads = refs[: len(steps)]
    refs = refs[len(steps) :]
    if last:
        dq_out = refs[0]
        refs = refs[1:]
    if first:
        delta_t = refs[0]
        refs = refs[1:]
    dq_s = refs[0]
    chip, core = info[0], info[1]
    if first:
        for h in range(GROUPS):
            cols = slice(h * HD, (h + 1) * HD)
            prod = da[:, cols].astype(F32) * att[:, cols].astype(F32)
            delta = jnp.sum(prod, axis=1, keepdims=True)
            wide = jnp.broadcast_to(delta, (rows, LANES))
            delta_t[h * 8 : (h + 1) * 8, :] = jnp.transpose(wide)[:8, :]
        dq_s[...] = jnp.zeros_like(dq_s)
    else:
        dq_s[...] = dq_in[...]
    for at, step in enumerate(steps):
        mask = admitted(step, rows, core, 1)

        def block(at=at, mask=mask):
            keys = chunks[at][:, :HD]
            keys_t = jnp.transpose(keys)
            vals = chunks[at][:, HD:]
            for h in range(GROUPS):
                cols = slice(h * HD, (h + 1) * HD)
                qh = q[:, cols]
                dah = da[:, cols]
                s = dot(keys, qh, NT)
                p = jnp.exp(s - lse_t[h * 8 : h * 8 + 1, :])
                if mask is not None:
                    p = jnp.where(mask, p, 0.0)
                dp = dot(vals, dah, NT)
                ds = (p * (dp - delta_t[h * 8 : h * 8 + 1, :])).astype(BF16)
                dk = dot(ds, qh)
                dv = dot(p.astype(BF16), dah)
                dq_s[cols, :] += dot(keys_t, ds)
                if h == 0:
                    dk_sum, dv_sum = dk, dv
                else:
                    dk_sum, dv_sum = dk_sum + dk, dv_sum + dv
            grads[at][:, :HD] = dk_sum.astype(grads[at].dtype)
            grads[at][:, HD:] = dv_sum.astype(grads[at].dtype)

        if step == 0:
            block()
        else:

            def blank(at=at):
                grads[at][...] = jnp.zeros_like(grads[at])

            pl.when(chip >= step)(block)
            pl.when(chip < step)(blank)
    if last:
        for h in range(GROUPS):
            cols = slice(h * HD, (h + 1) * HD)
            dq_out[:, cols] = jnp.transpose(dq_s[cols, :] * HD ** (-0.5)).astype(BF16)


def backward(info, q, da, lse_t, chunks, steps, att, carried, last):
    rows = q.shape[0]
    first = carried is None
    vmem = pl.BlockSpec(memory_space=pltpu.VMEM)
    smem = pl.BlockSpec(memory_space=pltpu.SMEM)
    wide = (rows, GROUPS * HD)
    tall = (GROUPS * HD, rows)
    outs = [jax.ShapeDtypeStruct((rows, 2 * HD), F32 if s == 0 else BF16) for s in steps]
    if last:
        outs.append(jax.ShapeDtypeStruct(wide, BF16))
    if first:
        outs.append(jax.ShapeDtypeStruct((GROUPS * 8, rows), F32))
    scratch = []
    if last:
        scratch = [pltpu.VMEM(tall, F32)]
    else:
        outs.append(jax.ShapeDtypeStruct(tall, F32))
    args = [info, q, da, lse_t, *chunks] + ([att] if first else list(carried))
    return pl.pallas_call(
        functools.partial(backward_kernel, steps, rows, first, last),
        out_shape=tuple(outs),
        in_specs=[smem] + [vmem] * (len(args) - 1),
        out_specs=tuple(vmem for _ in outs),
        scratch_shapes=scratch,
        cost_estimate=FILLER,
        compiler_params=pltpu.CompilerParams(vmem_limit_bytes=16 * 1024 * 1024),
        name="attend_backward",
    )(*args)


def column_kernel(info, *refs):
    *pieces, own, other = refs
    chip, core = info[0], info[1]
    chips = len(pieces)
    half = own.shape[2]
    for k, ref in enumerate(pieces):
        at = lax.rem(chip - k + chips, chips)
        left, right = ref[:, :half], ref[:, half:]
        own[at] = jnp.where(core == 0, left, right)
        other[at] = jnp.where(core == 0, right, left)


def column_halves(info, pieces):
    rows, width = pieces[0].shape
    shape = jax.ShapeDtypeStruct((len(pieces), rows, width // 2), BF16)
    vmem = pl.BlockSpec(memory_space=pltpu.VMEM)
    return pl.pallas_call(
        column_kernel,
        out_shape=(shape, shape),
        in_specs=[pl.BlockSpec(memory_space=pltpu.SMEM)] + [vmem] * len(pieces),
        out_specs=(vmem, vmem),
        cost_estimate=pl.CostEstimate(flops=4 * 10**9, bytes_accessed=1, transcendentals=0),
        compiler_params=pltpu.CompilerParams(vmem_limit_bytes=8 * 1024 * 1024),
        name="column_halves",
    )(info, *pieces)


def into_heads_kernel(places, info, mine, theirs, *refs):
    *pieces, weight, out = refs
    half = pieces[0].shape[0]
    for (k, at), ref in zip(places, pieces):
        start = ((info[2] ^ k) * 2 + at) * half
        weight[pl.ds(pl.multiple_of(start, half), half), :] = ref[...]
    depth = weight.shape[0]
    wide = 256
    tok = mine.shape[0]
    for at, grad in ((0, mine), (tok, theirs)):
        total = dot(grad[:, :wide], weight[:wide, :])
        for i in range(wide, depth, wide):
            total = total + dot(grad[:, i : i + wide], weight[i : i + wide, :])
        out[at : at + tok, :] = total.astype(BF16)


def gradient_into_heads(info, mine, theirs, pieces):
    arrays = [x for x, _, _ in pieces]
    half, width = arrays[0].shape
    vmem = pl.BlockSpec(memory_space=pltpu.VMEM)
    return pl.pallas_call(
        functools.partial(into_heads_kernel, [(k, at) for _, k, at in pieces]),
        out_shape=(
            jax.ShapeDtypeStruct((half * len(pieces), width), BF16),
            jax.ShapeDtypeStruct((2 * mine.shape[0], width), BF16),
        ),
        in_specs=[pl.BlockSpec(memory_space=pltpu.SMEM)] + [vmem] * (2 + len(pieces)),
        out_specs=(vmem, vmem),
        cost_estimate=FILLER,
        compiler_params=pltpu.CompilerParams(vmem_limit_bytes=20 * 1024 * 1024),
        name="gradient_into_heads",
    )(info, mine, theirs, *arrays)


def product_kernel(x, w, *outs):
    result = dot(x[...], w[...], NT if len(outs) == 2 else (((1,), (0,)), ((), ())))
    if len(outs) == 2:
        half = result.shape[0] // 2
        outs[0][...] = result[:half]
        outs[1][...] = result[half:].astype(BF16)
    else:
        outs[0][...] = result


def layer_product(att, weight):
    rows, depth = att.shape
    features = weight.shape[0]
    wide = 256
    block = pl.BlockSpec((rows // 2, wide), lambda i: (0, i))
    return pl.pallas_call(
        product_kernel,
        grid=(features // wide,),
        out_shape=(
            jax.ShapeDtypeStruct((rows // 2, features), F32),
            jax.ShapeDtypeStruct((rows // 2, features), BF16),
        ),
        in_specs=[
            pl.BlockSpec((rows, depth), lambda i: (0, 0)),
            pl.BlockSpec((wide, depth), lambda i: (i, 0)),
        ],
        out_specs=(block, block),
        cost_estimate=FILLER,
        compiler_params=pltpu.CompilerParams(vmem_limit_bytes=16 * 1024 * 1024),
        name="layer_product",
    )(att, weight)


def strip_product(strips, att):
    rows, depth = strips.shape
    tall = rows // 4
    return pl.pallas_call(
        product_kernel,
        grid=(4,),
        out_shape=jax.ShapeDtypeStruct((rows, att.shape[1]), F32),
        in_specs=[
            pl.BlockSpec((tall, depth), lambda i: (i, 0)),
            pl.BlockSpec(att.shape, lambda i: (0, 0)),
        ],
        out_specs=pl.BlockSpec((tall, att.shape[1]), lambda i: (i, 0)),
        cost_estimate=FILLER,
        compiler_params=pltpu.CompilerParams(vmem_limit_bytes=16 * 1024 * 1024),
        name="strip_product",
    )(strips, att)


def on_device(queries, key_rows, values, out_weight, out_grad):
    chip = lax.axis_index("chip")
    core = lax.axis_index("core")
    row = lax.axis_index("dp")
    chips = lax.axis_size("chip")
    rows_dp = lax.axis_size("dp")
    tok = queries.shape[1]
    rows = 2 * tok
    prior = min(-(-WINDOW // rows), chips - 1)
    steps = tuple(range(prior + 1))
    low = core == 0
    info = jnp.stack([chip, core, row]).astype(jnp.int32)
    together = lax.optimization_barrier

    def own(x):
        half = x.shape[-1] // 2
        return jnp.where(low, x[..., :half], x[..., half:])

    def other(x):
        half = x.shape[-1] // 2
        return jnp.where(low, x[..., half:], x[..., :half])

    def swap(x):
        return lax.ppermute(x, "core", [(0, 1), (1, 0)])

    def up(x, k):
        return lax.ppermute(x, "chip", [(i, i + k) for i in range(chips - k)])

    def down(x, k):
        return lax.ppermute(x, "chip", [(i + k, i) for i in range(chips - k)])

    def round_chips(x, k):
        return lax.ppermute(x, "chip", [(i, (i + k) % chips) for i in range(chips)])

    def across(x, k):
        return lax.ppermute(x, "dp", [(i, i ^ k) for i in range(rows_dp)])

    def in_order(mine, theirs, axis):
        return jnp.where(
            low,
            jnp.concatenate([mine, theirs], axis),
            jnp.concatenate([theirs, mine], axis),
        )

    k0, v0, q0, g0 = key_rows[0], values[0], queries[0], out_grad[0]
    near = chips <= 4
    moved = [round_chips(out_weight, k) for k in range(1, chips)] if near else []
    kv_theirs = swap(jnp.concatenate([other(k0), other(v0)], 1))
    kv = jnp.concatenate([own(k0), own(v0)], 1)
    kv = jnp.concatenate([kv, kv_theirs], 0)
    hop = up(kv, 1)
    q = jnp.concatenate([own(q0), swap(other(q0))], 0) * jnp.asarray(HD ** (-0.5), BF16)
    state = forward(info, q, kv, 0, None)
    piece = out_weight.shape[0]
    part = 2 * piece
    if near:
        column, column_theirs = column_halves(info, [out_weight, *moved])
    else:
        column = lax.all_gather(out_weight, "chip", axis=0)
        column, column_theirs = own(column), other(column)
    ours = in_order(column[:, None], swap(column_theirs)[:, None], 1)
    ours = ours.reshape(chips * part, ours.shape[-1])
    share = ours.shape[0]
    half = share // 2
    lower, upper = ours[:half], ours[half:]
    upper_x, lower_y = across(upper, 1), across(lower, 2)
    hop, q, state, lower, upper, upper_x, lower_y, grad_theirs = together(
        (hop, q, state, lower, upper, upper_x, lower_y, swap(g0))
    )
    chunks = [kv, hop]

    hop = up(hop, 1)
    state = forward(info, q, chunks[1], 1, state)
    lower_x, upper_y, diagonal_x, diagonal_y, hop, state = together(
        (across(lower, 1), across(upper, 2), across(lower_y, 1), across(upper_x, 2), hop, state)
    )
    chunks.append(hop)

    last_hop = up(hop, 1)
    for step in steps[2:prior]:
        state = forward(info, q, hop, step, state)
        hop = last_hop
        if step + 1 < prior:
            chunks.append(hop)
            last_hop = up(hop, 1)
    turned = jnp.concatenate([g0.T, grad_theirs.T], 1)

    def strip(k, at, size):
        return lax.dynamic_slice_in_dim(turned, (row ^ k) * share + at, size, 0)

    strips = [
        jnp.concatenate([strip(3, 0, half), strip(1, 0, half)], 0),
        jnp.concatenate([strip(3, half, half), strip(2, half, half)], 0),
        jnp.concatenate([strip(1, half, half), strip(2, 0, half), strip(0, 0, share)], 0),
    ]
    weight, da = gradient_into_heads(
        info,
        g0,
        grad_theirs,
        [(lower, 0, 0), (upper, 0, 1), (lower_x, 1, 0), (upper_x, 1, 1), (lower_y, 2, 0)]
        + [(upper_y, 2, 1), (diagonal_x, 3, 0), (diagonal_y, 3, 1)],
    )
    da, last_hop, state, *strips = together((da, last_hop, state, *strips))
    chunks.append(last_hop)
    att, lse_t, to_x, to_y = forward(info, q, last_hop, prior, state, strips[:2])

    carried = None
    terms = {}
    for step in reversed(steps):
        last = step == 0
        res = backward(info, q, da, lse_t, [chunks[step]], (step,), att, carried, last)
        terms[step] = res[0]
        if carried is None:
            delta_t = res[1]
        if last:
            dq = res[1]
        else:
            carried = (delta_t, res[-1])

    passing = terms[prior]
    for step in range(prior - 1, 2, -1):
        passing = (terms[step].astype(F32) + down(passing, 1).astype(F32)).astype(BF16)
    rest = strip_product(strips[2], att)
    from_x, from_y, got, rest, terms, dq, att = together(
        (across(to_x, 1), across(to_y, 2), down(passing, 1), rest, terms, dq, att)
    )
    part_mine, part_sent = layer_product(att, weight)
    later_x, later_y, here = rest[:half], rest[half:share], rest[share:]
    passing = (terms[2].astype(F32) + got.astype(F32)).astype(BF16)
    to_x = (later_x + from_y[:half].astype(F32)).astype(BF16)
    to_y = (later_y + from_x[:half].astype(F32)).astype(BF16)
    by_x1, by_y0, dq_theirs, part_sent, got = together(
        (across(to_x, 1), across(to_y, 2), swap(dq[tok:]), part_sent, down(passing, 1))
    )
    passing = (terms[1].astype(F32) + got.astype(F32)).astype(BF16)
    coming = down(passing, 1)
    mine = here + jnp.concatenate(
        [
            from_x[half:].astype(F32) + by_y0.astype(F32),
            by_x1.astype(F32) + from_y[half:].astype(F32),
        ],
        0,
    )

    layer_out = (part_mine + swap(part_sent).astype(F32)).astype(BF16)
    query_grad = in_order(dq[:tok], dq_theirs, 1)
    if near:
        final = lax.dynamic_slice_in_dim(mine, chip * part, part, 0)
        got = []
        for k in range(1, chips):
            target = lax.rem(chip + k, chips)
            sent = lax.dynamic_slice_in_dim(mine, target * part, part, 0).astype(BF16)
            got.append(round_chips(sent, k))
        coming, layer_out, query_grad, *got = together((coming, layer_out, query_grad, *got))
        for x in got:
            final = final + x.astype(F32)
    else:
        final = lax.psum_scatter(mine, "chip", scatter_dimension=0, tiled=True)
    total_tokens = rows_dp * chips * rows
    final = final * (1.0 / math.sqrt(total_tokens))
    first_rows, last_rows = final[:piece], final[piece:]
    weight_grad = in_order(
        jnp.where(low, first_rows, last_rows), swap(jnp.where(low, last_rows, first_rows)), 1
    )
    kv_grad = (terms[0] + coming.astype(F32)).astype(BF16)
    theirs = swap(kv_grad[tok:])
    key_grad = in_order(kv_grad[:tok, :HD], theirs[:, :HD], 1)
    value_grad = in_order(kv_grad[:tok, HD:], theirs[:, HD:], 1)
    return (
        layer_out[None],
        query_grad[None],
        key_grad[None],
        value_grad[None],
        weight_grad,
    )


def solution(mesh):
    devices = mesh.devices
    pairs = Mesh(
        devices.reshape(devices.shape[0], devices.shape[1] // 2, 2), ("dp", "chip", "core")
    )
    tokens = P("dp", ("chip", "core"), None)
    features = P(("dp", "chip", "core"), None)
    return jax.shard_map(
        on_device,
        mesh=pairs,
        in_specs=(tokens, tokens, tokens, features, tokens),
        out_specs=(tokens, tokens, tokens, tokens, features),
        check_vma=False,
    )
```

```python
import functools
import math

import jax
import jax.numpy as jnp
from jax import lax
from jax.experimental import pallas as pl
from jax.experimental.layout import Layout, with_layout_constraint
from jax.experimental.pallas import tpu as pltpu
from jax.sharding import Mesh
from jax.sharding import PartitionSpec as P

QH = 4
KH = 2
HD = 256
WINDOW = 2048
GROUPS = QH // KH
LANES = 128
NEG = -1e30
F32 = jnp.float32
BF16 = jnp.bfloat16
NT = (((1,), (1,)), ((), ()))
TN = (((0,), (0,)), ((), ()))
FILLER = pl.CostEstimate(flops=1, bytes_accessed=1, transcendentals=0)


def dot(a, b, dims=(((1,), (0,)), ((), ()))):
    return lax.dot_general(a, b, dims, preferred_element_type=F32)


def admitted(step, rows, core, query_axis):
    if step > 0 and (step + 1) * rows <= WINDOW:
        return None
    shape = (rows, rows)
    half = rows // 2
    query = (lax.broadcasted_iota(jnp.int32, shape, query_axis) + core * half) % rows
    key = (lax.broadcasted_iota(jnp.int32, shape, 1 - query_axis) + core * half) % rows
    gap = key - query - step * rows
    return (gap <= 0) & (gap > -WINDOW)


def forward_kernel(step, rows, first, last, info, q, kv, *refs):
    if not first:
        m_in, l_in, acc_in = refs[:3]
        refs = refs[3:]
    if last:
        strip_x, strip_y, out, lse_t, to_x, to_y, m_s, l_s, acc_s = refs
    else:
        m_s, l_s, acc_s = refs
    chip, core = info[0], info[1]
    mask = admitted(step, rows, core, 1)

    def block():
        keys = kv[:, :HD]
        vals_t = jnp.transpose(kv[:, HD:])
        for h in range(GROUPS):
            cols = slice(h * HD, (h + 1) * HD)
            stat = slice(h * 8, h * 8 + 1)
            whole = slice(h * 8, (h + 1) * 8)
            s = dot(keys, q[:, cols], NT)
            if mask is not None:
                s = jnp.where(mask, s, NEG)
            top = jnp.max(s, axis=0, keepdims=True)
            if first:
                p = jnp.exp(s - top)
                total = jnp.sum(p, axis=0, keepdims=True)
                acc_s[cols, :] = dot(vals_t, p.astype(BF16))
            else:
                before = m_in[stat, :]
                top = jnp.maximum(top, before)
                p = jnp.exp(s - top)
                keep = jnp.exp(before - top)
                total = keep * l_in[stat, :] + jnp.sum(p, axis=0, keepdims=True)
                acc_s[cols, :] = keep * acc_in[cols, :] + dot(vals_t, p.astype(BF16))
            m_s[whole, :] = jnp.broadcast_to(top, (8, rows))
            l_s[whole, :] = jnp.broadcast_to(total, (8, rows))

    if first:
        block()
    else:

        def keep_all():
            m_s[...] = m_in[...]
            l_s[...] = l_in[...]
            acc_s[...] = acc_in[...]

        pl.when(chip >= step)(block)
        pl.when(chip < step)(keep_all)
    if last:
        for h in range(GROUPS):
            cols = slice(h * HD, (h + 1) * HD)
            total = l_s[h * 8 : h * 8 + 1, :]
            out[:, cols] = jnp.transpose(acc_s[cols, :] / total).astype(BF16)
        lse_t[...] = m_s[...] + jnp.log(l_s[...])
        to_x[...] = dot(strip_x[...], out[...]).astype(BF16)
        to_y[...] = dot(strip_y[...], out[...]).astype(BF16)


def forward(info, q, kv, step, state, strips=()):
    rows = q.shape[0]
    first = state is None
    last = len(strips) > 0
    stat = jax.ShapeDtypeStruct((GROUPS * 8, rows), F32)
    acc = jax.ShapeDtypeStruct((GROUPS * HD, rows), F32)
    vmem = pl.BlockSpec(memory_space=pltpu.VMEM)
    smem = pl.BlockSpec(memory_space=pltpu.SMEM)
    scratch = []
    if last:
        outs = (jax.ShapeDtypeStruct((rows, GROUPS * HD), BF16), stat)
        outs += tuple(jax.ShapeDtypeStruct((x.shape[0], GROUPS * HD), BF16) for x in strips)
        scratch = [pltpu.VMEM(s.shape, F32) for s in (stat, stat, acc)]
    else:
        outs = (stat, stat, acc)
    args = [info, q, kv] + ([] if first else list(state)) + list(strips)
    return pl.pallas_call(
        functools.partial(forward_kernel, step, rows, first, last),
        out_shape=outs,
        in_specs=[smem] + [vmem] * (len(args) - 1),
        out_specs=tuple(vmem for _ in outs),
        scratch_shapes=scratch,
        cost_estimate=FILLER,
        compiler_params=pltpu.CompilerParams(vmem_limit_bytes=16 * 1024 * 1024),
        name="attend_forward",
    )(*args)


def backward_kernel(steps, rows, first, last, info, q, da, lse_t, *refs):
    chunks = refs[: len(steps)]
    refs = refs[len(steps) :]
    if first:
        att = refs[0]
        refs = refs[1:]
    else:
        delta_t, dq_in = refs[:2]
        refs = refs[2:]
    grads = refs[: len(steps)]
    refs = refs[len(steps) :]
    if last:
        dq_out = refs[0]
        refs = refs[1:]
    if first:
        delta_t = refs[0]
        refs = refs[1:]
    dq_s = refs[0]
    chip, core = info[0], info[1]
    if first:
        for h in range(GROUPS):
            cols = slice(h * HD, (h + 1) * HD)
            prod = da[:, cols].astype(F32) * att[:, cols].astype(F32)
            delta = jnp.sum(prod, axis=1, keepdims=True)
            wide = jnp.broadcast_to(delta, (rows, LANES))
            delta_t[h * 8 : (h + 1) * 8, :] = jnp.transpose(wide)[:8, :]
        dq_s[...] = jnp.zeros_like(dq_s)
    else:
        dq_s[...] = dq_in[...]
    for at, step in enumerate(steps):
        mask = admitted(step, rows, core, 1)

        def block(at=at, mask=mask):
            keys = chunks[at][:, :HD]
            keys_t = jnp.transpose(keys)
            vals = chunks[at][:, HD:]
            for h in range(GROUPS):
                cols = slice(h * HD, (h + 1) * HD)
                qh = q[:, cols]
                dah = da[:, cols]
                s = dot(keys, qh, NT)
                p = jnp.exp(s - lse_t[h * 8 : h * 8 + 1, :])
                if mask is not None:
                    p = jnp.where(mask, p, 0.0)
                dp = dot(vals, dah, NT)
                ds = (p * (dp - delta_t[h * 8 : h * 8 + 1, :])).astype(BF16)
                dk = dot(ds, qh)
                dv = dot(p.astype(BF16), dah)
                dq_s[cols, :] += dot(keys_t, ds)
                if h == 0:
                    dk_sum, dv_sum = dk, dv
                else:
                    dk_sum, dv_sum = dk_sum + dk, dv_sum + dv
            grads[at][:, :HD] = dk_sum.astype(grads[at].dtype)
            grads[at][:, HD:] = dv_sum.astype(grads[at].dtype)

        if step == 0:
            block()
        else:

            def blank(at=at):
                grads[at][...] = jnp.zeros_like(grads[at])

            pl.when(chip >= step)(block)
            pl.when(chip < step)(blank)
    if last:
        for h in range(GROUPS):
            cols = slice(h * HD, (h + 1) * HD)
            dq_out[:, cols] = jnp.transpose(dq_s[cols, :] * HD ** (-0.5)).astype(BF16)


def backward(info, q, da, lse_t, chunks, steps, att, carried, last):
    rows = q.shape[0]
    first = carried is None
    vmem = pl.BlockSpec(memory_space=pltpu.VMEM)
    smem = pl.BlockSpec(memory_space=pltpu.SMEM)
    wide = (rows, GROUPS * HD)
    tall = (GROUPS * HD, rows)
    outs = [jax.ShapeDtypeStruct((rows, 2 * HD), F32 if s == 0 else BF16) for s in steps]
    if last:
        outs.append(jax.ShapeDtypeStruct(wide, BF16))
    if first:
        outs.append(jax.ShapeDtypeStruct((GROUPS * 8, rows), F32))
    scratch = []
    if last:
        scratch = [pltpu.VMEM(tall, F32)]
    else:
        outs.append(jax.ShapeDtypeStruct(tall, F32))
    args = [info, q, da, lse_t, *chunks] + ([att] if first else list(carried))
    return pl.pallas_call(
        functools.partial(backward_kernel, steps, rows, first, last),
        out_shape=tuple(outs),
        in_specs=[smem] + [vmem] * (len(args) - 1),
        out_specs=tuple(vmem for _ in outs),
        scratch_shapes=scratch,
        cost_estimate=FILLER,
        compiler_params=pltpu.CompilerParams(vmem_limit_bytes=16 * 1024 * 1024),
        name="attend_backward",
    )(*args)


def column_kernel(info, *refs):
    *pieces, own, other = refs
    chip, core = info[0], info[1]
    chips = len(pieces)
    half = own.shape[2]
    for k, ref in enumerate(pieces):
        at = lax.rem(chip - k + chips, chips)
        left, right = ref[:, :half], ref[:, half:]
        own[at] = jnp.where(core == 0, left, right)
        other[at] = jnp.where(core == 0, right, left)


def column_halves(info, pieces):
    rows, width = pieces[0].shape
    shape = jax.ShapeDtypeStruct((len(pieces), rows, width // 2), BF16)
    vmem = pl.BlockSpec(memory_space=pltpu.VMEM)
    return pl.pallas_call(
        column_kernel,
        out_shape=(shape, shape),
        in_specs=[pl.BlockSpec(memory_space=pltpu.SMEM)] + [vmem] * len(pieces),
        out_specs=(vmem, vmem),
        cost_estimate=FILLER,
        compiler_params=pltpu.CompilerParams(vmem_limit_bytes=8 * 1024 * 1024),
        name="column_halves",
    )(info, *pieces)


def into_heads_kernel(places, info, mine, theirs, *refs):
    *pieces, weight, out = refs
    half = pieces[0].shape[0]
    for (k, at), ref in zip(places, pieces):
        start = ((info[2] ^ k) * 2 + at) * half
        weight[pl.ds(pl.multiple_of(start, half), half), :] = ref[...]
    depth = weight.shape[0]
    wide = 256
    tok = mine.shape[0]
    for at, grad in ((0, mine), (tok, theirs)):
        total = dot(grad[:, :wide], weight[:wide, :])
        for i in range(wide, depth, wide):
            total = total + dot(grad[:, i : i + wide], weight[i : i + wide, :])
        out[at : at + tok, :] = total.astype(BF16)


def gradient_into_heads(info, mine, theirs, pieces):
    arrays = [x for x, _, _ in pieces]
    half, width = arrays[0].shape
    vmem = pl.BlockSpec(memory_space=pltpu.VMEM)
    return pl.pallas_call(
        functools.partial(into_heads_kernel, [(k, at) for _, k, at in pieces]),
        out_shape=(
            jax.ShapeDtypeStruct((half * len(pieces), width), BF16),
            jax.ShapeDtypeStruct((2 * mine.shape[0], width), BF16),
        ),
        in_specs=[pl.BlockSpec(memory_space=pltpu.SMEM)] + [vmem] * (2 + len(pieces)),
        out_specs=(vmem, vmem),
        cost_estimate=FILLER,
        compiler_params=pltpu.CompilerParams(vmem_limit_bytes=20 * 1024 * 1024),
        name="gradient_into_heads",
    )(info, mine, theirs, *arrays)


def product_kernel(x, w, *outs):
    result = dot(x[...], w[...], NT if len(outs) == 2 else (((1,), (0,)), ((), ())))
    if len(outs) == 2:
        half = result.shape[0] // 2
        outs[0][...] = result[:half]
        outs[1][...] = result[half:].astype(BF16)
    else:
        outs[0][...] = result


def layer_product(att, weight):
    rows, depth = att.shape
    features = weight.shape[0]
    wide = 256
    block = pl.BlockSpec((rows // 2, wide), lambda i: (0, i))
    return pl.pallas_call(
        product_kernel,
        grid=(features // wide,),
        out_shape=(
            jax.ShapeDtypeStruct((rows // 2, features), F32),
            jax.ShapeDtypeStruct((rows // 2, features), BF16),
        ),
        in_specs=[
            pl.BlockSpec((rows, depth), lambda i: (0, 0)),
            pl.BlockSpec((wide, depth), lambda i: (i, 0)),
        ],
        out_specs=(block, block),
        cost_estimate=FILLER,
        compiler_params=pltpu.CompilerParams(vmem_limit_bytes=16 * 1024 * 1024),
        name="layer_product",
    )(att, weight)


def strip_product(strips, att):
    rows, depth = strips.shape
    tall = rows // 4
    return pl.pallas_call(
        product_kernel,
        grid=(4,),
        out_shape=jax.ShapeDtypeStruct((rows, att.shape[1]), F32),
        in_specs=[
            pl.BlockSpec((tall, depth), lambda i: (i, 0)),
            pl.BlockSpec(att.shape, lambda i: (0, 0)),
        ],
        out_specs=pl.BlockSpec((tall, att.shape[1]), lambda i: (i, 0)),
        cost_estimate=FILLER,
        compiler_params=pltpu.CompilerParams(vmem_limit_bytes=16 * 1024 * 1024),
        name="strip_product",
    )(strips, att)


def on_device(queries, key_rows, values, out_weight, out_grad):
    chip = lax.axis_index("chip")
    core = lax.axis_index("core")
    row = lax.axis_index("dp")
    chips = lax.axis_size("chip")
    rows_dp = lax.axis_size("dp")
    tok = queries.shape[1]
    rows = 2 * tok
    prior = min(-(-WINDOW // rows), chips - 1)
    steps = tuple(range(prior + 1))
    low = core == 0
    info = jnp.stack([chip, core, row]).astype(jnp.int32)
    together = lax.optimization_barrier

    def own(x):
        half = x.shape[-1] // 2
        return jnp.where(low, x[..., :half], x[..., half:])

    def other(x):
        half = x.shape[-1] // 2
        return jnp.where(low, x[..., half:], x[..., :half])

    def swap(x):
        return lax.ppermute(x, "core", [(0, 1), (1, 0)])

    def up(x, k):
        return lax.ppermute(x, "chip", [(i, i + k) for i in range(chips - k)])

    def down(x, k):
        return lax.ppermute(x, "chip", [(i + k, i) for i in range(chips - k)])

    def round_chips(x, k):
        return lax.ppermute(x, "chip", [(i, (i + k) % chips) for i in range(chips)])

    def across(x, k):
        return lax.ppermute(x, "dp", [(i, i ^ k) for i in range(rows_dp)])

    def in_order(mine, theirs, axis):
        return jnp.where(
            low,
            jnp.concatenate([mine, theirs], axis),
            jnp.concatenate([theirs, mine], axis),
        )

    k0, v0, q0, g0 = key_rows[0], values[0], queries[0], out_grad[0]
    near = chips <= 4
    moved = [round_chips(out_weight, k) for k in range(1, chips)] if near else []
    kv_theirs = swap(jnp.concatenate([other(k0), other(v0)], 1))
    kv = jnp.concatenate([own(k0), own(v0)], 1)
    kv = jnp.concatenate([kv, kv_theirs], 0)
    hop = up(kv, 1)
    q = jnp.concatenate([own(q0), swap(other(q0))], 0) * jnp.asarray(HD ** (-0.5), BF16)
    state = forward(info, q, kv, 0, None)
    *moved, hop, q, m_s, l_s, acc_s = together((*moved, hop, q, *state))
    state = (m_s, l_s, acc_s)
    chunks = [kv, hop]

    piece = out_weight.shape[0]
    part = 2 * piece
    if near:
        column, column_theirs = column_halves(info, [out_weight, *moved])
    else:
        column = lax.all_gather(out_weight, "chip", axis=0)
        column, column_theirs = own(column), other(column)
    ours = in_order(column[:, None], swap(column_theirs)[:, None], 1)
    ours = ours.reshape(chips * part, ours.shape[-1])
    share = ours.shape[0]
    half = share // 2
    lower, upper = ours[:half], ours[half:]
    lower, upper, *state = together((lower, upper, *state))
    state = forward(info, q, hop, 1, state)
    hop = up(hop, 1)
    upper_x, lower_y, lower, upper, hop, state, grad_theirs = together(
        (across(upper, 1), across(lower, 2), lower, upper, hop, state, swap(g0))
    )
    grad_theirs = with_layout_constraint(grad_theirs, Layout(major_to_minor=(0, 1)))
    chunks.append(hop)

    last_hop = up(hop, 1)
    for step in steps[2:prior]:
        state = forward(info, q, hop, step, state)
        hop = last_hop
        if step + 1 < prior:
            chunks.append(hop)
            last_hop = up(hop, 1)
    turned = jnp.concatenate([g0.T, grad_theirs.T], 1)

    def strip(k, at, size):
        return lax.dynamic_slice_in_dim(turned, (row ^ k) * share + at, size, 0)

    strips = [
        jnp.concatenate([strip(3, 0, half), strip(1, 0, half)], 0),
        jnp.concatenate([strip(3, half, half), strip(2, half, half)], 0),
        jnp.concatenate([strip(1, half, half), strip(2, 0, half), strip(0, 0, share)], 0),
    ]
    last_hop, state, grad_theirs, *strips = together((last_hop, state, grad_theirs, *strips))
    lower_x, upper_y, diagonal_x, diagonal_y = (
        across(lower, 1),
        across(upper, 2),
        across(lower_y, 1),
        across(upper_x, 2),
    )
    chunks.append(last_hop)
    att, lse_t, to_x, to_y = forward(info, q, last_hop, prior, state, strips[:2])
    att, info = together((att, info))
    weight, da = gradient_into_heads(
        info,
        g0,
        grad_theirs,
        [(lower, 0, 0), (upper, 0, 1), (lower_x, 1, 0), (upper_x, 1, 1), (lower_y, 2, 0)]
        + [(upper_y, 2, 1), (diagonal_x, 3, 0), (diagonal_y, 3, 1)],
    )

    carried = None
    terms = {}
    for step in reversed(steps):
        last = step == 0
        res = backward(info, q, da, lse_t, [chunks[step]], (step,), att, carried, last)
        terms[step] = res[0]
        if carried is None:
            delta_t = res[1]
        if last:
            dq = res[1]
        else:
            carried = (delta_t, res[-1])

    passing = terms[prior]
    for step in range(prior - 1, 2, -1):
        passing = (terms[step].astype(F32) + down(passing, 1).astype(F32)).astype(BF16)
    rest = strip_product(strips[2], att)
    from_x, from_y, got, rest, terms, dq, att = together(
        (across(to_x, 1), across(to_y, 2), down(passing, 1), rest, terms, dq, att)
    )
    part_mine, part_sent = layer_product(att, weight)
    later_x, later_y, here = rest[:half], rest[half:share], rest[share:]
    passing = (terms[2].astype(F32) + got.astype(F32)).astype(BF16)
    to_x = (later_x + from_y[:half].astype(F32)).astype(BF16)
    to_y = (later_y + from_x[:half].astype(F32)).astype(BF16)
    by_x1, by_y0, dq_theirs, part_sent, got = together(
        (across(to_x, 1), across(to_y, 2), swap(dq[tok:]), part_sent, down(passing, 1))
    )
    passing = (terms[1].astype(F32) + got.astype(F32)).astype(BF16)
    coming = down(passing, 1)
    mine = here + jnp.concatenate(
        [
            from_x[half:].astype(F32) + by_y0.astype(F32),
            by_x1.astype(F32) + from_y[half:].astype(F32),
        ],
        0,
    )

    layer_out = (part_mine + swap(part_sent).astype(F32)).astype(BF16)
    query_grad = in_order(dq[:tok], dq_theirs, 1)
    if near:
        final = lax.dynamic_slice_in_dim(mine, chip * part, part, 0)
        got = []
        for k in range(1, chips):
            target = lax.rem(chip + k, chips)
            sent = lax.dynamic_slice_in_dim(mine, target * part, part, 0).astype(BF16)
            got.append(round_chips(sent, k))
        layer_out, query_grad, *got = together((layer_out, query_grad, *got))
        for x in got:
            final = final + x.astype(F32)
    else:
        final = lax.psum_scatter(mine, "chip", scatter_dimension=0, tiled=True)
    total_tokens = rows_dp * chips * rows
    final = final * (1.0 / math.sqrt(total_tokens))
    first_rows, last_rows = final[:piece], final[piece:]
    weight_grad = in_order(
        jnp.where(low, first_rows, last_rows), swap(jnp.where(low, last_rows, first_rows)), 1
    )
    coming, weight_grad = together((coming, weight_grad))
    kv_grad = (terms[0] + coming.astype(F32)).astype(BF16)
    theirs = swap(kv_grad[tok:])
    key_grad = in_order(kv_grad[:tok, :HD], theirs[:, :HD], 1)
    value_grad = in_order(kv_grad[:tok, HD:], theirs[:, HD:], 1)
    return (
        layer_out[None],
        query_grad[None],
        key_grad[None],
        value_grad[None],
        weight_grad,
    )


def solution(mesh):
    devices = mesh.devices
    pairs = Mesh(
        devices.reshape(devices.shape[0], devices.shape[1] // 2, 2), ("dp", "chip", "core")
    )
    tokens = P("dp", ("chip", "core"), None)
    features = P(("dp", "chip", "core"), None)
    return jax.shard_map(
        on_device,
        mesh=pairs,
        in_specs=(tokens, tokens, tokens, features, tokens),
        out_specs=(tokens, tokens, tokens, tokens, features),
        check_vma=False,
    )
```

```python
import functools
import math

import jax
import jax.numpy as jnp
from jax import lax
from jax.experimental import pallas as pl
from jax.experimental.pallas import tpu as pltpu
from jax.sharding import Mesh
from jax.sharding import PartitionSpec as P

QH = 4
KH = 2
HD = 256
WINDOW = 2048
GROUPS = QH // KH
LANES = 128
NEG = -1e30
F32 = jnp.float32
BF16 = jnp.bfloat16
NT = (((1,), (1,)), ((), ()))
TN = (((0,), (0,)), ((), ()))
FILLER = pl.CostEstimate(flops=1, bytes_accessed=1, transcendentals=0)


def dot(a, b, dims=(((1,), (0,)), ((), ()))):
    return lax.dot_general(a, b, dims, preferred_element_type=F32)


def admitted(step, rows, core, query_axis):
    if step > 0 and (step + 1) * rows <= WINDOW:
        return None
    shape = (rows, rows)
    half = rows // 2
    query = (lax.broadcasted_iota(jnp.int32, shape, query_axis) + core * half) % rows
    key = (lax.broadcasted_iota(jnp.int32, shape, 1 - query_axis) + core * half) % rows
    gap = key - query - step * rows
    return (gap <= 0) & (gap > -WINDOW)


def forward_kernel(step, rows, first, last, info, q, kv, *refs):
    if not first:
        m_in, l_in, acc_in = refs[:3]
        refs = refs[3:]
    if last:
        strip_x, strip_y, out, lse_t, to_x, to_y, m_s, l_s, acc_s = refs
    else:
        m_s, l_s, acc_s = refs
    chip, core = info[0], info[1]
    mask = admitted(step, rows, core, 1)

    def block():
        keys = kv[:, :HD]
        vals_t = jnp.transpose(kv[:, HD:])
        for h in range(GROUPS):
            cols = slice(h * HD, (h + 1) * HD)
            stat = slice(h * 8, h * 8 + 1)
            whole = slice(h * 8, (h + 1) * 8)
            s = dot(keys, q[:, cols], NT)
            if mask is not None:
                s = jnp.where(mask, s, NEG)
            top = jnp.max(s, axis=0, keepdims=True)
            if first:
                p = jnp.exp(s - top)
                total = jnp.sum(p, axis=0, keepdims=True)
                acc_s[cols, :] = dot(vals_t, p.astype(BF16))
            else:
                before = m_in[stat, :]
                top = jnp.maximum(top, before)
                p = jnp.exp(s - top)
                keep = jnp.exp(before - top)
                total = keep * l_in[stat, :] + jnp.sum(p, axis=0, keepdims=True)
                acc_s[cols, :] = keep * acc_in[cols, :] + dot(vals_t, p.astype(BF16))
            m_s[whole, :] = jnp.broadcast_to(top, (8, rows))
            l_s[whole, :] = jnp.broadcast_to(total, (8, rows))

    if first:
        block()
    else:

        def keep_all():
            m_s[...] = m_in[...]
            l_s[...] = l_in[...]
            acc_s[...] = acc_in[...]

        pl.when(chip >= step)(block)
        pl.when(chip < step)(keep_all)
    if last:
        for h in range(GROUPS):
            cols = slice(h * HD, (h + 1) * HD)
            total = l_s[h * 8 : h * 8 + 1, :]
            out[:, cols] = jnp.transpose(acc_s[cols, :] / total).astype(BF16)
        lse_t[...] = m_s[...] + jnp.log(l_s[...])
        to_x[...] = dot(strip_x[...], out[...]).astype(BF16)
        to_y[...] = dot(strip_y[...], out[...]).astype(BF16)


def forward(info, q, kv, step, state, strips=()):
    rows = q.shape[0]
    first = state is None
    last = len(strips) > 0
    stat = jax.ShapeDtypeStruct((GROUPS * 8, rows), F32)
    acc = jax.ShapeDtypeStruct((GROUPS * HD, rows), F32)
    vmem = pl.BlockSpec(memory_space=pltpu.VMEM)
    smem = pl.BlockSpec(memory_space=pltpu.SMEM)
    scratch = []
    if last:
        outs = (jax.ShapeDtypeStruct((rows, GROUPS * HD), BF16), stat)
        outs += tuple(jax.ShapeDtypeStruct((x.shape[0], GROUPS * HD), BF16) for x in strips)
        scratch = [pltpu.VMEM(s.shape, F32) for s in (stat, stat, acc)]
    else:
        outs = (stat, stat, acc)
    args = [info, q, kv] + ([] if first else list(state)) + list(strips)
    return pl.pallas_call(
        functools.partial(forward_kernel, step, rows, first, last),
        out_shape=outs,
        in_specs=[smem] + [vmem] * (len(args) - 1),
        out_specs=tuple(vmem for _ in outs),
        scratch_shapes=scratch,
        cost_estimate=FILLER,
        compiler_params=pltpu.CompilerParams(vmem_limit_bytes=16 * 1024 * 1024),
        name="attend_forward",
    )(*args)


def backward_kernel(steps, rows, first, last, info, q, da, lse_t, *refs):
    chunks = refs[: len(steps)]
    refs = refs[len(steps) :]
    if first:
        att = refs[0]
        refs = refs[1:]
    else:
        delta_t, dq_in = refs[:2]
        refs = refs[2:]
    grads = refs[: len(steps)]
    refs = refs[len(steps) :]
    if last:
        dq_out = refs[0]
        refs = refs[1:]
    if first:
        delta_t = refs[0]
        refs = refs[1:]
    dq_s = refs[0]
    chip, core = info[0], info[1]
    if first:
        for h in range(GROUPS):
            cols = slice(h * HD, (h + 1) * HD)
            prod = da[:, cols].astype(F32) * att[:, cols].astype(F32)
            delta = jnp.sum(prod, axis=1, keepdims=True)
            wide = jnp.broadcast_to(delta, (rows, LANES))
            delta_t[h * 8 : (h + 1) * 8, :] = jnp.transpose(wide)[:8, :]
        dq_s[...] = jnp.zeros_like(dq_s)
    else:
        dq_s[...] = dq_in[...]
    for at, step in enumerate(steps):
        mask = admitted(step, rows, core, 1)

        def block(at=at, mask=mask):
            keys = chunks[at][:, :HD]
            keys_t = jnp.transpose(keys)
            vals = chunks[at][:, HD:]
            for h in range(GROUPS):
                cols = slice(h * HD, (h + 1) * HD)
                qh = q[:, cols]
                dah = da[:, cols]
                s = dot(keys, qh, NT)
                p = jnp.exp(s - lse_t[h * 8 : h * 8 + 1, :])
                if mask is not None:
                    p = jnp.where(mask, p, 0.0)
                dp = dot(vals, dah, NT)
                ds = (p * (dp - delta_t[h * 8 : h * 8 + 1, :])).astype(BF16)
                dk = dot(ds, qh)
                dv = dot(p.astype(BF16), dah)
                dq_s[cols, :] += dot(keys_t, ds)
                if h == 0:
                    dk_sum, dv_sum = dk, dv
                else:
                    dk_sum, dv_sum = dk_sum + dk, dv_sum + dv
            grads[at][:, :HD] = dk_sum.astype(grads[at].dtype)
            grads[at][:, HD:] = dv_sum.astype(grads[at].dtype)

        if step == 0:
            block()
        else:

            def blank(at=at):
                grads[at][...] = jnp.zeros_like(grads[at])

            pl.when(chip >= step)(block)
            pl.when(chip < step)(blank)
    if last:
        for h in range(GROUPS):
            cols = slice(h * HD, (h + 1) * HD)
            dq_out[:, cols] = jnp.transpose(dq_s[cols, :] * HD ** (-0.5)).astype(BF16)


def backward(info, q, da, lse_t, chunks, steps, att, carried, last):
    rows = q.shape[0]
    first = carried is None
    vmem = pl.BlockSpec(memory_space=pltpu.VMEM)
    smem = pl.BlockSpec(memory_space=pltpu.SMEM)
    wide = (rows, GROUPS * HD)
    tall = (GROUPS * HD, rows)
    outs = [jax.ShapeDtypeStruct((rows, 2 * HD), F32 if s == 0 else BF16) for s in steps]
    if last:
        outs.append(jax.ShapeDtypeStruct(wide, BF16))
    if first:
        outs.append(jax.ShapeDtypeStruct((GROUPS * 8, rows), F32))
    scratch = []
    if last:
        scratch = [pltpu.VMEM(tall, F32)]
    else:
        outs.append(jax.ShapeDtypeStruct(tall, F32))
    args = [info, q, da, lse_t, *chunks] + ([att] if first else list(carried))
    return pl.pallas_call(
        functools.partial(backward_kernel, steps, rows, first, last),
        out_shape=tuple(outs),
        in_specs=[smem] + [vmem] * (len(args) - 1),
        out_specs=tuple(vmem for _ in outs),
        scratch_shapes=scratch,
        cost_estimate=FILLER,
        compiler_params=pltpu.CompilerParams(vmem_limit_bytes=16 * 1024 * 1024),
        name="attend_backward",
    )(*args)


def column_kernel(info, *refs):
    *pieces, own, other = refs
    chip, core = info[0], info[1]
    chips = len(pieces)
    half = own.shape[2]
    for k, ref in enumerate(pieces):
        at = lax.rem(chip - k + chips, chips)
        left, right = ref[:, :half], ref[:, half:]
        own[at] = jnp.where(core == 0, left, right)
        other[at] = jnp.where(core == 0, right, left)


def column_halves(info, pieces):
    rows, width = pieces[0].shape
    shape = jax.ShapeDtypeStruct((len(pieces), rows, width // 2), BF16)
    vmem = pl.BlockSpec(memory_space=pltpu.VMEM)
    return pl.pallas_call(
        column_kernel,
        out_shape=(shape, shape),
        in_specs=[pl.BlockSpec(memory_space=pltpu.SMEM)] + [vmem] * len(pieces),
        out_specs=(vmem, vmem),
        cost_estimate=pl.CostEstimate(flops=4 * 10**9, bytes_accessed=1, transcendentals=0),
        compiler_params=pltpu.CompilerParams(vmem_limit_bytes=8 * 1024 * 1024),
        name="column_halves",
    )(info, *pieces)


def into_heads_kernel(places, info, mine, theirs, *refs):
    *pieces, weight, out = refs
    half = pieces[0].shape[0]
    for (k, at), ref in zip(places, pieces):
        start = ((info[2] ^ k) * 2 + at) * half
        weight[pl.ds(pl.multiple_of(start, half), half), :] = ref[...]
    depth = weight.shape[0]
    wide = 256
    tok = mine.shape[0]
    for at, grad in ((0, mine), (tok, theirs)):
        total = dot(grad[:, :wide], weight[:wide, :])
        for i in range(wide, depth, wide):
            total = total + dot(grad[:, i : i + wide], weight[i : i + wide, :])
        out[at : at + tok, :] = total.astype(BF16)


def gradient_into_heads(info, mine, theirs, pieces):
    arrays = [x for x, _, _ in pieces]
    half, width = arrays[0].shape
    vmem = pl.BlockSpec(memory_space=pltpu.VMEM)
    return pl.pallas_call(
        functools.partial(into_heads_kernel, [(k, at) for _, k, at in pieces]),
        out_shape=(
            jax.ShapeDtypeStruct((half * len(pieces), width), BF16),
            jax.ShapeDtypeStruct((2 * mine.shape[0], width), BF16),
        ),
        in_specs=[pl.BlockSpec(memory_space=pltpu.SMEM)] + [vmem] * (2 + len(pieces)),
        out_specs=(vmem, vmem),
        cost_estimate=FILLER,
        compiler_params=pltpu.CompilerParams(vmem_limit_bytes=20 * 1024 * 1024),
        name="gradient_into_heads",
    )(info, mine, theirs, *arrays)


def product_kernel(x, w, *outs):
    result = dot(x[...], w[...], NT if len(outs) == 2 else (((1,), (0,)), ((), ())))
    if len(outs) == 2:
        half = result.shape[0] // 2
        outs[0][...] = result[:half]
        outs[1][...] = result[half:].astype(BF16)
    else:
        outs[0][...] = result


def layer_product(att, weight):
    rows, depth = att.shape
    features = weight.shape[0]
    wide = 256
    block = pl.BlockSpec((rows // 2, wide), lambda i: (0, i))
    return pl.pallas_call(
        product_kernel,
        grid=(features // wide,),
        out_shape=(
            jax.ShapeDtypeStruct((rows // 2, features), F32),
            jax.ShapeDtypeStruct((rows // 2, features), BF16),
        ),
        in_specs=[
            pl.BlockSpec((rows, depth), lambda i: (0, 0)),
            pl.BlockSpec((wide, depth), lambda i: (i, 0)),
        ],
        out_specs=(block, block),
        cost_estimate=FILLER,
        compiler_params=pltpu.CompilerParams(vmem_limit_bytes=16 * 1024 * 1024),
        name="layer_product",
    )(att, weight)


def strip_product(strips, att):
    rows, depth = strips.shape
    tall = rows // 4
    return pl.pallas_call(
        product_kernel,
        grid=(4,),
        out_shape=jax.ShapeDtypeStruct((rows, att.shape[1]), F32),
        in_specs=[
            pl.BlockSpec((tall, depth), lambda i: (i, 0)),
            pl.BlockSpec(att.shape, lambda i: (0, 0)),
        ],
        out_specs=pl.BlockSpec((tall, att.shape[1]), lambda i: (i, 0)),
        cost_estimate=FILLER,
        compiler_params=pltpu.CompilerParams(vmem_limit_bytes=16 * 1024 * 1024),
        name="strip_product",
    )(strips, att)


def on_device(queries, key_rows, values, out_weight, out_grad):
    chip = lax.axis_index("chip")
    core = lax.axis_index("core")
    row = lax.axis_index("dp")
    chips = lax.axis_size("chip")
    rows_dp = lax.axis_size("dp")
    tok = queries.shape[1]
    rows = 2 * tok
    prior = min(-(-WINDOW // rows), chips - 1)
    steps = tuple(range(prior + 1))
    low = core == 0
    info = jnp.stack([chip, core, row]).astype(jnp.int32)
    together = lax.optimization_barrier

    def own(x):
        half = x.shape[-1] // 2
        return jnp.where(low, x[..., :half], x[..., half:])

    def other(x):
        half = x.shape[-1] // 2
        return jnp.where(low, x[..., half:], x[..., :half])

    def swap(x):
        return lax.ppermute(x, "core", [(0, 1), (1, 0)])

    def up(x, k):
        return lax.ppermute(x, "chip", [(i, i + k) for i in range(chips - k)])

    def down(x, k):
        return lax.ppermute(x, "chip", [(i + k, i) for i in range(chips - k)])

    def round_chips(x, k):
        return lax.ppermute(x, "chip", [(i, (i + k) % chips) for i in range(chips)])

    def across(x, k):
        return lax.ppermute(x, "dp", [(i, i ^ k) for i in range(rows_dp)])

    def in_order(mine, theirs, axis):
        return jnp.where(
            low,
            jnp.concatenate([mine, theirs], axis),
            jnp.concatenate([theirs, mine], axis),
        )

    k0, v0, q0, g0 = key_rows[0], values[0], queries[0], out_grad[0]
    near = chips <= 4
    moved = [round_chips(out_weight, k) for k in range(1, chips)] if near else []
    kv_theirs = swap(jnp.concatenate([other(k0), other(v0)], 1))
    kv = jnp.concatenate([own(k0), own(v0)], 1)
    kv = jnp.concatenate([kv, kv_theirs], 0)
    hop = up(kv, 1)
    q = jnp.concatenate([own(q0), swap(other(q0))], 0) * jnp.asarray(HD ** (-0.5), BF16)
    state = forward(info, q, kv, 0, None)
    piece = out_weight.shape[0]
    part = 2 * piece
    if near:
        column, column_theirs = column_halves(info, [out_weight, *moved])
    else:
        column = lax.all_gather(out_weight, "chip", axis=0)
        column, column_theirs = own(column), other(column)
    ours = in_order(column[:, None], swap(column_theirs)[:, None], 1)
    ours = ours.reshape(chips * part, ours.shape[-1])
    share = ours.shape[0]
    half = share // 2
    lower, upper = ours[:half], ours[half:]
    upper_x, lower_y = across(upper, 1), across(lower, 2)
    hop, q, state, lower, upper, upper_x, lower_y, grad_theirs = together(
        (hop, q, state, lower, upper, upper_x, lower_y, swap(g0))
    )
    chunks = [kv, hop]

    hop = up(hop, 1)
    state = forward(info, q, chunks[1], 1, state)
    lower_x, upper_y, diagonal_x, diagonal_y, hop, state = together(
        (across(lower, 1), across(upper, 2), across(lower_y, 1), across(upper_x, 2), hop, state)
    )
    chunks.append(hop)

    last_hop = up(hop, 1)
    for step in steps[2:prior]:
        state = forward(info, q, hop, step, state)
        hop = last_hop
        if step + 1 < prior:
            chunks.append(hop)
            last_hop = up(hop, 1)
    turned = jnp.concatenate([g0.T, grad_theirs.T], 1)

    def strip(k, at, size):
        return lax.dynamic_slice_in_dim(turned, (row ^ k) * share + at, size, 0)

    strips = [
        jnp.concatenate([strip(3, 0, half), strip(1, 0, half)], 0),
        jnp.concatenate([strip(3, half, half), strip(2, half, half)], 0),
        jnp.concatenate([strip(1, half, half), strip(2, 0, half), strip(0, 0, share)], 0),
    ]
    weight, da = gradient_into_heads(
        info,
        g0,
        grad_theirs,
        [(lower, 0, 0), (upper, 0, 1), (lower_x, 1, 0), (upper_x, 1, 1), (lower_y, 2, 0)]
        + [(upper_y, 2, 1), (diagonal_x, 3, 0), (diagonal_y, 3, 1)],
    )
    da, last_hop, state, *strips = together((da, last_hop, state, *strips))
    chunks.append(last_hop)
    att, lse_t, to_x, to_y = forward(info, q, last_hop, prior, state, strips[:2])

    carried = None
    terms = {}
    for step in reversed(steps):
        last = step == 0
        res = backward(info, q, da, lse_t, [chunks[step]], (step,), att, carried, last)
        terms[step] = res[0]
        if carried is None:
            delta_t = res[1]
        if last:
            dq = res[1]
        else:
            carried = (delta_t, res[-1])

    passing = terms[prior]
    for step in range(prior - 1, 2, -1):
        passing = (terms[step].astype(F32) + down(passing, 1).astype(F32)).astype(BF16)
    rest = strip_product(strips[2], att)
    from_x, from_y, got, rest, terms, dq, att = together(
        (across(to_x, 1), across(to_y, 2), down(passing, 1), rest, terms, dq, att)
    )
    part_mine, part_sent = layer_product(att, weight)
    later_x, later_y, here = rest[:half], rest[half:share], rest[share:]
    passing = (terms[2].astype(F32) + got.astype(F32)).astype(BF16)
    to_x = (later_x + from_y[:half].astype(F32)).astype(BF16)
    to_y = (later_y + from_x[:half].astype(F32)).astype(BF16)
    by_x1, by_y0, dq_theirs, part_sent, got = together(
        (across(to_x, 1), across(to_y, 2), swap(dq[tok:]), part_sent, down(passing, 1))
    )
    passing = (terms[1].astype(F32) + got.astype(F32)).astype(BF16)
    coming = down(passing, 1)
    mine = here + jnp.concatenate(
        [
            from_x[half:].astype(F32) + by_y0.astype(F32),
            by_x1.astype(F32) + from_y[half:].astype(F32),
        ],
        0,
    )

    layer_out = (part_mine + swap(part_sent).astype(F32)).astype(BF16)
    query_grad = in_order(dq[:tok], dq_theirs, 1)
    if near:
        final = lax.dynamic_slice_in_dim(mine, chip * part, part, 0)
        got = []
        for k in range(1, chips):
            target = lax.rem(chip + k, chips)
            sent = lax.dynamic_slice_in_dim(mine, target * part, part, 0).astype(BF16)
            got.append(round_chips(sent, k))
        *got, layer_out, query_grad, coming = together((*got, layer_out, query_grad, coming))
        for x in got:
            final = final + x.astype(F32)
    else:
        final = lax.psum_scatter(mine, "chip", scatter_dimension=0, tiled=True)
    total_tokens = rows_dp * chips * rows
    final = final * (1.0 / math.sqrt(total_tokens))
    first_rows, last_rows = final[:piece], final[piece:]
    weight_grad = in_order(
        jnp.where(low, first_rows, last_rows), swap(jnp.where(low, last_rows, first_rows)), 1
    )
    kv_grad = (terms[0] + coming.astype(F32)).astype(BF16)
    theirs = swap(kv_grad[tok:])
    key_grad = in_order(kv_grad[:tok, :HD], theirs[:, :HD], 1)
    value_grad = in_order(kv_grad[:tok, HD:], theirs[:, HD:], 1)
    return (
        layer_out[None],
        query_grad[None],
        key_grad[None],
        value_grad[None],
        weight_grad,
    )


def solution(mesh):
    devices = mesh.devices
    pairs = Mesh(
        devices.reshape(devices.shape[0], devices.shape[1] // 2, 2), ("dp", "chip", "core")
    )
    tokens = P("dp", ("chip", "core"), None)
    features = P(("dp", "chip", "core"), None)
    return jax.shard_map(
        on_device,
        mesh=pairs,
        in_specs=(tokens, tokens, tokens, features, tokens),
        out_specs=(tokens, tokens, tokens, tokens, features),
        check_vma=False,
    )
```

```python
import functools
import math

import jax
import jax.numpy as jnp
from jax import lax
from jax.experimental import pallas as pl
from jax.experimental.pallas import tpu as pltpu
from jax.sharding import Mesh
from jax.sharding import PartitionSpec as P

QH = 4
KH = 2
HD = 256
WINDOW = 2048
GROUPS = QH // KH
LANES = 128
NEG = -1e30
F32 = jnp.float32
BF16 = jnp.bfloat16
NT = (((1,), (1,)), ((), ()))
TN = (((0,), (0,)), ((), ()))
FILLER = pl.CostEstimate(flops=1, bytes_accessed=1, transcendentals=0)


def dot(a, b, dims=(((1,), (0,)), ((), ()))):
    return lax.dot_general(a, b, dims, preferred_element_type=F32)


def admitted(step, rows, core, query_axis):
    if step > 0 and (step + 1) * rows <= WINDOW:
        return None
    shape = (rows, rows)
    half = rows // 2
    query = (lax.broadcasted_iota(jnp.int32, shape, query_axis) + core * half) % rows
    key = (lax.broadcasted_iota(jnp.int32, shape, 1 - query_axis) + core * half) % rows
    gap = key - query - step * rows
    return (gap <= 0) & (gap > -WINDOW)


def forward_kernel(step, rows, first, last, info, q, kv, *refs):
    if not first:
        m_in, l_in, acc_in = refs[:3]
        refs = refs[3:]
    if last:
        strip_x, strip_y, out, lse_t, to_x, to_y, m_s, l_s, acc_s = refs
    else:
        m_s, l_s, acc_s = refs
    chip, core = info[0], info[1]
    mask = admitted(step, rows, core, 1)

    def block():
        keys = kv[:, :HD]
        vals_t = jnp.transpose(kv[:, HD:])
        for h in range(GROUPS):
            cols = slice(h * HD, (h + 1) * HD)
            stat = slice(h * 8, h * 8 + 1)
            whole = slice(h * 8, (h + 1) * 8)
            s = dot(keys, q[:, cols], NT)
            if mask is not None:
                s = jnp.where(mask, s, NEG)
            top = jnp.max(s, axis=0, keepdims=True)
            if first:
                p = jnp.exp(s - top)
                total = jnp.sum(p, axis=0, keepdims=True)
                acc_s[cols, :] = dot(vals_t, p.astype(BF16))
            else:
                before = m_in[stat, :]
                top = jnp.maximum(top, before)
                p = jnp.exp(s - top)
                keep = jnp.exp(before - top)
                total = keep * l_in[stat, :] + jnp.sum(p, axis=0, keepdims=True)
                acc_s[cols, :] = keep * acc_in[cols, :] + dot(vals_t, p.astype(BF16))
            m_s[whole, :] = jnp.broadcast_to(top, (8, rows))
            l_s[whole, :] = jnp.broadcast_to(total, (8, rows))

    if first:
        block()
    else:

        def keep_all():
            m_s[...] = m_in[...]
            l_s[...] = l_in[...]
            acc_s[...] = acc_in[...]

        pl.when(chip >= step)(block)
        pl.when(chip < step)(keep_all)
    if last:
        for h in range(GROUPS):
            cols = slice(h * HD, (h + 1) * HD)
            total = l_s[h * 8 : h * 8 + 1, :]
            out[:, cols] = jnp.transpose(acc_s[cols, :] / total).astype(BF16)
        lse_t[...] = m_s[...] + jnp.log(l_s[...])
        to_x[...] = dot(strip_x[...], out[...]).astype(BF16)
        to_y[...] = dot(strip_y[...], out[...]).astype(BF16)


def forward(info, q, kv, step, state, strips=()):
    rows = q.shape[0]
    first = state is None
    last = len(strips) > 0
    stat = jax.ShapeDtypeStruct((GROUPS * 8, rows), F32)
    acc = jax.ShapeDtypeStruct((GROUPS * HD, rows), F32)
    vmem = pl.BlockSpec(memory_space=pltpu.VMEM)
    smem = pl.BlockSpec(memory_space=pltpu.SMEM)
    scratch = []
    if last:
        outs = (jax.ShapeDtypeStruct((rows, GROUPS * HD), BF16), stat)
        outs += tuple(jax.ShapeDtypeStruct((x.shape[0], GROUPS * HD), BF16) for x in strips)
        scratch = [pltpu.VMEM(s.shape, F32) for s in (stat, stat, acc)]
    else:
        outs = (stat, stat, acc)
    args = [info, q, kv] + ([] if first else list(state)) + list(strips)
    return pl.pallas_call(
        functools.partial(forward_kernel, step, rows, first, last),
        out_shape=outs,
        in_specs=[smem] + [vmem] * (len(args) - 1),
        out_specs=tuple(vmem for _ in outs),
        scratch_shapes=scratch,
        cost_estimate=FILLER,
        compiler_params=pltpu.CompilerParams(vmem_limit_bytes=16 * 1024 * 1024),
        name="attend_forward",
    )(*args)


def backward_kernel(steps, rows, first, last, info, q, da, lse_t, *refs):
    chunks = refs[: len(steps)]
    refs = refs[len(steps) :]
    if first:
        att = refs[0]
        refs = refs[1:]
    else:
        delta_t, dq_in = refs[:2]
        refs = refs[2:]
    grads = refs[: len(steps)]
    refs = refs[len(steps) :]
    if last:
        dq_out = refs[0]
        refs = refs[1:]
    if first:
        delta_t = refs[0]
        refs = refs[1:]
    dq_s = refs[0]
    chip, core = info[0], info[1]
    if first:
        for h in range(GROUPS):
            cols = slice(h * HD, (h + 1) * HD)
            prod = da[:, cols].astype(F32) * att[:, cols].astype(F32)
            delta = jnp.sum(prod, axis=1, keepdims=True)
            wide = jnp.broadcast_to(delta, (rows, LANES))
            delta_t[h * 8 : (h + 1) * 8, :] = jnp.transpose(wide)[:8, :]
        dq_s[...] = jnp.zeros_like(dq_s)
    else:
        dq_s[...] = dq_in[...]
    for at, step in enumerate(steps):
        mask = admitted(step, rows, core, 1)

        def block(at=at, mask=mask):
            keys = chunks[at][:, :HD]
            keys_t = jnp.transpose(keys)
            vals = chunks[at][:, HD:]
            for h in range(GROUPS):
                cols = slice(h * HD, (h + 1) * HD)
                qh = q[:, cols]
                dah = da[:, cols]
                s = dot(keys, qh, NT)
                p = jnp.exp(s - lse_t[h * 8 : h * 8 + 1, :])
                if mask is not None:
                    p = jnp.where(mask, p, 0.0)
                dp = dot(vals, dah, NT)
                ds = (p * (dp - delta_t[h * 8 : h * 8 + 1, :])).astype(BF16)
                dk = dot(ds, qh)
                dv = dot(p.astype(BF16), dah)
                dq_s[cols, :] += dot(keys_t, ds)
                if h == 0:
                    dk_sum, dv_sum = dk, dv
                else:
                    dk_sum, dv_sum = dk_sum + dk, dv_sum + dv
            grads[at][:, :HD] = dk_sum.astype(grads[at].dtype)
            grads[at][:, HD:] = dv_sum.astype(grads[at].dtype)

        if step == 0:
            block()
        else:

            def blank(at=at):
                grads[at][...] = jnp.zeros_like(grads[at])

            pl.when(chip >= step)(block)
            pl.when(chip < step)(blank)
    if last:
        for h in range(GROUPS):
            cols = slice(h * HD, (h + 1) * HD)
            dq_out[:, cols] = jnp.transpose(dq_s[cols, :] * HD ** (-0.5)).astype(BF16)


def backward(info, q, da, lse_t, chunks, steps, att, carried, last):
    rows = q.shape[0]
    first = carried is None
    vmem = pl.BlockSpec(memory_space=pltpu.VMEM)
    smem = pl.BlockSpec(memory_space=pltpu.SMEM)
    wide = (rows, GROUPS * HD)
    tall = (GROUPS * HD, rows)
    outs = [jax.ShapeDtypeStruct((rows, 2 * HD), F32 if s == 0 else BF16) for s in steps]
    if last:
        outs.append(jax.ShapeDtypeStruct(wide, BF16))
    if first:
        outs.append(jax.ShapeDtypeStruct((GROUPS * 8, rows), F32))
    scratch = []
    if last:
        scratch = [pltpu.VMEM(tall, F32)]
    else:
        outs.append(jax.ShapeDtypeStruct(tall, F32))
    args = [info, q, da, lse_t, *chunks] + ([att] if first else list(carried))
    return pl.pallas_call(
        functools.partial(backward_kernel, steps, rows, first, last),
        out_shape=tuple(outs),
        in_specs=[smem] + [vmem] * (len(args) - 1),
        out_specs=tuple(vmem for _ in outs),
        scratch_shapes=scratch,
        cost_estimate=FILLER,
        compiler_params=pltpu.CompilerParams(vmem_limit_bytes=16 * 1024 * 1024),
        name="attend_backward",
    )(*args)


def column_kernel(info, *refs):
    *pieces, own, other = refs
    chip, core = info[0], info[1]
    chips = len(pieces)
    half = own.shape[2]
    for k, ref in enumerate(pieces):
        at = lax.rem(chip - k + chips, chips)
        left, right = ref[:, :half], ref[:, half:]
        own[at] = jnp.where(core == 0, left, right)
        other[at] = jnp.where(core == 0, right, left)


def column_halves(info, pieces):
    rows, width = pieces[0].shape
    shape = jax.ShapeDtypeStruct((len(pieces), rows, width // 2), BF16)
    vmem = pl.BlockSpec(memory_space=pltpu.VMEM)
    return pl.pallas_call(
        column_kernel,
        out_shape=(shape, shape),
        in_specs=[pl.BlockSpec(memory_space=pltpu.SMEM)] + [vmem] * len(pieces),
        out_specs=(vmem, vmem),
        cost_estimate=pl.CostEstimate(flops=4 * 10**9, bytes_accessed=1, transcendentals=0),
        compiler_params=pltpu.CompilerParams(vmem_limit_bytes=8 * 1024 * 1024),
        name="column_halves",
    )(info, *pieces)


def into_heads_kernel(places, info, mine, theirs, *refs):
    *pieces, weight, out = refs
    half = pieces[0].shape[0]
    for (k, at), ref in zip(places, pieces):
        start = ((info[2] ^ k) * 2 + at) * half
        weight[pl.ds(pl.multiple_of(start, half), half), :] = ref[...]
    depth = weight.shape[0]
    wide = 256
    tok = mine.shape[0]
    for at, grad in ((0, mine), (tok, theirs)):
        total = dot(grad[:, :wide], weight[:wide, :])
        for i in range(wide, depth, wide):
            total = total + dot(grad[:, i : i + wide], weight[i : i + wide, :])
        out[at : at + tok, :] = total.astype(BF16)


def gradient_into_heads(info, mine, theirs, pieces):
    arrays = [x for x, _, _ in pieces]
    half, width = arrays[0].shape
    vmem = pl.BlockSpec(memory_space=pltpu.VMEM)
    return pl.pallas_call(
        functools.partial(into_heads_kernel, [(k, at) for _, k, at in pieces]),
        out_shape=(
            jax.ShapeDtypeStruct((half * len(pieces), width), BF16),
            jax.ShapeDtypeStruct((2 * mine.shape[0], width), BF16),
        ),
        in_specs=[pl.BlockSpec(memory_space=pltpu.SMEM)] + [vmem] * (2 + len(pieces)),
        out_specs=(vmem, vmem),
        cost_estimate=FILLER,
        compiler_params=pltpu.CompilerParams(vmem_limit_bytes=20 * 1024 * 1024),
        name="gradient_into_heads",
    )(info, mine, theirs, *arrays)


def plane_sum_kernel(info, rest, from_x, from_y, by_x1, by_y0, kept, farther, sent, total):
    share, part = total.shape[0], kept.shape[0]
    half = share // 2
    total[:half, :] = (
        rest[share : share + half, :] + from_x[half:, :].astype(F32) + by_y0[...].astype(F32)
    )
    total[half:, :] = (
        rest[share + half :, :] + by_x1[...].astype(F32) + from_y[half:, :].astype(F32)
    )

    def block(k):
        return total[pl.ds(pl.multiple_of((info[0] ^ k) * part, part), part), :]

    kept[...] = block(0)
    farther[...] = block(2)
    sent[:part, :] = block(1).astype(BF16)
    sent[part:, :] = block(3).astype(BF16)


def plane_sum(info, rest, *arrived):
    share = rest.shape[0] // 2
    part, width = share // 4, rest.shape[1]
    vmem = pl.BlockSpec(memory_space=pltpu.VMEM)
    return pl.pallas_call(
        plane_sum_kernel,
        out_shape=(
            jax.ShapeDtypeStruct((part, width), F32),
            jax.ShapeDtypeStruct((part, width), F32),
            jax.ShapeDtypeStruct((2 * part, width), BF16),
        ),
        in_specs=[pl.BlockSpec(memory_space=pltpu.SMEM)] + [vmem] * (1 + len(arrived)),
        out_specs=(vmem, vmem, vmem),
        scratch_shapes=[pltpu.VMEM((share, width), F32)],
        cost_estimate=FILLER,
        compiler_params=pltpu.CompilerParams(vmem_limit_bytes=16 * 1024 * 1024),
        name="plane_sum",
    )(info, rest, *arrived)


def product_kernel(x, w, *outs):
    result = dot(x[...], w[...], NT if len(outs) == 2 else (((1,), (0,)), ((), ())))
    if len(outs) == 2:
        half = result.shape[0] // 2
        outs[0][...] = result[:half]
        outs[1][...] = result[half:].astype(BF16)
    else:
        outs[0][...] = result


def layer_product(att, weight):
    rows, depth = att.shape
    features = weight.shape[0]
    wide = 256
    block = pl.BlockSpec((rows // 2, wide), lambda i: (0, i))
    return pl.pallas_call(
        product_kernel,
        grid=(features // wide,),
        out_shape=(
            jax.ShapeDtypeStruct((rows // 2, features), F32),
            jax.ShapeDtypeStruct((rows // 2, features), BF16),
        ),
        in_specs=[
            pl.BlockSpec((rows, depth), lambda i: (0, 0)),
            pl.BlockSpec((wide, depth), lambda i: (i, 0)),
        ],
        out_specs=(block, block),
        cost_estimate=FILLER,
        compiler_params=pltpu.CompilerParams(vmem_limit_bytes=16 * 1024 * 1024),
        name="layer_product",
    )(att, weight)


def strip_product(strips, att):
    rows, depth = strips.shape
    tall = rows // 4
    return pl.pallas_call(
        product_kernel,
        grid=(4,),
        out_shape=jax.ShapeDtypeStruct((rows, att.shape[1]), F32),
        in_specs=[
            pl.BlockSpec((tall, depth), lambda i: (i, 0)),
            pl.BlockSpec(att.shape, lambda i: (0, 0)),
        ],
        out_specs=pl.BlockSpec((tall, att.shape[1]), lambda i: (i, 0)),
        cost_estimate=FILLER,
        compiler_params=pltpu.CompilerParams(vmem_limit_bytes=16 * 1024 * 1024),
        name="strip_product",
    )(strips, att)


def on_device(queries, key_rows, values, out_weight, out_grad):
    chip = lax.axis_index("chip")
    core = lax.axis_index("core")
    row = lax.axis_index("dp")
    chips = lax.axis_size("chip")
    rows_dp = lax.axis_size("dp")
    tok = queries.shape[1]
    rows = 2 * tok
    prior = min(-(-WINDOW // rows), chips - 1)
    steps = tuple(range(prior + 1))
    low = core == 0
    info = jnp.stack([chip, core, row]).astype(jnp.int32)
    together = lax.optimization_barrier

    def own(x):
        half = x.shape[-1] // 2
        return jnp.where(low, x[..., :half], x[..., half:])

    def other(x):
        half = x.shape[-1] // 2
        return jnp.where(low, x[..., half:], x[..., :half])

    def swap(x):
        return lax.ppermute(x, "core", [(0, 1), (1, 0)])

    def up(x, k):
        return lax.ppermute(x, "chip", [(i, i + k) for i in range(chips - k)])

    def down(x, k):
        return lax.ppermute(x, "chip", [(i + k, i) for i in range(chips - k)])

    def round_chips(x, k):
        return lax.ppermute(x, "chip", [(i, (i + k) % chips) for i in range(chips)])

    def across(x, k):
        return lax.ppermute(x, "dp", [(i, i ^ k) for i in range(rows_dp)])

    def in_order(mine, theirs, axis):
        return jnp.where(
            low,
            jnp.concatenate([mine, theirs], axis),
            jnp.concatenate([theirs, mine], axis),
        )

    k0, v0, q0, g0 = key_rows[0], values[0], queries[0], out_grad[0]
    near = chips <= 4
    moved = [round_chips(out_weight, k) for k in range(1, chips)] if near else []
    kv_theirs = swap(jnp.concatenate([other(k0), other(v0)], 1))
    kv = jnp.concatenate([own(k0), own(v0)], 1)
    kv = jnp.concatenate([kv, kv_theirs], 0)
    hop = up(kv, 1)
    q = jnp.concatenate([own(q0), swap(other(q0))], 0) * jnp.asarray(HD ** (-0.5), BF16)
    state = forward(info, q, kv, 0, None)
    piece = out_weight.shape[0]
    part = 2 * piece
    if near:
        column, column_theirs = column_halves(info, [out_weight, *moved])
    else:
        column = lax.all_gather(out_weight, "chip", axis=0)
        column, column_theirs = own(column), other(column)
    ours = in_order(column[:, None], swap(column_theirs)[:, None], 1)
    ours = ours.reshape(chips * part, ours.shape[-1])
    share = ours.shape[0]
    half = share // 2
    lower, upper = ours[:half], ours[half:]
    upper_x, lower_y = across(upper, 1), across(lower, 2)
    hop, q, state, lower, upper, upper_x, lower_y, grad_theirs = together(
        (hop, q, state, lower, upper, upper_x, lower_y, swap(g0))
    )
    chunks = [kv, hop]

    hop = up(hop, 1)
    state = forward(info, q, chunks[1], 1, state)
    lower_x, upper_y, diagonal_x, diagonal_y, hop, state = together(
        (across(lower, 1), across(upper, 2), across(lower_y, 1), across(upper_x, 2), hop, state)
    )
    chunks.append(hop)

    last_hop = up(hop, 1)
    for step in steps[2:prior]:
        state = forward(info, q, hop, step, state)
        hop = last_hop
        if step + 1 < prior:
            chunks.append(hop)
            last_hop = up(hop, 1)
    turned = jnp.concatenate([g0.T, grad_theirs.T], 1)

    def strip(k, at, size):
        return lax.dynamic_slice_in_dim(turned, (row ^ k) * share + at, size, 0)

    strips = [
        jnp.concatenate([strip(3, 0, half), strip(1, 0, half)], 0),
        jnp.concatenate([strip(3, half, half), strip(2, half, half)], 0),
        jnp.concatenate([strip(1, half, half), strip(2, 0, half), strip(0, 0, share)], 0),
    ]
    weight, da = gradient_into_heads(
        info,
        g0,
        grad_theirs,
        [(lower, 0, 0), (upper, 0, 1), (lower_x, 1, 0), (upper_x, 1, 1), (lower_y, 2, 0)]
        + [(upper_y, 2, 1), (diagonal_x, 3, 0), (diagonal_y, 3, 1)],
    )
    da, last_hop, state, *strips = together((da, last_hop, state, *strips))
    chunks.append(last_hop)
    att, lse_t, to_x, to_y = forward(info, q, last_hop, prior, state, strips[:2])

    carried = None
    terms = {}
    for step in reversed(steps):
        last = step == 0
        res = backward(info, q, da, lse_t, [chunks[step]], (step,), att, carried, last)
        terms[step] = res[0]
        if carried is None:
            delta_t = res[1]
        if last:
            dq = res[1]
        else:
            carried = (delta_t, res[-1])

    passing = terms[prior]
    for step in range(prior - 1, 2, -1):
        passing = (terms[step].astype(F32) + down(passing, 1).astype(F32)).astype(BF16)
    rest = strip_product(strips[2], att)
    from_x, from_y, got, rest, terms, dq, att = together(
        (across(to_x, 1), across(to_y, 2), down(passing, 1), rest, terms, dq, att)
    )
    part_mine, part_sent = layer_product(att, weight)
    later_x, later_y, here = rest[:half], rest[half:share], rest[share:]
    passing = (terms[2].astype(F32) + got.astype(F32)).astype(BF16)
    to_x = (later_x + from_y[:half].astype(F32)).astype(BF16)
    to_y = (later_y + from_x[:half].astype(F32)).astype(BF16)
    by_x1, by_y0, dq_theirs, part_sent, got = together(
        (across(to_x, 1), across(to_y, 2), swap(dq[tok:]), part_sent, down(passing, 1))
    )
    passing = (terms[1].astype(F32) + got.astype(F32)).astype(BF16)
    coming = down(passing, 1)
    layer_out = (part_mine + swap(part_sent).astype(F32)).astype(BF16)
    query_grad = in_order(dq[:tok], dq_theirs, 1)
    if chips == 4:

        def pair(x, k):
            return lax.ppermute(x, "chip", [(i, i ^ k) for i in range(chips)])

        final, farther, sent = plane_sum(info, rest, from_x, from_y, by_x1, by_y0)
        got = pair(sent, 1)
        final = final + got[:part].astype(F32)
        got = pair((farther + got[part:].astype(F32)).astype(BF16), 2)
        got, layer_out, query_grad, coming = together((got, layer_out, query_grad, coming))
        final = final + got.astype(F32)
    else:
        mine = here + jnp.concatenate(
            [
                from_x[half:].astype(F32) + by_y0.astype(F32),
                by_x1.astype(F32) + from_y[half:].astype(F32),
            ],
            0,
        )
        final = lax.psum_scatter(mine, "chip", scatter_dimension=0, tiled=True)
    total_tokens = rows_dp * chips * rows
    final = final * (1.0 / math.sqrt(total_tokens))
    first_rows, last_rows = final[:piece], final[piece:]
    weight_grad = in_order(
        jnp.where(low, first_rows, last_rows), swap(jnp.where(low, last_rows, first_rows)), 1
    )
    kv_grad = (terms[0] + coming.astype(F32)).astype(BF16)
    theirs = swap(kv_grad[tok:])
    key_grad = in_order(kv_grad[:tok, :HD], theirs[:, :HD], 1)
    value_grad = in_order(kv_grad[:tok, HD:], theirs[:, HD:], 1)
    return (
        layer_out[None],
        query_grad[None],
        key_grad[None],
        value_grad[None],
        weight_grad,
    )


def solution(mesh):
    devices = mesh.devices
    pairs = Mesh(
        devices.reshape(devices.shape[0], devices.shape[1] // 2, 2), ("dp", "chip", "core")
    )
    tokens = P("dp", ("chip", "core"), None)
    features = P(("dp", "chip", "core"), None)
    return jax.shard_map(
        on_device,
        mesh=pairs,
        in_specs=(tokens, tokens, tokens, features, tokens),
        out_specs=(tokens, tokens, tokens, tokens, features),
        check_vma=False,
    )
```

```python
import functools
import math

import jax
import jax.numpy as jnp
from jax import lax
from jax.experimental import pallas as pl
from jax.experimental.pallas import tpu as pltpu
from jax.sharding import Mesh
from jax.sharding import PartitionSpec as P

QH = 4
KH = 2
HD = 256
WINDOW = 2048
GROUPS = QH // KH
LANES = 128
NEG = -1e30
F32 = jnp.float32
BF16 = jnp.bfloat16
NT = (((1,), (1,)), ((), ()))
TN = (((0,), (0,)), ((), ()))
FILLER = pl.CostEstimate(flops=1, bytes_accessed=1, transcendentals=0)


def dot(a, b, dims=(((1,), (0,)), ((), ()))):
    return lax.dot_general(a, b, dims, preferred_element_type=F32)


def admitted(step, rows, core, query_axis):
    if step > 0 and (step + 1) * rows <= WINDOW:
        return None
    shape = (rows, rows)
    half = rows // 2
    query = (lax.broadcasted_iota(jnp.int32, shape, query_axis) + core * half) % rows
    key = (lax.broadcasted_iota(jnp.int32, shape, 1 - query_axis) + core * half) % rows
    gap = key - query - step * rows
    return (gap <= 0) & (gap > -WINDOW)


def forward_kernel(step, rows, first, last, info, q, kv, *refs):
    if not first:
        m_in, l_in, acc_in = refs[:3]
        refs = refs[3:]
    if last:
        strip_x, strip_y, out, lse_t, to_x, to_y, m_s, l_s, acc_s = refs
    else:
        m_s, l_s, acc_s = refs
    chip, core = info[0], info[1]
    mask = admitted(step, rows, core, 1)

    def block():
        keys = kv[:, :HD]
        vals_t = jnp.transpose(kv[:, HD:])
        for h in range(GROUPS):
            cols = slice(h * HD, (h + 1) * HD)
            stat = slice(h * 8, h * 8 + 1)
            whole = slice(h * 8, (h + 1) * 8)
            s = dot(keys, q[:, cols], NT)
            if mask is not None:
                s = jnp.where(mask, s, NEG)
            top = jnp.max(s, axis=0, keepdims=True)
            if first:
                p = jnp.exp(s - top)
                total = jnp.sum(p, axis=0, keepdims=True)
                acc_s[cols, :] = dot(vals_t, p.astype(BF16))
            else:
                before = m_in[stat, :]
                top = jnp.maximum(top, before)
                p = jnp.exp(s - top)
                keep = jnp.exp(before - top)
                total = keep * l_in[stat, :] + jnp.sum(p, axis=0, keepdims=True)
                acc_s[cols, :] = keep * acc_in[cols, :] + dot(vals_t, p.astype(BF16))
            m_s[whole, :] = jnp.broadcast_to(top, (8, rows))
            l_s[whole, :] = jnp.broadcast_to(total, (8, rows))

    if first:
        block()
    else:

        def keep_all():
            m_s[...] = m_in[...]
            l_s[...] = l_in[...]
            acc_s[...] = acc_in[...]

        pl.when(chip >= step)(block)
        pl.when(chip < step)(keep_all)
    if last:
        for h in range(GROUPS):
            cols = slice(h * HD, (h + 1) * HD)
            total = l_s[h * 8 : h * 8 + 1, :]
            out[:, cols] = jnp.transpose(acc_s[cols, :] / total).astype(BF16)
        lse_t[...] = m_s[...] + jnp.log(l_s[...])
        to_x[...] = dot(strip_x[...], out[...]).astype(BF16)
        to_y[...] = dot(strip_y[...], out[...]).astype(BF16)


def forward(info, q, kv, step, state, strips=()):
    rows = q.shape[0]
    first = state is None
    last = len(strips) > 0
    stat = jax.ShapeDtypeStruct((GROUPS * 8, rows), F32)
    acc = jax.ShapeDtypeStruct((GROUPS * HD, rows), F32)
    vmem = pl.BlockSpec(memory_space=pltpu.VMEM)
    smem = pl.BlockSpec(memory_space=pltpu.SMEM)
    scratch = []
    if last:
        outs = (jax.ShapeDtypeStruct((rows, GROUPS * HD), BF16), stat)
        outs += tuple(jax.ShapeDtypeStruct((x.shape[0], GROUPS * HD), BF16) for x in strips)
        scratch = [pltpu.VMEM(s.shape, F32) for s in (stat, stat, acc)]
    else:
        outs = (stat, stat, acc)
    args = [info, q, kv] + ([] if first else list(state)) + list(strips)
    return pl.pallas_call(
        functools.partial(forward_kernel, step, rows, first, last),
        out_shape=outs,
        in_specs=[smem] + [vmem] * (len(args) - 1),
        out_specs=tuple(vmem for _ in outs),
        scratch_shapes=scratch,
        cost_estimate=FILLER,
        compiler_params=pltpu.CompilerParams(vmem_limit_bytes=16 * 1024 * 1024),
        name="attend_forward",
    )(*args)


def backward_kernel(steps, rows, first, last, info, q, da, lse_t, *refs):
    chunks = refs[: len(steps)]
    refs = refs[len(steps) :]
    if first:
        att = refs[0]
        refs = refs[1:]
    else:
        delta_t, dq_in = refs[:2]
        refs = refs[2:]
    grads = refs[: len(steps)]
    refs = refs[len(steps) :]
    if last:
        dq_out = refs[0]
        refs = refs[1:]
    if first:
        delta_t = refs[0]
        refs = refs[1:]
    dq_s = refs[0]
    chip, core = info[0], info[1]
    if first:
        for h in range(GROUPS):
            cols = slice(h * HD, (h + 1) * HD)
            prod = da[:, cols].astype(F32) * att[:, cols].astype(F32)
            delta = jnp.sum(prod, axis=1, keepdims=True)
            wide = jnp.broadcast_to(delta, (rows, LANES))
            delta_t[h * 8 : (h + 1) * 8, :] = jnp.transpose(wide)[:8, :]
        dq_s[...] = jnp.zeros_like(dq_s)
    else:
        dq_s[...] = dq_in[...]
    for at, step in enumerate(steps):
        mask = admitted(step, rows, core, 1)

        def block(at=at, mask=mask):
            keys = chunks[at][:, :HD]
            keys_t = jnp.transpose(keys)
            vals = chunks[at][:, HD:]
            for h in range(GROUPS):
                cols = slice(h * HD, (h + 1) * HD)
                qh = q[:, cols]
                dah = da[:, cols]
                s = dot(keys, qh, NT)
                p = jnp.exp(s - lse_t[h * 8 : h * 8 + 1, :])
                if mask is not None:
                    p = jnp.where(mask, p, 0.0)
                dp = dot(vals, dah, NT)
                ds = (p * (dp - delta_t[h * 8 : h * 8 + 1, :])).astype(BF16)
                dk = dot(ds, qh)
                dv = dot(p.astype(BF16), dah)
                dq_s[cols, :] += dot(keys_t, ds)
                if h == 0:
                    dk_sum, dv_sum = dk, dv
                else:
                    dk_sum, dv_sum = dk_sum + dk, dv_sum + dv
            grads[at][:, :HD] = dk_sum.astype(grads[at].dtype)
            grads[at][:, HD:] = dv_sum.astype(grads[at].dtype)

        if step == 0:
            block()
        else:

            def blank(at=at):
                grads[at][...] = jnp.zeros_like(grads[at])

            pl.when(chip >= step)(block)
            pl.when(chip < step)(blank)
    if last:
        for h in range(GROUPS):
            cols = slice(h * HD, (h + 1) * HD)
            dq_out[:, cols] = jnp.transpose(dq_s[cols, :] * HD ** (-0.5)).astype(BF16)


def backward(info, q, da, lse_t, chunks, steps, att, carried, last):
    rows = q.shape[0]
    first = carried is None
    vmem = pl.BlockSpec(memory_space=pltpu.VMEM)
    smem = pl.BlockSpec(memory_space=pltpu.SMEM)
    wide = (rows, GROUPS * HD)
    tall = (GROUPS * HD, rows)
    outs = [jax.ShapeDtypeStruct((rows, 2 * HD), F32 if s == 0 else BF16) for s in steps]
    if last:
        outs.append(jax.ShapeDtypeStruct(wide, BF16))
    if first:
        outs.append(jax.ShapeDtypeStruct((GROUPS * 8, rows), F32))
    scratch = []
    if last:
        scratch = [pltpu.VMEM(tall, F32)]
    else:
        outs.append(jax.ShapeDtypeStruct(tall, F32))
    args = [info, q, da, lse_t, *chunks] + ([att] if first else list(carried))
    return pl.pallas_call(
        functools.partial(backward_kernel, steps, rows, first, last),
        out_shape=tuple(outs),
        in_specs=[smem] + [vmem] * (len(args) - 1),
        out_specs=tuple(vmem for _ in outs),
        scratch_shapes=scratch,
        cost_estimate=FILLER,
        compiler_params=pltpu.CompilerParams(vmem_limit_bytes=16 * 1024 * 1024),
        name="attend_backward",
    )(*args)


def column_kernel(info, *refs):
    *pieces, own, other = refs
    chip, core = info[0], info[1]
    chips = len(pieces)
    half = own.shape[2]
    for k, ref in enumerate(pieces):
        at = lax.rem(chip - k + chips, chips)
        left, right = ref[:, :half], ref[:, half:]
        own[at] = jnp.where(core == 0, left, right)
        other[at] = jnp.where(core == 0, right, left)


def column_halves(info, pieces):
    rows, width = pieces[0].shape
    shape = jax.ShapeDtypeStruct((len(pieces), rows, width // 2), BF16)
    vmem = pl.BlockSpec(memory_space=pltpu.VMEM)
    return pl.pallas_call(
        column_kernel,
        out_shape=(shape, shape),
        in_specs=[pl.BlockSpec(memory_space=pltpu.SMEM)] + [vmem] * len(pieces),
        out_specs=(vmem, vmem),
        cost_estimate=pl.CostEstimate(flops=4 * 10**9, bytes_accessed=1, transcendentals=0),
        compiler_params=pltpu.CompilerParams(vmem_limit_bytes=8 * 1024 * 1024),
        name="column_halves",
    )(info, *pieces)


def into_heads_kernel(places, based, info, turned, *refs):
    *pieces, out = refs
    total = None
    if based:
        base, *pieces = pieces
        total = base[...]
    half = pieces[0].shape[0]
    for (k, at), ref in zip(places, pieces):
        start = pl.multiple_of(((info[2] ^ k) * 2 + at) * half, half)
        term = dot(turned[pl.ds(start, half), :], ref[...], TN)
        total = term if total is None else total + term
    out[...] = total.astype(out.dtype)


def gradient_into_heads(info, turned, pieces, base=None):
    arrays = [x for x, _, _ in pieces]
    based = base is not None
    args = ([base] if based else []) + arrays
    vmem = pl.BlockSpec(memory_space=pltpu.VMEM)
    return pl.pallas_call(
        functools.partial(into_heads_kernel, [(k, at) for _, k, at in pieces], based),
        out_shape=jax.ShapeDtypeStruct(
            (turned.shape[1], arrays[0].shape[1]), BF16 if based else F32
        ),
        in_specs=[pl.BlockSpec(memory_space=pltpu.SMEM)] + [vmem] * (1 + len(args)),
        out_specs=vmem,
        cost_estimate=FILLER,
        compiler_params=pltpu.CompilerParams(vmem_limit_bytes=20 * 1024 * 1024),
        name="gradient_into_heads",
    )(info, turned, *args)


def place_kernel(places, info, *refs):
    *pieces, out = refs
    half = pieces[0].shape[0]
    for (k, at), ref in zip(places, pieces):
        start = pl.multiple_of(((info[2] ^ k) * 2 + at) * half, half)
        out[pl.ds(start, half), :] = ref[...]


def placed(info, pieces):
    arrays = [x for x, _, _ in pieces]
    half, width = arrays[0].shape
    vmem = pl.BlockSpec(memory_space=pltpu.VMEM)
    return pl.pallas_call(
        functools.partial(place_kernel, [(k, at) for _, k, at in pieces]),
        out_shape=jax.ShapeDtypeStruct((half * len(pieces), width), BF16),
        in_specs=[pl.BlockSpec(memory_space=pltpu.SMEM)] + [vmem] * len(arrays),
        out_specs=vmem,
        cost_estimate=FILLER,
        compiler_params=pltpu.CompilerParams(vmem_limit_bytes=8 * 1024 * 1024),
        name="place_shares",
    )(info, *arrays)


def plane_sum_kernel(info, rest, from_x, from_y, by_x1, by_y0, kept, farther, sent, total):
    share, part = total.shape[0], kept.shape[0]
    half = share // 2
    total[:half, :] = (
        rest[share : share + half, :] + from_x[half:, :].astype(F32) + by_y0[...].astype(F32)
    )
    total[half:, :] = (
        rest[share + half :, :] + by_x1[...].astype(F32) + from_y[half:, :].astype(F32)
    )

    def block(k):
        return total[pl.ds(pl.multiple_of((info[0] ^ k) * part, part), part), :]

    kept[...] = block(0)
    farther[...] = block(2)
    sent[:part, :] = block(1).astype(BF16)
    sent[part:, :] = block(3).astype(BF16)


def plane_sum(info, rest, *arrived):
    share = rest.shape[0] // 2
    part, width = share // 4, rest.shape[1]
    vmem = pl.BlockSpec(memory_space=pltpu.VMEM)
    return pl.pallas_call(
        plane_sum_kernel,
        out_shape=(
            jax.ShapeDtypeStruct((part, width), F32),
            jax.ShapeDtypeStruct((part, width), F32),
            jax.ShapeDtypeStruct((2 * part, width), BF16),
        ),
        in_specs=[pl.BlockSpec(memory_space=pltpu.SMEM)] + [vmem] * (1 + len(arrived)),
        out_specs=(vmem, vmem, vmem),
        scratch_shapes=[pltpu.VMEM((share, width), F32)],
        cost_estimate=FILLER,
        compiler_params=pltpu.CompilerParams(vmem_limit_bytes=16 * 1024 * 1024),
        name="plane_sum",
    )(info, rest, *arrived)


def product_kernel(x, w, *outs):
    result = dot(x[...], w[...], NT if len(outs) == 2 else (((1,), (0,)), ((), ())))
    if len(outs) == 2:
        half = result.shape[0] // 2
        outs[0][...] = result[:half]
        outs[1][...] = result[half:].astype(BF16)
    else:
        outs[0][...] = result


def layer_product(att, weight):
    rows, depth = att.shape
    features = weight.shape[0]
    wide = 256
    block = pl.BlockSpec((rows // 2, wide), lambda i: (0, i))
    return pl.pallas_call(
        product_kernel,
        grid=(features // wide,),
        out_shape=(
            jax.ShapeDtypeStruct((rows // 2, features), F32),
            jax.ShapeDtypeStruct((rows // 2, features), BF16),
        ),
        in_specs=[
            pl.BlockSpec((rows, depth), lambda i: (0, 0)),
            pl.BlockSpec((wide, depth), lambda i: (i, 0)),
        ],
        out_specs=(block, block),
        cost_estimate=FILLER,
        compiler_params=pltpu.CompilerParams(vmem_limit_bytes=16 * 1024 * 1024),
        name="layer_product",
    )(att, weight)


def strip_product(strips, att):
    rows, depth = strips.shape
    tall = rows // 4
    return pl.pallas_call(
        product_kernel,
        grid=(4,),
        out_shape=jax.ShapeDtypeStruct((rows, att.shape[1]), F32),
        in_specs=[
            pl.BlockSpec((tall, depth), lambda i: (i, 0)),
            pl.BlockSpec(att.shape, lambda i: (0, 0)),
        ],
        out_specs=pl.BlockSpec((tall, att.shape[1]), lambda i: (i, 0)),
        cost_estimate=FILLER,
        compiler_params=pltpu.CompilerParams(vmem_limit_bytes=16 * 1024 * 1024),
        name="strip_product",
    )(strips, att)


def on_device(queries, key_rows, values, out_weight, out_grad):
    chip = lax.axis_index("chip")
    core = lax.axis_index("core")
    row = lax.axis_index("dp")
    chips = lax.axis_size("chip")
    rows_dp = lax.axis_size("dp")
    tok = queries.shape[1]
    rows = 2 * tok
    prior = min(-(-WINDOW // rows), chips - 1)
    steps = tuple(range(prior + 1))
    low = core == 0
    info = jnp.stack([chip, core, row]).astype(jnp.int32)
    together = lax.optimization_barrier

    def own(x):
        half = x.shape[-1] // 2
        return jnp.where(low, x[..., :half], x[..., half:])

    def other(x):
        half = x.shape[-1] // 2
        return jnp.where(low, x[..., half:], x[..., :half])

    def swap(x):
        return lax.ppermute(x, "core", [(0, 1), (1, 0)])

    def up(x, k):
        return lax.ppermute(x, "chip", [(i, i + k) for i in range(chips - k)])

    def down(x, k):
        return lax.ppermute(x, "chip", [(i + k, i) for i in range(chips - k)])

    def round_chips(x, k):
        return lax.ppermute(x, "chip", [(i, (i + k) % chips) for i in range(chips)])

    def across(x, k):
        return lax.ppermute(x, "dp", [(i, i ^ k) for i in range(rows_dp)])

    def in_order(mine, theirs, axis):
        return jnp.where(
            low,
            jnp.concatenate([mine, theirs], axis),
            jnp.concatenate([theirs, mine], axis),
        )

    k0, v0, q0, g0 = key_rows[0], values[0], queries[0], out_grad[0]
    near = chips <= 4
    moved = [round_chips(out_weight, k) for k in range(1, chips)] if near else []
    kv_theirs = swap(jnp.concatenate([other(k0), other(v0)], 1))
    kv = jnp.concatenate([own(k0), own(v0)], 1)
    kv = jnp.concatenate([kv, kv_theirs], 0)
    hop = up(kv, 1)
    q = jnp.concatenate([own(q0), swap(other(q0))], 0) * jnp.asarray(HD ** (-0.5), BF16)
    state = forward(info, q, kv, 0, None)
    piece = out_weight.shape[0]
    part = 2 * piece
    if near:
        column, column_theirs = column_halves(info, [out_weight, *moved])
    else:
        column = lax.all_gather(out_weight, "chip", axis=0)
        column, column_theirs = own(column), other(column)
    ours = in_order(column[:, None], swap(column_theirs)[:, None], 1)
    ours = ours.reshape(chips * part, ours.shape[-1])
    share = ours.shape[0]
    half = share // 2
    lower, upper = ours[:half], ours[half:]
    upper_x, lower_y = across(upper, 1), across(lower, 2)
    hop, q, state, lower, upper, upper_x, lower_y, grad_theirs = together(
        (hop, q, state, lower, upper, upper_x, lower_y, swap(g0))
    )
    chunks = [kv, hop]

    hop = up(hop, 1)
    state = forward(info, q, chunks[1], 1, state)
    diagonal_x, diagonal_y, hop, state, lower, upper = together(
        (across(lower_y, 1), across(upper_x, 2), hop, state, lower, upper)
    )
    chunks.append(hop)

    last_hop = up(hop, 1)
    for step in steps[2:prior]:
        state = forward(info, q, hop, step, state)
        hop = last_hop
        if step + 1 < prior:
            chunks.append(hop)
            last_hop = up(hop, 1)
    turned = jnp.concatenate([g0.T, grad_theirs.T], 1)

    def strip(k, at, size):
        return lax.dynamic_slice_in_dim(turned, (row ^ k) * share + at, size, 0)

    strips = [
        jnp.concatenate([strip(3, 0, half), strip(1, 0, half)], 0),
        jnp.concatenate([strip(3, half, half), strip(2, half, half)], 0),
        jnp.concatenate([strip(1, half, half), strip(2, 0, half), strip(0, 0, share)], 0),
    ]
    early = [(lower, 0, 0), (upper, 0, 1), (upper_x, 1, 1), (lower_y, 2, 0)]
    early += [(diagonal_x, 3, 0), (diagonal_y, 3, 1)]
    da = gradient_into_heads(info, turned, early)
    last_hop, lower_x, upper_y, da, state, *strips = together(
        (last_hop, across(lower, 1), across(upper, 2), da, state, *strips)
    )
    chunks.append(last_hop)
    att, lse_t, to_x, to_y = forward(info, q, last_hop, prior, state, strips[:2])
    att, info = together((att, info))
    late = [(lower_x, 1, 0), (upper_y, 2, 1)]
    da = gradient_into_heads(info, turned, late, da)
    weight = placed(info, early + late)

    carried = None
    terms = {}
    for step in reversed(steps):
        last = step == 0
        res = backward(info, q, da, lse_t, [chunks[step]], (step,), att, carried, last)
        terms[step] = res[0]
        if carried is None:
            delta_t = res[1]
        if last:
            dq = res[1]
        else:
            carried = (delta_t, res[-1])

    passing = terms[prior]
    for step in range(prior - 1, 2, -1):
        passing = (terms[step].astype(F32) + down(passing, 1).astype(F32)).astype(BF16)
    rest = strip_product(strips[2], att)
    from_x, from_y, got, rest, terms, dq, att = together(
        (across(to_x, 1), across(to_y, 2), down(passing, 1), rest, terms, dq, att)
    )
    part_mine, part_sent = layer_product(att, weight)
    later_x, later_y, here = rest[:half], rest[half:share], rest[share:]
    passing = (terms[2].astype(F32) + got.astype(F32)).astype(BF16)
    to_x = (later_x + from_y[:half].astype(F32)).astype(BF16)
    to_y = (later_y + from_x[:half].astype(F32)).astype(BF16)
    by_x1, by_y0, dq_theirs, part_sent, got = together(
        (across(to_x, 1), across(to_y, 2), swap(dq[tok:]), part_sent, down(passing, 1))
    )
    passing = (terms[1].astype(F32) + got.astype(F32)).astype(BF16)
    coming = down(passing, 1)
    layer_out = (part_mine + swap(part_sent).astype(F32)).astype(BF16)
    query_grad = in_order(dq[:tok], dq_theirs, 1)
    if chips == 4:

        def pair(x, k):
            return lax.ppermute(x, "chip", [(i, i ^ k) for i in range(chips)])

        final, farther, sent = plane_sum(info, rest, from_x, from_y, by_x1, by_y0)
        got = pair(sent, 1)
        final = final + got[:part].astype(F32)
        got = pair((farther + got[part:].astype(F32)).astype(BF16), 2)
        got, layer_out, query_grad, coming = together((got, layer_out, query_grad, coming))
        final = final + got.astype(F32)
    else:
        mine = here + jnp.concatenate(
            [
                from_x[half:].astype(F32) + by_y0.astype(F32),
                by_x1.astype(F32) + from_y[half:].astype(F32),
            ],
            0,
        )
        final = lax.psum_scatter(mine, "chip", scatter_dimension=0, tiled=True)
    total_tokens = rows_dp * chips * rows
    final = final * (1.0 / math.sqrt(total_tokens))
    first_rows, last_rows = final[:piece], final[piece:]
    weight_grad = in_order(
        jnp.where(low, first_rows, last_rows), swap(jnp.where(low, last_rows, first_rows)), 1
    )
    kv_grad = (terms[0] + coming.astype(F32)).astype(BF16)
    theirs = swap(kv_grad[tok:])
    key_grad = in_order(kv_grad[:tok, :HD], theirs[:, :HD], 1)
    value_grad = in_order(kv_grad[:tok, HD:], theirs[:, HD:], 1)
    return (
        layer_out[None],
        query_grad[None],
        key_grad[None],
        value_grad[None],
        weight_grad,
    )


def solution(mesh):
    devices = mesh.devices
    pairs = Mesh(
        devices.reshape(devices.shape[0], devices.shape[1] // 2, 2), ("dp", "chip", "core")
    )
    tokens = P("dp", ("chip", "core"), None)
    features = P(("dp", "chip", "core"), None)
    return jax.shard_map(
        on_device,
        mesh=pairs,
        in_specs=(tokens, tokens, tokens, features, tokens),
        out_specs=(tokens, tokens, tokens, tokens, features),
        check_vma=False,
    )
```

```python
import functools
import math

import jax
import jax.numpy as jnp
from jax import lax
from jax.experimental import pallas as pl
from jax.experimental.pallas import tpu as pltpu
from jax.sharding import Mesh
from jax.sharding import PartitionSpec as P

QH = 4
KH = 2
HD = 256
WINDOW = 2048
GROUPS = QH // KH
LANES = 128
NEG = -1e30
F32 = jnp.float32
BF16 = jnp.bfloat16
NT = (((1,), (1,)), ((), ()))
TN = (((0,), (0,)), ((), ()))
FILLER = pl.CostEstimate(flops=1, bytes_accessed=1, transcendentals=0)


def dot(a, b, dims=(((1,), (0,)), ((), ()))):
    return lax.dot_general(a, b, dims, preferred_element_type=F32)


def admitted(step, rows, core, query_axis):
    if step > 0 and (step + 1) * rows <= WINDOW:
        return None
    shape = (rows, rows)
    half = rows // 2
    query = (lax.broadcasted_iota(jnp.int32, shape, query_axis) + core * half) % rows
    key = (lax.broadcasted_iota(jnp.int32, shape, 1 - query_axis) + core * half) % rows
    gap = key - query - step * rows
    return (gap <= 0) & (gap > -WINDOW)


def forward_kernel(step, rows, first, last, info, q, kv, *refs):
    if not first:
        m_in, l_in, acc_in = refs[:3]
        refs = refs[3:]
    if last:
        strip_x, strip_y, out, lse_t, to_x, to_y, m_s, l_s, acc_s = refs
    else:
        m_s, l_s, acc_s = refs
    chip, core = info[0], info[1]
    mask = admitted(step, rows, core, 1)

    def block():
        keys = kv[:, :HD]
        vals_t = jnp.transpose(kv[:, HD:])
        for h in range(GROUPS):
            cols = slice(h * HD, (h + 1) * HD)
            stat = slice(h * 8, h * 8 + 1)
            whole = slice(h * 8, (h + 1) * 8)
            s = dot(keys, q[:, cols], NT)
            if mask is not None:
                s = jnp.where(mask, s, NEG)
            top = jnp.max(s, axis=0, keepdims=True)
            if first:
                p = jnp.exp(s - top)
                total = jnp.sum(p, axis=0, keepdims=True)
                acc_s[cols, :] = dot(vals_t, p.astype(BF16))
            else:
                before = m_in[stat, :]
                top = jnp.maximum(top, before)
                p = jnp.exp(s - top)
                keep = jnp.exp(before - top)
                total = keep * l_in[stat, :] + jnp.sum(p, axis=0, keepdims=True)
                acc_s[cols, :] = keep * acc_in[cols, :] + dot(vals_t, p.astype(BF16))
            m_s[whole, :] = jnp.broadcast_to(top, (8, rows))
            l_s[whole, :] = jnp.broadcast_to(total, (8, rows))

    if first:
        block()
    else:

        def keep_all():
            m_s[...] = m_in[...]
            l_s[...] = l_in[...]
            acc_s[...] = acc_in[...]

        pl.when(chip >= step)(block)
        pl.when(chip < step)(keep_all)
    if last:
        for h in range(GROUPS):
            cols = slice(h * HD, (h + 1) * HD)
            total = l_s[h * 8 : h * 8 + 1, :]
            out[:, cols] = jnp.transpose(acc_s[cols, :] / total).astype(BF16)
        lse_t[...] = m_s[...] + jnp.log(l_s[...])
        to_x[...] = dot(strip_x[...], out[...]).astype(BF16)
        to_y[...] = dot(strip_y[...], out[...]).astype(BF16)


def forward(info, q, kv, step, state, strips=()):
    rows = q.shape[0]
    first = state is None
    last = len(strips) > 0
    stat = jax.ShapeDtypeStruct((GROUPS * 8, rows), F32)
    acc = jax.ShapeDtypeStruct((GROUPS * HD, rows), F32)
    vmem = pl.BlockSpec(memory_space=pltpu.VMEM)
    smem = pl.BlockSpec(memory_space=pltpu.SMEM)
    scratch = []
    if last:
        outs = (jax.ShapeDtypeStruct((rows, GROUPS * HD), BF16), stat)
        outs += tuple(jax.ShapeDtypeStruct((x.shape[0], GROUPS * HD), BF16) for x in strips)
        scratch = [pltpu.VMEM(s.shape, F32) for s in (stat, stat, acc)]
    else:
        outs = (stat, stat, acc)
    args = [info, q, kv] + ([] if first else list(state)) + list(strips)
    return pl.pallas_call(
        functools.partial(forward_kernel, step, rows, first, last),
        out_shape=outs,
        in_specs=[smem] + [vmem] * (len(args) - 1),
        out_specs=tuple(vmem for _ in outs),
        scratch_shapes=scratch,
        cost_estimate=FILLER,
        compiler_params=pltpu.CompilerParams(vmem_limit_bytes=16 * 1024 * 1024),
        name="attend_forward",
    )(*args)


def backward_kernel(steps, rows, first, last, info, q, da, lse_t, *refs):
    chunks = refs[: len(steps)]
    refs = refs[len(steps) :]
    if first:
        att = refs[0]
        refs = refs[1:]
    else:
        delta_t, dq_in = refs[:2]
        refs = refs[2:]
    grads = refs[: len(steps)]
    refs = refs[len(steps) :]
    if last:
        dq_out = refs[0]
        refs = refs[1:]
    if first:
        delta_t = refs[0]
        refs = refs[1:]
    dq_s = refs[0]
    chip, core = info[0], info[1]
    if first:
        for h in range(GROUPS):
            cols = slice(h * HD, (h + 1) * HD)
            prod = da[:, cols].astype(F32) * att[:, cols].astype(F32)
            delta = jnp.sum(prod, axis=1, keepdims=True)
            wide = jnp.broadcast_to(delta, (rows, LANES))
            delta_t[h * 8 : (h + 1) * 8, :] = jnp.transpose(wide)[:8, :]
        dq_s[...] = jnp.zeros_like(dq_s)
    else:
        dq_s[...] = dq_in[...]
    for at, step in enumerate(steps):
        mask = admitted(step, rows, core, 1)

        def block(at=at, mask=mask):
            keys = chunks[at][:, :HD]
            keys_t = jnp.transpose(keys)
            vals = chunks[at][:, HD:]
            for h in range(GROUPS):
                cols = slice(h * HD, (h + 1) * HD)
                qh = q[:, cols]
                dah = da[:, cols]
                s = dot(keys, qh, NT)
                p = jnp.exp(s - lse_t[h * 8 : h * 8 + 1, :])
                if mask is not None:
                    p = jnp.where(mask, p, 0.0)
                dp = dot(vals, dah, NT)
                ds = (p * (dp - delta_t[h * 8 : h * 8 + 1, :])).astype(BF16)
                dk = dot(ds, qh)
                dv = dot(p.astype(BF16), dah)
                dq_s[cols, :] += dot(keys_t, ds)
                if h == 0:
                    dk_sum, dv_sum = dk, dv
                else:
                    dk_sum, dv_sum = dk_sum + dk, dv_sum + dv
            grads[at][:, :HD] = dk_sum.astype(grads[at].dtype)
            grads[at][:, HD:] = dv_sum.astype(grads[at].dtype)

        if step == 0:
            block()
        else:

            def blank(at=at):
                grads[at][...] = jnp.zeros_like(grads[at])

            pl.when(chip >= step)(block)
            pl.when(chip < step)(blank)
    if last:
        for h in range(GROUPS):
            cols = slice(h * HD, (h + 1) * HD)
            dq_out[:, cols] = jnp.transpose(dq_s[cols, :] * HD ** (-0.5)).astype(BF16)


def backward(info, q, da, lse_t, chunks, steps, att, carried, last):
    rows = q.shape[0]
    first = carried is None
    vmem = pl.BlockSpec(memory_space=pltpu.VMEM)
    smem = pl.BlockSpec(memory_space=pltpu.SMEM)
    wide = (rows, GROUPS * HD)
    tall = (GROUPS * HD, rows)
    outs = [jax.ShapeDtypeStruct((rows, 2 * HD), F32 if s == 0 else BF16) for s in steps]
    if last:
        outs.append(jax.ShapeDtypeStruct(wide, BF16))
    if first:
        outs.append(jax.ShapeDtypeStruct((GROUPS * 8, rows), F32))
    scratch = []
    if last:
        scratch = [pltpu.VMEM(tall, F32)]
    else:
        outs.append(jax.ShapeDtypeStruct(tall, F32))
    args = [info, q, da, lse_t, *chunks] + ([att] if first else list(carried))
    return pl.pallas_call(
        functools.partial(backward_kernel, steps, rows, first, last),
        out_shape=tuple(outs),
        in_specs=[smem] + [vmem] * (len(args) - 1),
        out_specs=tuple(vmem for _ in outs),
        scratch_shapes=scratch,
        cost_estimate=FILLER,
        compiler_params=pltpu.CompilerParams(vmem_limit_bytes=16 * 1024 * 1024),
        name="attend_backward",
    )(*args)


def column_kernel(info, *refs):
    *pieces, own, other = refs
    chip, core = info[0], info[1]
    chips = len(pieces)
    half = own.shape[2]
    for k, ref in enumerate(pieces):
        at = lax.rem(chip - k + chips, chips)
        left, right = ref[:, :half], ref[:, half:]
        own[at] = jnp.where(core == 0, left, right)
        other[at] = jnp.where(core == 0, right, left)


def column_halves(info, pieces):
    rows, width = pieces[0].shape
    shape = jax.ShapeDtypeStruct((len(pieces), rows, width // 2), BF16)
    vmem = pl.BlockSpec(memory_space=pltpu.VMEM)
    return pl.pallas_call(
        column_kernel,
        out_shape=(shape, shape),
        in_specs=[pl.BlockSpec(memory_space=pltpu.SMEM)] + [vmem] * len(pieces),
        out_specs=(vmem, vmem),
        cost_estimate=pl.CostEstimate(flops=4 * 10**9, bytes_accessed=1, transcendentals=0),
        compiler_params=pltpu.CompilerParams(vmem_limit_bytes=8 * 1024 * 1024),
        name="column_halves",
    )(info, *pieces)


def into_heads_kernel(places, based, info, turned, *refs):
    *pieces, out = refs
    total = None
    if based:
        base, *pieces = pieces
        total = base[...]
    half = pieces[0].shape[0]
    for (k, at), ref in zip(places, pieces):
        start = pl.multiple_of(((info[2] ^ k) * 2 + at) * half, half)
        term = dot(turned[pl.ds(start, half), :], ref[...], TN)
        total = term if total is None else total + term
    out[...] = total.astype(out.dtype)


def gradient_into_heads(info, turned, pieces, base=None):
    arrays = [x for x, _, _ in pieces]
    based = base is not None
    args = ([base] if based else []) + arrays
    vmem = pl.BlockSpec(memory_space=pltpu.VMEM)
    return pl.pallas_call(
        functools.partial(into_heads_kernel, [(k, at) for _, k, at in pieces], based),
        out_shape=jax.ShapeDtypeStruct(
            (turned.shape[1], arrays[0].shape[1]), BF16 if based else F32
        ),
        in_specs=[pl.BlockSpec(memory_space=pltpu.SMEM)] + [vmem] * (1 + len(args)),
        out_specs=vmem,
        cost_estimate=FILLER,
        compiler_params=pltpu.CompilerParams(vmem_limit_bytes=20 * 1024 * 1024),
        name="gradient_into_heads",
    )(info, turned, *args)


def place_kernel(places, info, *refs):
    *pieces, out = refs
    half = pieces[0].shape[0]
    for (k, at), ref in zip(places, pieces):
        start = pl.multiple_of(((info[2] ^ k) * 2 + at) * half, half)
        out[pl.ds(start, half), :] = ref[...]


def placed(info, pieces):
    arrays = [x for x, _, _ in pieces]
    half, width = arrays[0].shape
    vmem = pl.BlockSpec(memory_space=pltpu.VMEM)
    return pl.pallas_call(
        functools.partial(place_kernel, [(k, at) for _, k, at in pieces]),
        out_shape=jax.ShapeDtypeStruct((half * len(pieces), width), BF16),
        in_specs=[pl.BlockSpec(memory_space=pltpu.SMEM)] + [vmem] * len(arrays),
        out_specs=vmem,
        cost_estimate=FILLER,
        compiler_params=pltpu.CompilerParams(vmem_limit_bytes=8 * 1024 * 1024),
        name="place_shares",
    )(info, *arrays)


def plane_sum_kernel(info, rest, from_x, from_y, by_x1, by_y0, kept, farther, sent, total):
    share, part = total.shape[0], kept.shape[0]
    half = share // 2
    total[:half, :] = (
        rest[share : share + half, :] + from_x[half:, :].astype(F32) + by_y0[...].astype(F32)
    )
    total[half:, :] = (
        rest[share + half :, :] + by_x1[...].astype(F32) + from_y[half:, :].astype(F32)
    )

    def block(k):
        return total[pl.ds(pl.multiple_of((info[0] ^ k) * part, part), part), :]

    kept[...] = block(0)
    farther[...] = block(2)
    sent[:part, :] = block(1).astype(BF16)
    sent[part:, :] = block(3).astype(BF16)


def plane_sum(info, rest, *arrived):
    share = rest.shape[0] // 2
    part, width = share // 4, rest.shape[1]
    vmem = pl.BlockSpec(memory_space=pltpu.VMEM)
    return pl.pallas_call(
        plane_sum_kernel,
        out_shape=(
            jax.ShapeDtypeStruct((part, width), F32),
            jax.ShapeDtypeStruct((part, width), F32),
            jax.ShapeDtypeStruct((2 * part, width), BF16),
        ),
        in_specs=[pl.BlockSpec(memory_space=pltpu.SMEM)] + [vmem] * (1 + len(arrived)),
        out_specs=(vmem, vmem, vmem),
        scratch_shapes=[pltpu.VMEM((share, width), F32)],
        cost_estimate=FILLER,
        compiler_params=pltpu.CompilerParams(vmem_limit_bytes=16 * 1024 * 1024),
        name="plane_sum",
    )(info, rest, *arrived)


def product_kernel(x, w, *outs):
    result = dot(x[...], w[...], NT if len(outs) == 2 else (((1,), (0,)), ((), ())))
    if len(outs) == 2:
        half = result.shape[0] // 2
        outs[0][...] = result[:half]
        outs[1][...] = result[half:].astype(BF16)
    else:
        outs[0][...] = result


def layer_product(att, weight):
    rows, depth = att.shape
    features = weight.shape[0]
    wide = 256
    block = pl.BlockSpec((rows // 2, wide), lambda i: (0, i))
    return pl.pallas_call(
        product_kernel,
        grid=(features // wide,),
        out_shape=(
            jax.ShapeDtypeStruct((rows // 2, features), F32),
            jax.ShapeDtypeStruct((rows // 2, features), BF16),
        ),
        in_specs=[
            pl.BlockSpec((rows, depth), lambda i: (0, 0)),
            pl.BlockSpec((wide, depth), lambda i: (i, 0)),
        ],
        out_specs=(block, block),
        cost_estimate=FILLER,
        compiler_params=pltpu.CompilerParams(vmem_limit_bytes=16 * 1024 * 1024),
        name="layer_product",
    )(att, weight)


def strip_product(strips, att):
    rows, depth = strips.shape
    tall = rows // 4
    return pl.pallas_call(
        product_kernel,
        grid=(4,),
        out_shape=jax.ShapeDtypeStruct((rows, att.shape[1]), F32),
        in_specs=[
            pl.BlockSpec((tall, depth), lambda i: (i, 0)),
            pl.BlockSpec(att.shape, lambda i: (0, 0)),
        ],
        out_specs=pl.BlockSpec((tall, att.shape[1]), lambda i: (i, 0)),
        cost_estimate=FILLER,
        compiler_params=pltpu.CompilerParams(vmem_limit_bytes=16 * 1024 * 1024),
        name="strip_product",
    )(strips, att)


def on_device(queries, key_rows, values, out_weight, out_grad):
    chip = lax.axis_index("chip")
    core = lax.axis_index("core")
    row = lax.axis_index("dp")
    chips = lax.axis_size("chip")
    rows_dp = lax.axis_size("dp")
    tok = queries.shape[1]
    rows = 2 * tok
    prior = min(-(-WINDOW // rows), chips - 1)
    steps = tuple(range(prior + 1))
    low = core == 0
    info = jnp.stack([chip, core, row]).astype(jnp.int32)
    together = lax.optimization_barrier

    def own(x):
        half = x.shape[-1] // 2
        return jnp.where(low, x[..., :half], x[..., half:])

    def other(x):
        half = x.shape[-1] // 2
        return jnp.where(low, x[..., half:], x[..., :half])

    def swap(x):
        return lax.ppermute(x, "core", [(0, 1), (1, 0)])

    def up(x, k):
        return lax.ppermute(x, "chip", [(i, i + k) for i in range(chips - k)])

    def down(x, k):
        return lax.ppermute(x, "chip", [(i + k, i) for i in range(chips - k)])

    def round_chips(x, k):
        return lax.ppermute(x, "chip", [(i, (i + k) % chips) for i in range(chips)])

    def across(x, k):
        return lax.ppermute(x, "dp", [(i, i ^ k) for i in range(rows_dp)])

    def in_order(mine, theirs, axis):
        return jnp.where(
            low,
            jnp.concatenate([mine, theirs], axis),
            jnp.concatenate([theirs, mine], axis),
        )

    k0, v0, q0, g0 = key_rows[0], values[0], queries[0], out_grad[0]
    near = chips <= 4
    moved = [round_chips(out_weight, k) for k in range(1, chips)] if near else []
    kv_theirs = swap(jnp.concatenate([other(k0), other(v0)], 1))
    kv = jnp.concatenate([own(k0), own(v0)], 1)
    kv = jnp.concatenate([kv, kv_theirs], 0)
    hop = up(kv, 1)
    q = jnp.concatenate([own(q0), swap(other(q0))], 0) * jnp.asarray(HD ** (-0.5), BF16)
    state = forward(info, q, kv, 0, None)
    piece = out_weight.shape[0]
    part = 2 * piece
    if near:
        column, column_theirs = column_halves(info, [out_weight, *moved])
    else:
        column = lax.all_gather(out_weight, "chip", axis=0)
        column, column_theirs = own(column), other(column)
    ours = in_order(column[:, None], swap(column_theirs)[:, None], 1)
    ours = ours.reshape(chips * part, ours.shape[-1])
    share = ours.shape[0]
    half = share // 2
    lower, upper = ours[:half], ours[half:]
    upper_x, lower_y = across(upper, 1), across(lower, 2)
    hop, q, state, lower, upper, upper_x, lower_y, grad_theirs = together(
        (hop, q, state, lower, upper, upper_x, lower_y, swap(g0))
    )
    chunks = [kv, hop]

    hop = up(hop, 1)
    state = forward(info, q, chunks[1], 1, state)
    state, lower_y, upper_x = together((state, lower_y, upper_x))
    diagonal_x, diagonal_y, hop, lower, upper = together(
        (across(lower_y, 1), across(upper_x, 2), hop, lower, upper)
    )
    chunks.append(hop)

    last_hop = up(hop, 1)
    for step in steps[2:prior]:
        state = forward(info, q, hop, step, state)
        hop = last_hop
        if step + 1 < prior:
            chunks.append(hop)
            last_hop = up(hop, 1)
    turned = jnp.concatenate([g0.T, grad_theirs.T], 1)

    def strip(k, at, size):
        return lax.dynamic_slice_in_dim(turned, (row ^ k) * share + at, size, 0)

    strips = [
        jnp.concatenate([strip(3, 0, half), strip(1, 0, half)], 0),
        jnp.concatenate([strip(3, half, half), strip(2, half, half)], 0),
        jnp.concatenate([strip(1, half, half), strip(2, 0, half), strip(0, 0, share)], 0),
    ]
    early = [(lower, 0, 0), (upper, 0, 1), (upper_x, 1, 1), (lower_y, 2, 0)]
    early += [(diagonal_x, 3, 0), (diagonal_y, 3, 1)]
    da = gradient_into_heads(info, turned, early)
    last_hop, lower_x, upper_y, da, state, *strips = together(
        (last_hop, across(lower, 1), across(upper, 2), da, state, *strips)
    )
    chunks.append(last_hop)
    att, lse_t, to_x, to_y = forward(info, q, last_hop, prior, state, strips[:2])
    att, info = together((att, info))
    late = [(lower_x, 1, 0), (upper_y, 2, 1)]
    da = gradient_into_heads(info, turned, late, da)
    weight = placed(info, early + late)

    carried = None
    terms = {}
    for step in reversed(steps):
        last = step == 0
        res = backward(info, q, da, lse_t, [chunks[step]], (step,), att, carried, last)
        terms[step] = res[0]
        if carried is None:
            delta_t = res[1]
        if last:
            dq = res[1]
        else:
            carried = (delta_t, res[-1])

    passing = terms[prior]
    for step in range(prior - 1, 2, -1):
        passing = (terms[step].astype(F32) + down(passing, 1).astype(F32)).astype(BF16)
    rest = strip_product(strips[2], att)
    from_x, from_y, got, rest, terms, dq, att = together(
        (across(to_x, 1), across(to_y, 2), down(passing, 1), rest, terms, dq, att)
    )
    part_mine, part_sent = layer_product(att, weight)
    later_x, later_y, here = rest[:half], rest[half:share], rest[share:]
    passing = (terms[2].astype(F32) + got.astype(F32)).astype(BF16)
    to_x = (later_x + from_y[:half].astype(F32)).astype(BF16)
    to_y = (later_y + from_x[:half].astype(F32)).astype(BF16)
    by_x1, by_y0, dq_theirs, part_sent, got = together(
        (across(to_x, 1), across(to_y, 2), swap(dq[tok:]), part_sent, down(passing, 1))
    )
    passing = (terms[1].astype(F32) + got.astype(F32)).astype(BF16)
    coming = down(passing, 1)
    layer_out = (part_mine + swap(part_sent).astype(F32)).astype(BF16)
    query_grad = in_order(dq[:tok], dq_theirs, 1)
    if chips == 4:

        def pair(x, k):
            return lax.ppermute(x, "chip", [(i, i ^ k) for i in range(chips)])

        final, farther, sent = plane_sum(info, rest, from_x, from_y, by_x1, by_y0)
        got = pair(sent, 1)
        final = final + got[:part].astype(F32)
        got = pair((farther + got[part:].astype(F32)).astype(BF16), 2)
        got, layer_out, query_grad, coming = together((got, layer_out, query_grad, coming))
        final = final + got.astype(F32)
    else:
        mine = here + jnp.concatenate(
            [
                from_x[half:].astype(F32) + by_y0.astype(F32),
                by_x1.astype(F32) + from_y[half:].astype(F32),
            ],
            0,
        )
        final = lax.psum_scatter(mine, "chip", scatter_dimension=0, tiled=True)
    total_tokens = rows_dp * chips * rows
    final = final * (1.0 / math.sqrt(total_tokens))
    first_rows, last_rows = final[:piece], final[piece:]
    weight_grad = in_order(
        jnp.where(low, first_rows, last_rows), swap(jnp.where(low, last_rows, first_rows)), 1
    )
    kv_grad = (terms[0] + coming.astype(F32)).astype(BF16)
    theirs = swap(kv_grad[tok:])
    key_grad = in_order(kv_grad[:tok, :HD], theirs[:, :HD], 1)
    value_grad = in_order(kv_grad[:tok, HD:], theirs[:, HD:], 1)
    return (
        layer_out[None],
        query_grad[None],
        key_grad[None],
        value_grad[None],
        weight_grad,
    )


def solution(mesh):
    devices = mesh.devices
    pairs = Mesh(
        devices.reshape(devices.shape[0], devices.shape[1] // 2, 2), ("dp", "chip", "core")
    )
    tokens = P("dp", ("chip", "core"), None)
    features = P(("dp", "chip", "core"), None)
    return jax.shard_map(
        on_device,
        mesh=pairs,
        in_specs=(tokens, tokens, tokens, features, tokens),
        out_specs=(tokens, tokens, tokens, tokens, features),
        check_vma=False,
    )
```
